32 devices in a mesh: dp: 8 (over z, x), tensor: 4 (over y, core).
Axes of the slice: x: 2, y: 2, z: 4, core: 2. Of those that a mesh axis runs over, the one named last changes fastest.
Arguments:
- tokens: bfloat16 [32, 512, 768], P('dp', 'tensor'), may hold values from -6 to 6
- lengths: int32 [32], P('dp'), may hold values from 64 to 512, as said below
- grad_out: bfloat16 [32, 512, 768], P('dp', 'tensor'), may hold values from -6 to 6
- qkv_weight: bfloat16 [3, 768, 768], P(None, 'dp', 'tensor'), may hold values from -0.21875 to 0.21875
- out_weight: bfloat16 [768, 768], P('tensor', 'dp'), may hold values from -1.25 to 1.25
- up_weight: bfloat16 [768, 3072], P('dp', 'tensor'), may hold values from -0.21875 to 0.21875
- down_weight: bfloat16 [3072, 768], P('tensor', 'dp'), may hold values from -0.109375 to 0.109375
- vectors: bfloat16 [8, 768], P(None, 'dp'), may hold values from -1.6 to 1.6
- hidden_bias: bfloat16 [3072], P('dp'), may hold values from -1.5 to 1.5
Outputs:
- output: bfloat16 [32, 512, 768], P('dp', 'tensor')
- grad_tokens: float32 [32, 512, 768], P('dp', 'tensor')
- query_key_value_gradient: float32 [3, 768, 768], P(None, 'dp', 'tensor')
- grad_out_weight: float32 [768, 768], P('tensor', 'dp')
- grad_up: float32 [768, 3072], P('dp', 'tensor')
- grad_down: float32 [3072, 768], P('tensor', 'dp')
- grad_vectors: float32 [8, 768], P(None, 'dp')
- grad_hidden_bias: float32 [3072], P('dp')
The draws below stay inside these ranges and needn't reach their ends.
Inputs may be any that keep to these rules, and one draw needn't show every extreme that they name: `lengths`: each sequence's valid tokens; some sequence has all 512 valid in every draw.
All inputs are finite; a program needn't handle non-finite values.
Results may differ from the reference program's by a relative error of at most 0.02.
Values may be sent and summed in bfloat16 or wider, within the bound.
A program may use at most 128 MiB of HBM per device.

```python
import jax
import jax.numpy as jnp
from jax import lax

D = 768
H = 12
HD = 64
FF = 3072
LEN = 512
SEQS = 32


def draw_lengths(key, part):
    sampled = jax.random.randint(jax.random.fold_in(key, 21), (SEQS,), LEN // 8, LEN + 1)
    chosen = jax.random.randint(jax.random.fold_in(key, 22), (), 0, SEQS)
    return jnp.where(jnp.arange(SEQS) == chosen, LEN, sampled).astype(jnp.int32)


def draw_vectors(key, part):
    normal_part = jax.random.normal(jax.random.fold_in(key, 11), (8, D), jnp.float32)
    gain_part = jax.random.uniform(jax.random.fold_in(key, 12), (8, D), jnp.float32, 0.5, 1.5)
    shifts = jnp.clip(0.4 * normal_part, -1.6, 1.6)
    gain_rows = (jnp.arange(8) == 3) | (jnp.arange(8) == 6)
    return jnp.where(gain_rows[:, None], gain_part, shifts).astype(jnp.bfloat16)


def steps_of(own_key, extent, cuts, smallest, high):
    def one(dim, parts):
        draws = jax.random.uniform(jax.random.fold_in(jax.random.fold_in(own_key, 6), dim), (parts,), jnp.float32, smallest / len(cuts), high / len(cuts))
        return jnp.repeat(jnp.exp(draws), extent[dim] // parts).reshape((-1,) + (1,) * (len(extent) - dim - 1))

    gain = one(*cuts[0])
    for cut in cuts[1:]:
        gain = gain * one(*cut)
    return gain


def scatter_about(key, shape, deviation, limit, cuts=(), dtype=jnp.bfloat16):
    gain = steps_of(key, shape, cuts, -0.22, 0.18) if cuts else 1.0
    drawn = jax.random.normal(key, shape, jnp.float32) * deviation * gain
    return jnp.minimum(jnp.maximum(drawn, -limit), limit).astype(dtype)


def setup_inputs(seed: int = 0) -> dict:
    keys = jax.random.split(jax.random.key(seed), 10)
    return {
        "tokens": scatter_about(keys[0], (SEQS, LEN, D), 1.0, 6.0, ((0, 8), (1, 4))),
        "lengths": draw_lengths(jax.random.fold_in(keys[9], 71), 0),
        "grad_out": scatter_about(keys[2], (SEQS, LEN, D), 1.0, 6.0, ((0, 8), (1, 4))),
        "qkv_weight": scatter_about(keys[3], (3, D, D), D ** -0.5, 0.21875, ((1, 8), (2, 4))),
        "out_weight": scatter_about(keys[4], (D, D), (D // 32) ** -0.5, 1.25, ((0, 4), (1, 8))),
        "up_weight": scatter_about(keys[5], (D, FF), D ** -0.5, 0.21875, ((0, 8), (1, 4))),
        "down_weight": scatter_about(keys[6], (FF, D), FF ** -0.5, 0.109375, ((0, 4), (1, 8))),
        "vectors": draw_vectors(jax.random.fold_in(keys[9], 71), 0),
        "hidden_bias": scatter_about(keys[8], (FF,), 0.3, 1.5, ((0, 8),)),
    }


@jax.custom_vjp
def low(v):
    return lax.optimization_barrier(v.astype(jnp.bfloat16)).astype(jnp.float32)

@jax.custom_vjp
def low_back(v):
    return v

def low_keep(v):
    return (low(v), None)

def low_pass(kept, grad):
    return (grad,)

def back_keep(v):
    return (v, None)

def back_low(kept, grad):
    return (low(grad),)
low.defvjp(low_keep, low_pass)
low_back.defvjp(back_keep, back_low)

def product(left, right):
    return jnp.dot(left, right, precision=lax.Precision.HIGHEST)

def layer_norm(residual, norm_gain, norm_shift):
    mean_row = lax.optimization_barrier(jnp.mean(residual, axis=-1, keepdims=True))
    centred = residual - mean_row
    spread = lax.optimization_barrier(jnp.mean(centred * centred, axis=-1, keepdims=True))
    return centred * lax.rsqrt(spread + 1e-12) * norm_gain + norm_shift

def forward_sequence(tokens_seq, length, qkv_param, out_param, up_param, down_param, vector_param, bias_param):
    queries = low(low_back(product(tokens_seq, qkv_param[0])) + vector_param[0])
    key_rows = low(low_back(product(tokens_seq, qkv_param[1])))
    values = low(low_back(product(tokens_seq, qkv_param[2])) + vector_param[1])
    head_query = queries.reshape(LEN, H, HD)
    head_key = key_rows.reshape(LEN, H, HD)
    head_value = values.reshape(LEN, H, HD)
    scores = low_back(jnp.einsum('qhe,khe->hqk', head_query, head_key, precision=lax.Precision.HIGHEST) * 0.125)
    key_valid = jnp.arange(LEN) < length
    scores = jnp.where(key_valid[None, None, :], scores, -1e+30)
    highest = lax.optimization_barrier(jnp.max(scores, axis=-1, keepdims=True))
    exponent = jnp.exp(scores - highest)
    probabilities = low(exponent / lax.optimization_barrier(jnp.sum(exponent, axis=-1, keepdims=True)))
    attention_context = jnp.einsum('hqk,khe->qhe', probabilities, head_value, precision=lax.Precision.HIGHEST)
    attention_context = low(low_back(attention_context.reshape(LEN, D)))
    attended = low_back(product(attention_context, out_param))
    hidden = layer_norm(tokens_seq + attended + vector_param[2], vector_param[3], vector_param[4])
    pre_act = low_back(product(low(hidden), up_param)) + bias_param
    gelu_activations = low(jax.nn.gelu(pre_act, approximate=False))
    resid_two = hidden + low_back(product(gelu_activations, down_param)) + vector_param[5]
    return layer_norm(resid_two, vector_param[6], vector_param[7])

def reference(tokens, lengths, grad_out, qkv_weight, out_weight, up_weight, down_weight, vectors, hidden_bias):
    params = (qkv_weight.astype(jnp.float32), out_weight.astype(jnp.float32), up_weight.astype(jnp.float32), down_weight.astype(jnp.float32), vectors.astype(jnp.float32), hidden_bias.astype(jnp.float32))

    def one_sequence(totals, operands):
        tokens_seq, length, cotangent = operands

        def forward(tokens_in, qkv_param, out_param, up_param, down_param, vector_param, bias_param):
            return forward_sequence(tokens_in, length, qkv_param, out_param, up_param, down_param, vector_param, bias_param)
        result, pullback = jax.vjp(forward, tokens_seq.astype(jnp.float32), params[0], params[1], params[2], params[3], params[4], params[5])
        gradients = pullback(cotangent.astype(jnp.float32))
        new_totals = jax.tree.map(jnp.add, totals, tuple(gradients[1:]))
        return (new_totals, (result.astype(jnp.bfloat16), gradients[0]))
    starting = tuple((jnp.zeros_like(param) for param in params))
    totals, (outputs, input_grads) = lax.scan(one_sequence, starting, (tokens, lengths, grad_out))
    return (outputs, input_grads, totals[0], totals[1], totals[2], totals[3], totals[4], totals[5])
```

```python
import functools

import jax
import jax.numpy as jnp
import numpy as np
from jax import lax
from jax.experimental import pallas as pl
from jax.experimental.pallas import tpu as pltpu
from jax.sharding import PartitionSpec as P

HD = 64
EPS = 1e-12
NEG = -1e30
F32 = jnp.float32
BF16 = jnp.bfloat16
VMEM_LIMIT = 67043328
ROWS = 128


def dot(left, right):
    return lax.dot_general(left, right, (((1,), (0,)), ((), ())), preferred_element_type=F32)


def dot_nt(left, right):
    return lax.dot_general(left, right, (((1,), (1,)), ((), ())), preferred_element_type=F32)


def lane_masks(scale):
    lane = lax.broadcasted_iota(jnp.int32, (1, 128), 1)
    low = jnp.where(lane < HD, F32(scale), F32(0)).astype(BF16)
    high = jnp.where(lane < HD, F32(0), F32(scale)).astype(BF16)
    return low, high


def is_low(shape):
    return lax.broadcasted_iota(jnp.int32, shape, 1) < HD


def put_row(ref, row, span, value):
    old = ref[8:16, span]
    here = lax.broadcasted_iota(jnp.int32, old.shape, 0) == row
    ref[8:16, span] = jnp.where(here, value, old)


def forward_kernel(
    x_ref, go_ref, len_ref, w_ref, sm_ref,
    out_ref, qkv_ref, ctx_ref, act_ref, gp_ref, hb_ref, n1_ref, s1_ref, g2_ref, stat_ref, gsm_ref,
    acc, hid, pre,
):
    seq, width = x_ref.shape
    blocks = seq // ROWS
    low, high = lane_masks(0.125)
    length = len_ref[0, 0]
    key_bias = jnp.where(lax.broadcasted_iota(jnp.int32, (1, seq), 1) < length, F32(0), F32(NEG))

    acc[...] = jnp.zeros_like(acc)

    @pl.loop(0, 4)
    def _(t):
        proj = dot(x_ref[...], w_ref[0, t, :, 0:640]) + sm_ref[pl.ds(12 + t, 1), 0:640]
        qkv_ref[t, :, 0:640] = proj.astype(BF16)
        q_two = pltpu.roll(jnp.where(is_low((seq, 128)), proj[:, 384:512] * 0.125, 0.0), 64, 1)
        qkv_ref[t, :, 640:768] = q_two.astype(BF16)

        @pl.loop(0, seq // 256)
        def _(r):
            rows = pl.ds(pl.multiple_of(r * 256, 256), 256)
            q_pair = qkv_ref[t, rows, 0:128]
            outs = []
            stats = []
            for h in range(3):
                if h < 2:
                    queries = q_pair * (low, high)[h]
                    keys = qkv_ref[t, :, 128:256]
                    values = qkv_ref[t, :, 256:384]
                else:
                    queries = qkv_ref[t, rows, 640:768]
                    keys = qkv_ref[t, :, 384:512]
                    values = qkv_ref[t, :, 512:640]
                scores = dot_nt(queries, keys) + key_bias
                highest = jnp.max(scores, axis=1, keepdims=True)
                grown = jnp.exp(scores - highest)
                total = jnp.sum(grown, axis=1, keepdims=True)
                probs = (grown * (1.0 / total)).astype(BF16)
                outs.append(dot(probs, values))
                stats.append(highest + jnp.log(total))
            lowest = is_low((256, 128))
            ctx_ref[t, rows, 0:128] = jnp.where(lowest, pltpu.roll(outs[2], 64, 1), 0.0).astype(BF16)
            ctx_ref[t, rows, 128:256] = jnp.where(lowest, outs[0], outs[1]).astype(BF16)
            lane = lax.broadcasted_iota(jnp.int32, (256, 128), 1)
            stat = jnp.where(lane == 0, stats[0], jnp.where(lane == 1, stats[1], stats[2]))
            stat_ref[t, rows, :] = stat

        acc[...] += dot_nt(ctx_ref[t], w_ref[0, t, :, 512:768])

    @pl.loop(0, blocks)
    def _(r):
        rows = pl.ds(pl.multiple_of(r * ROWS, ROWS), ROWS)
        resid = x_ref[rows, :].astype(F32) + acc[rows, :] + sm_ref[2:3, :]
        centred = resid - jnp.mean(resid, axis=1, keepdims=True)
        scale = lax.rsqrt(jnp.mean(centred * centred, axis=1, keepdims=True) + EPS)
        normed = centred * scale
        hidden = normed * sm_ref[3:4, :] + sm_ref[4:5, :]
        n1_ref[rows, :] = normed
        s1_ref[rows, :] = jnp.broadcast_to(scale, (ROWS, 128))
        hid[rows, :] = hidden
        hb_ref[rows, :] = hidden.astype(BF16)
        acc[rows, :] = hidden + sm_ref[5:6, :]

    @pl.loop(0, 4)
    def _(t):
        pre[...] = dot(hb_ref[...], w_ref[1, t])

        @pl.loop(0, blocks)
        def _(r):
            rows = pl.ds(pl.multiple_of(r * ROWS, ROWS), ROWS)
            u = pre[rows, :] + sm_ref[pl.ds(8 + t, 1), :]
            cdf = 0.5 + 0.5 * lax.erf(u * F32(np.sqrt(0.5)))
            density = jnp.exp(u * u * -0.5) * F32(1.0 / np.sqrt(2.0 * np.pi))
            act_ref[t, rows, :] = (u * cdf).astype(BF16)
            gp_ref[t, rows, :] = cdf + u * density

        acc[...] += dot_nt(act_ref[t], w_ref[2, t])

    gsm_ref[...] = jnp.zeros_like(gsm_ref)

    @pl.loop(0, blocks)
    def _(r):
        rows = pl.ds(pl.multiple_of(r * ROWS, ROWS), ROWS)
        resid = acc[rows, :]
        centred = resid - jnp.mean(resid, axis=1, keepdims=True)
        scale = lax.rsqrt(jnp.mean(centred * centred, axis=1, keepdims=True) + EPS)
        normed = centred * scale
        gain = sm_ref[6:7, :]
        out_ref[rows, :] = (normed * gain + sm_ref[7:8, :]).astype(BF16)
        cot = go_ref[rows, :].astype(F32)
        e = cot * gain
        en = jnp.mean(e * normed, axis=1, keepdims=True)
        grad = scale * (e - jnp.mean(e, axis=1, keepdims=True) - normed * en)
        g2_ref[rows, :] = grad
        gsm_ref[5:6, :] += jnp.sum(grad, axis=0, keepdims=True)
        gsm_ref[6:7, :] += jnp.sum(cot * normed, axis=0, keepdims=True)
        gsm_ref[7:8, :] += jnp.sum(cot, axis=0, keepdims=True)


def backward_kernel(
    x_ref, len_ref, w_ref, sm_ref, qkv_ref, ctx_ref, act_ref, gp_ref, hb_ref, n1_ref, s1_ref, g2_ref, stat_ref,
    gsm_in,
    gtok_ref, g_ref, gsm_ref,
    acc, low_grad, tall, gpre, gctx, gpacked,
):
    seq, width = x_ref.shape
    blocks = seq // ROWS
    low, high = lane_masks(0.125)
    one_low, one_high = lane_masks(1.0)
    length = len_ref[0, 0]
    key_bias = jnp.where(lax.broadcasted_iota(jnp.int32, (seq, 1), 0) < length, F32(0), F32(NEG))
    gsm_ref[0:8, :] = gsm_in[0:8, :]
    gsm_ref[8:16, :] = jnp.zeros((8, gsm_ref.shape[1]), F32)

    low_grad[...] = g2_ref[...].astype(BF16)
    tall[0] = jnp.transpose(g2_ref[...]).astype(BF16)
    tall[1] = jnp.transpose(hb_ref[...].astype(F32)).astype(BF16)
    acc[...] = g2_ref[...]

    @pl.loop(0, 4)
    def _(t):
        g_ref[2, t] = dot(tall[0], act_ref[t]).astype(BF16)
        grad_act = dot(low_grad[...], w_ref[2, t])
        grad_pre = grad_act * gp_ref[t]
        put_row(gsm_ref, t, slice(0, 768), jnp.sum(grad_pre, axis=0, keepdims=True))
        gpre[...] = grad_pre.astype(BF16)
        g_ref[1, t] = dot(tall[1], gpre[...]).astype(BF16)
        acc[...] += dot_nt(gpre[...], w_ref[1, t])

    @pl.loop(0, blocks)
    def _(r):
        rows = pl.ds(pl.multiple_of(r * ROWS, ROWS), ROWS)
        cot = acc[rows, :]
        normed = n1_ref[rows, :]
        e = cot * sm_ref[3:4, :]
        en = jnp.mean(e * normed, axis=1, keepdims=True)
        grad = s1_ref[rows, 0:1] * (e - jnp.mean(e, axis=1, keepdims=True) - normed * en)
        acc[rows, :] = grad
        low_grad[rows, :] = grad.astype(BF16)
        gsm_ref[2:3, :] += jnp.sum(grad, axis=0, keepdims=True)
        gsm_ref[3:4, :] += jnp.sum(cot * normed, axis=0, keepdims=True)
        gsm_ref[4:5, :] += jnp.sum(cot, axis=0, keepdims=True)

    tall[0] = jnp.transpose(acc[...]).astype(BF16)
    tall[1] = jnp.transpose(x_ref[...].astype(F32)).astype(BF16)

    @pl.loop(0, 4)
    def _(t):
        back = dot(low_grad[...], w_ref[0, t, :, 512:768])
        gctx[:, 0:128] = pltpu.roll(jnp.where(is_low((seq, 128)), back[:, 0:128], 0.0), 64, 1).astype(BF16)
        gctx[:, 128:256] = back[:, 128:256].astype(BF16)
        log_rows = jnp.transpose(stat_ref[t])
        grads_q = []
        grads_k = []
        grads_v = []
        for h in range(3):
            if h < 2:
                queries = qkv_ref[t, :, 0:128] * (low, high)[h]
                keys = qkv_ref[t, :, 128:256]
                values = qkv_ref[t, :, 256:384]
                cots = gctx[:, 128:256] * (one_low, one_high)[h]
            else:
                queries = qkv_ref[t, :, 640:768]
                keys = qkv_ref[t, :, 384:512]
                values = qkv_ref[t, :, 512:640]
                cots = gctx[:, 0:128]
            scores = dot_nt(keys, queries) + key_bias
            probs = jnp.exp(scores - log_rows[h : h + 1, :])
            grad_probs = dot_nt(values, cots)
            row_dots = jnp.sum(grad_probs * probs, axis=0, keepdims=True)
            grad_scores = (probs * (grad_probs - row_dots)).astype(BF16)
            grads_v.append(dot(probs.astype(BF16), cots))
            grads_k.append(dot(grad_scores, queries))
            part = (0, HD, HD)[h]
            keys_tall = jnp.transpose(keys.astype(F32))[part : part + HD, :].astype(BF16)
            grads_q.append(dot(keys_tall, grad_scores) * 0.125)
        pair = jnp.transpose(jnp.concatenate([grads_q[0], grads_q[1]], axis=0))
        single = jnp.transpose(jnp.concatenate([grads_q[2], jnp.zeros_like(grads_q[2])], axis=0))
        tiles = [pair, grads_k[0] + grads_k[1], grads_v[0] + grads_v[1], single + grads_k[2], grads_v[2]]
        for i, tile in enumerate(tiles):
            span = slice(128 * i, 128 * i + 128)
            put_row(gsm_ref, 4 + t, span, jnp.sum(tile, axis=0, keepdims=True))
            gpacked[:, span] = tile.astype(BF16)
        g_ref[0, t, :, 0:512] = dot(tall[1], gpacked[:, 0:512]).astype(BF16)
        g_ref[0, t, :, 512:640] = (
            dot(tall[1], gpacked[:, 512:640]) + dot(tall[0], ctx_ref[t, :, 0:128])
        ).astype(BF16)
        g_ref[0, t, :, 640:768] = dot(tall[0], ctx_ref[t, :, 128:256]).astype(BF16)
        acc[...] += dot_nt(gpacked[...], w_ref[0, t, :, 0:640])

    gtok_ref[...] = acc[...].astype(BF16)


def forward_call(x, go, length, w, sm):
    seq, width = x.shape
    shapes = (
        ((seq, width), BF16), ((4, seq, 768), BF16), ((4, seq, 256), BF16), ((4, seq, 768), BF16),
        ((4, seq, 768), F32), ((seq, width), BF16), ((seq, width), F32), ((seq, 128), F32),
        ((seq, width), F32), ((4, seq, 128), F32), ((16, width), F32),
    )
    vmem = pl.BlockSpec(memory_space=pltpu.VMEM)
    smem = pl.BlockSpec(memory_space=pltpu.SMEM)
    return pl.pallas_call(
        forward_kernel,
        out_shape=[jax.ShapeDtypeStruct(s, d) for s, d in shapes],
        in_specs=[vmem, vmem, smem, vmem, vmem],
        out_specs=[vmem] * len(shapes),
        scratch_shapes=[pltpu.VMEM((seq, width), F32)] * 3,
        compiler_params=pltpu.CompilerParams(vmem_limit_bytes=VMEM_LIMIT),
        name="forward",
    )(x, go, length, w, sm)


def backward_call(x, length, w, sm, saved, gsm):
    seq, width = x.shape
    shapes = (((seq, width), BF16), ((3, 4, width, 768), BF16), ((16, width), F32))
    vmem = pl.BlockSpec(memory_space=pltpu.VMEM)
    smem = pl.BlockSpec(memory_space=pltpu.SMEM)
    return pl.pallas_call(
        backward_kernel,
        out_shape=[jax.ShapeDtypeStruct(s, d) for s, d in shapes],
        in_specs=[vmem, smem] + [vmem] * (3 + len(saved)),
        out_specs=[vmem] * len(shapes),
        scratch_shapes=[
            pltpu.VMEM((seq, width), F32), pltpu.VMEM((seq, width), BF16), pltpu.VMEM((2, width, seq), BF16),
            pltpu.VMEM((seq, 768), BF16), pltpu.VMEM((seq, 256), BF16), pltpu.VMEM((seq, 640), BF16),
        ],
        compiler_params=pltpu.CompilerParams(vmem_limit_bytes=VMEM_LIMIT),
        name="backward",
    )(x, length, w, sm, *saved, gsm)


def pack_attention(q, k, v, o):
    return jnp.concatenate(
        [q[:, :128], k[:, :128], v[:, :128], q[:, 128:], k[:, 128:], o[:, 128:], v[:, 128:], o[:, :128]], axis=1
    )


def shards(tokens, lengths, grad_out, qkv_weight, out_weight, up_weight, down_weight, vectors, hidden_bias):
    dp_count = lax.axis_size("dp")
    tensor_count = lax.axis_size("tensor")
    dp_rank = lax.axis_index("dp")
    tensor_rank = lax.axis_index("tensor")
    width = tokens.shape[2]
    seq = tokens.shape[1] * tensor_count
    part = width // dp_count

    own = jnp.stack([
        pack_attention(qkv_weight[0], qkv_weight[1], qkv_weight[2], out_weight.T), up_weight, down_weight.T
    ])
    w = lax.all_gather(lax.all_gather(own, "dp", axis=1, tiled=True), "tensor", axis=1)
    vec = lax.all_gather(vectors, "dp", axis=1, tiled=True).astype(F32)
    hb = lax.all_gather(hidden_bias, "dp", axis=0, tiled=True).astype(F32).reshape(4, 768)
    qb = vec[0].reshape(4, 192)
    vb = vec[1].reshape(4, 192)
    none = jnp.zeros((4, 128), F32)
    qkvb = jnp.concatenate(
        [qb[:, :128], none, vb[:, :128], qb[:, 128:], none, vb[:, 128:], none], axis=1
    )
    sm = jnp.concatenate([vec, hb, qkvb], axis=0)
    x = lax.all_to_all(tokens, "tensor", 0, 1, tiled=True)[0]
    go = lax.all_to_all(grad_out, "tensor", 0, 1, tiled=True)[0]
    length = lax.dynamic_slice_in_dim(lengths, tensor_rank, 1).reshape(1, 1)

    out, *saved, gsm = forward_call(x, go, length, w, sm)
    gtok, grads, gsm = backward_call(x, length, w, sm, saved, gsm)

    output = lax.all_to_all(out[None], "tensor", 1, 0, tiled=True)
    grad_tokens = lax.all_to_all(gtok[None], "tensor", 1, 0, tiled=True).astype(F32)
    g = lax.psum_scatter(grads, "tensor", scatter_dimension=1)
    g = lax.psum_scatter(g, "dp", scatter_dimension=1, tiled=True).astype(F32)
    a = g[0]
    gq = jnp.concatenate([a[:, 0:128], a[:, 384:448]], axis=1)
    gk = jnp.concatenate([a[:, 128:256], a[:, 448:512]], axis=1)
    gv = jnp.concatenate([a[:, 256:384], a[:, 576:640]], axis=1)
    gout = jnp.concatenate([a[:, 640:768], a[:, 512:576]], axis=1).T
    gsm = lax.psum(gsm, ("dp", "tensor"))
    packed = gsm[12:16]
    row_q = jnp.concatenate([packed[:, 0:128], packed[:, 384:448]], axis=1).reshape(1, width)
    row_v = jnp.concatenate([packed[:, 256:384], packed[:, 576:640]], axis=1).reshape(1, width)
    rows = jnp.concatenate([row_q, row_v, gsm[2:8]], axis=0)
    grad_vectors = lax.dynamic_slice_in_dim(rows, dp_rank * part, part, 1)
    units = gsm[8:12].reshape(-1)
    grad_bias = lax.dynamic_slice_in_dim(units, dp_rank * (part * 4), part * 4)
    return output, grad_tokens, jnp.stack([gq, gk, gv]), gout, g[1], g[2].T, grad_vectors, grad_bias


def solution(mesh):
    in_specs = (
        P("dp", "tensor", None), P("dp"), P("dp", "tensor", None), P(None, "dp", "tensor"), P("tensor", "dp"),
        P("dp", "tensor"), P("tensor", "dp"), P(None, "dp"), P("dp"),
    )
    out_specs = (
        P("dp", "tensor", None), P("dp", "tensor", None), P(None, "dp", "tensor"), P("tensor", "dp"),
        P("dp", "tensor"), P("tensor", "dp"), P(None, "dp"), P("dp"),
    )
    return jax.shard_map(shards, mesh=mesh, in_specs=in_specs, out_specs=out_specs, check_vma=False)
```

```python
import functools

import jax
import jax.numpy as jnp
import numpy as np
from jax import lax
from jax.experimental import pallas as pl
from jax.experimental.pallas import tpu as pltpu
from jax.sharding import PartitionSpec as P

HD = 64
EPS = 1e-12
NEG = -1e30
F32 = jnp.float32
BF16 = jnp.bfloat16
VMEM_LIMIT = 67043328
ROWS = 128


def dot(left, right):
    return lax.dot_general(left, right, (((1,), (0,)), ((), ())), preferred_element_type=F32)


def dot_nt(left, right):
    return lax.dot_general(left, right, (((1,), (1,)), ((), ())), preferred_element_type=F32)


def lane_masks(scale):
    lane = lax.broadcasted_iota(jnp.int32, (1, 128), 1)
    low = jnp.where(lane < HD, F32(scale), F32(0)).astype(BF16)
    high = jnp.where(lane < HD, F32(0), F32(scale)).astype(BF16)
    return low, high


def is_low(shape):
    return lax.broadcasted_iota(jnp.int32, shape, 1) < HD


def put_row(ref, row, span, value):
    old = ref[8:16, span]
    here = lax.broadcasted_iota(jnp.int32, old.shape, 0) == row
    ref[8:16, span] = jnp.where(here, value, old)


def forward_kernel(
    x_ref, go_ref, len_ref, w_ref, sm_ref,
    out_ref, qkv_ref, ctx_ref, act_ref, gp_ref, hb_ref, n1_ref, s1_ref, g2_ref, stat_ref, gsm_ref,
    acc, hid, pre,
):
    seq, width = x_ref.shape
    blocks = seq // ROWS
    low, high = lane_masks(0.125)
    length = len_ref[0, 0]
    key_bias = jnp.where(lax.broadcasted_iota(jnp.int32, (1, seq), 1) < length, F32(0), F32(NEG))

    acc[...] = jnp.zeros_like(acc)

    @pl.loop(0, 4)
    def _(t):
        proj = dot(x_ref[...], w_ref[0, t, :, 0:640]) + sm_ref[pl.ds(12 + t, 1), 0:640]
        qkv_ref[t, :, 0:640] = proj.astype(BF16)
        q_two = pltpu.roll(jnp.where(is_low((seq, 128)), proj[:, 384:512] * 0.125, 0.0), 64, 1)
        qkv_ref[t, :, 640:768] = q_two.astype(BF16)

        @pl.loop(0, seq // 256)
        def _(r):
            rows = pl.ds(pl.multiple_of(r * 256, 256), 256)
            q_pair = qkv_ref[t, rows, 0:128]
            outs = []
            stats = []
            for h in range(3):
                if h < 2:
                    queries = q_pair * (low, high)[h]
                    keys = qkv_ref[t, :, 128:256]
                    values = qkv_ref[t, :, 256:384]
                else:
                    queries = qkv_ref[t, rows, 640:768]
                    keys = qkv_ref[t, :, 384:512]
                    values = qkv_ref[t, :, 512:640]
                scores = dot_nt(queries, keys) + key_bias
                highest = jnp.max(scores, axis=1, keepdims=True)
                grown = jnp.exp(scores - highest)
                total = jnp.sum(grown, axis=1, keepdims=True)
                probs = (grown * (1.0 / total)).astype(BF16)
                outs.append(dot(probs, values))
                stats.append(highest + jnp.log(total))
            lowest = is_low((256, 128))
            ctx_ref[t, rows, 0:128] = jnp.where(lowest, pltpu.roll(outs[2], 64, 1), 0.0).astype(BF16)
            ctx_ref[t, rows, 128:256] = jnp.where(lowest, outs[0], outs[1]).astype(BF16)
            lane = lax.broadcasted_iota(jnp.int32, (256, 128), 1)
            stat = jnp.where(lane == 0, stats[0], jnp.where(lane == 1, stats[1], stats[2]))
            stat_ref[t, rows, :] = stat

        acc[...] += dot_nt(ctx_ref[t], w_ref[0, t, :, 512:768])

    @pl.loop(0, blocks)
    def _(r):
        rows = pl.ds(pl.multiple_of(r * ROWS, ROWS), ROWS)
        resid = x_ref[rows, :].astype(F32) + acc[rows, :] + sm_ref[2:3, :]
        centred = resid - jnp.mean(resid, axis=1, keepdims=True)
        scale = lax.rsqrt(jnp.mean(centred * centred, axis=1, keepdims=True) + EPS)
        normed = centred * scale
        hidden = normed * sm_ref[3:4, :] + sm_ref[4:5, :]
        n1_ref[rows, :] = normed
        s1_ref[rows, :] = jnp.broadcast_to(scale, (ROWS, 128))
        hid[rows, :] = hidden
        hb_ref[rows, :] = hidden.astype(BF16)
        acc[rows, :] = hidden + sm_ref[5:6, :]

    @pl.loop(0, 4)
    def _(t):
        pre[...] = dot(hb_ref[...], w_ref[1, t])

        @pl.loop(0, blocks)
        def _(r):
            rows = pl.ds(pl.multiple_of(r * ROWS, ROWS), ROWS)
            u = pre[rows, :] + sm_ref[pl.ds(8 + t, 1), :]
            cdf = 0.5 + 0.5 * lax.erf(u * F32(np.sqrt(0.5)))
            density = jnp.exp(u * u * -0.5) * F32(1.0 / np.sqrt(2.0 * np.pi))
            act_ref[t, rows, :] = (u * cdf).astype(BF16)
            gp_ref[t, rows, :] = cdf + u * density

        acc[...] += dot_nt(act_ref[t], w_ref[2, t])

    gsm_ref[...] = jnp.zeros_like(gsm_ref)

    @pl.loop(0, blocks)
    def _(r):
        rows = pl.ds(pl.multiple_of(r * ROWS, ROWS), ROWS)
        resid = acc[rows, :]
        centred = resid - jnp.mean(resid, axis=1, keepdims=True)
        scale = lax.rsqrt(jnp.mean(centred * centred, axis=1, keepdims=True) + EPS)
        normed = centred * scale
        gain = sm_ref[6:7, :]
        out_ref[rows, :] = (normed * gain + sm_ref[7:8, :]).astype(BF16)
        cot = go_ref[rows, :].astype(F32)
        e = cot * gain
        en = jnp.mean(e * normed, axis=1, keepdims=True)
        grad = scale * (e - jnp.mean(e, axis=1, keepdims=True) - normed * en)
        g2_ref[rows, :] = grad
        gsm_ref[5:6, :] += jnp.sum(grad, axis=0, keepdims=True)
        gsm_ref[6:7, :] += jnp.sum(cot * normed, axis=0, keepdims=True)
        gsm_ref[7:8, :] += jnp.sum(cot, axis=0, keepdims=True)


def backward_kernel(
    x_ref, len_ref, w_ref, sm_ref, qkv_ref, ctx_ref, act_ref, gp_ref, hb_ref, n1_ref, s1_ref, g2_ref, stat_ref,
    gsm_in,
    gtok_ref, g_ref, gsm_ref,
    acc, low_grad, tall, gpre, gctx, gpacked,
):
    seq, width = x_ref.shape
    blocks = seq // ROWS
    low, high = lane_masks(0.125)
    one_low, one_high = lane_masks(1.0)
    length = len_ref[0, 0]
    key_bias = jnp.where(lax.broadcasted_iota(jnp.int32, (seq, 1), 0) < length, F32(0), F32(NEG))
    gsm_ref[0:8, :] = gsm_in[0:8, :]
    gsm_ref[8:16, :] = jnp.zeros((8, gsm_ref.shape[1]), F32)

    low_grad[...] = g2_ref[...].astype(BF16)
    tall[0] = jnp.transpose(g2_ref[...]).astype(BF16)
    tall[1] = jnp.transpose(hb_ref[...].astype(F32)).astype(BF16)
    acc[...] = g2_ref[...]

    @pl.loop(0, 4)
    def _(t):
        g_ref[2, t] = dot(tall[0], act_ref[t]).astype(BF16)
        grad_act = dot(low_grad[...], w_ref[2, t])
        grad_pre = grad_act * gp_ref[t]
        put_row(gsm_ref, t, slice(0, 768), jnp.sum(grad_pre, axis=0, keepdims=True))
        gpre[...] = grad_pre.astype(BF16)
        g_ref[1, t] = dot(tall[1], gpre[...]).astype(BF16)
        acc[...] += dot_nt(gpre[...], w_ref[1, t])

    @pl.loop(0, blocks)
    def _(r):
        rows = pl.ds(pl.multiple_of(r * ROWS, ROWS), ROWS)
        cot = acc[rows, :]
        normed = n1_ref[rows, :]
        e = cot * sm_ref[3:4, :]
        en = jnp.mean(e * normed, axis=1, keepdims=True)
        grad = s1_ref[rows, 0:1] * (e - jnp.mean(e, axis=1, keepdims=True) - normed * en)
        acc[rows, :] = grad
        low_grad[rows, :] = grad.astype(BF16)
        gsm_ref[2:3, :] += jnp.sum(grad, axis=0, keepdims=True)
        gsm_ref[3:4, :] += jnp.sum(cot * normed, axis=0, keepdims=True)
        gsm_ref[4:5, :] += jnp.sum(cot, axis=0, keepdims=True)

    tall[0] = jnp.transpose(acc[...]).astype(BF16)
    tall[1] = jnp.transpose(x_ref[...].astype(F32)).astype(BF16)

    @pl.loop(0, 4)
    def _(t):
        back = dot(low_grad[...], w_ref[0, t, :, 512:768])
        gctx[:, 0:128] = pltpu.roll(jnp.where(is_low((seq, 128)), back[:, 0:128], 0.0), 64, 1).astype(BF16)
        gctx[:, 128:256] = back[:, 128:256].astype(BF16)
        log_rows = jnp.transpose(stat_ref[t])
        grads_q = []
        grads_k = []
        grads_v = []
        for h in range(3):
            if h < 2:
                queries = qkv_ref[t, :, 0:128] * (low, high)[h]
                keys = qkv_ref[t, :, 128:256]
                values = qkv_ref[t, :, 256:384]
                cots = gctx[:, 128:256] * (one_low, one_high)[h]
            else:
                queries = qkv_ref[t, :, 640:768]
                keys = qkv_ref[t, :, 384:512]
                values = qkv_ref[t, :, 512:640]
                cots = gctx[:, 0:128]
            scores = dot_nt(keys, queries) + key_bias
            probs = jnp.exp(scores - log_rows[h : h + 1, :])
            grad_probs = dot_nt(values, cots)
            row_dots = jnp.sum(grad_probs * probs, axis=0, keepdims=True)
            grad_scores = (probs * (grad_probs - row_dots)).astype(BF16)
            grads_v.append(dot(probs.astype(BF16), cots))
            grads_k.append(dot(grad_scores, queries))
            part = (0, HD, HD)[h]
            keys_tall = jnp.transpose(keys.astype(F32))[part : part + HD, :].astype(BF16)
            grads_q.append(dot(keys_tall, grad_scores) * 0.125)
        pair = jnp.transpose(jnp.concatenate([grads_q[0], grads_q[1]], axis=0))
        single = jnp.transpose(jnp.concatenate([grads_q[2], jnp.zeros_like(grads_q[2])], axis=0))
        tiles = [pair, grads_k[0] + grads_k[1], grads_v[0] + grads_v[1], single + grads_k[2], grads_v[2]]
        for i, tile in enumerate(tiles):
            span = slice(128 * i, 128 * i + 128)
            put_row(gsm_ref, 4 + t, span, jnp.sum(tile, axis=0, keepdims=True))
            gpacked[:, span] = tile.astype(BF16)
        g_ref[0, t, :, 0:512] = dot(tall[1], gpacked[:, 0:512]).astype(BF16)
        g_ref[0, t, :, 512:640] = (
            dot(tall[1], gpacked[:, 512:640]) + dot(tall[0], ctx_ref[t, :, 0:128])
        ).astype(BF16)
        g_ref[0, t, :, 640:768] = dot(tall[0], ctx_ref[t, :, 128:256]).astype(BF16)
        acc[...] += dot_nt(gpacked[...], w_ref[0, t, :, 0:640])

    gtok_ref[...] = acc[...].astype(BF16)


def forward_call(x, go, length, w, sm):
    seq, width = x.shape
    shapes = (
        ((seq, width), BF16), ((4, seq, 768), BF16), ((4, seq, 256), BF16), ((4, seq, 768), BF16),
        ((4, seq, 768), F32), ((seq, width), BF16), ((seq, width), F32), ((seq, 128), F32),
        ((seq, width), F32), ((4, seq, 128), F32), ((16, width), F32),
    )
    vmem = pl.BlockSpec(memory_space=pltpu.VMEM)
    smem = pl.BlockSpec(memory_space=pltpu.SMEM)
    return pl.pallas_call(
        forward_kernel,
        out_shape=[jax.ShapeDtypeStruct(s, d) for s, d in shapes],
        in_specs=[vmem, vmem, smem, vmem, vmem],
        out_specs=[vmem] * len(shapes),
        scratch_shapes=[pltpu.VMEM((seq, width), F32)] * 3,
        compiler_params=pltpu.CompilerParams(vmem_limit_bytes=VMEM_LIMIT),
        name="forward",
    )(x, go, length, w, sm)


def backward_call(x, length, w, sm, saved, gsm):
    seq, width = x.shape
    shapes = (((seq, width), BF16), ((3, 4, width, 768), BF16), ((16, width), F32))
    vmem = pl.BlockSpec(memory_space=pltpu.VMEM)
    smem = pl.BlockSpec(memory_space=pltpu.SMEM)
    return pl.pallas_call(
        backward_kernel,
        out_shape=[jax.ShapeDtypeStruct(s, d) for s, d in shapes],
        in_specs=[vmem, smem] + [vmem] * (3 + len(saved)),
        out_specs=[vmem] * len(shapes),
        scratch_shapes=[
            pltpu.VMEM((seq, width), F32), pltpu.VMEM((seq, width), BF16), pltpu.VMEM((2, width, seq), BF16),
            pltpu.VMEM((seq, 768), BF16), pltpu.VMEM((seq, 256), BF16), pltpu.VMEM((seq, 640), BF16),
        ],
        compiler_params=pltpu.CompilerParams(vmem_limit_bytes=VMEM_LIMIT),
        name="backward",
    )(x, length, w, sm, *saved, gsm)


class Place:
    def __init__(self, dp_count):
        self.stride = dp_count // 8
        dp_rank = lax.axis_index("dp")
        tensor_rank = lax.axis_index("tensor")
        group = dp_rank // self.stride
        self.rest = dp_rank % self.stride
        self.z, self.x = group // 2, group % 2
        self.y, self.c = tensor_rank // 2, tensor_rank % 2

    def device(self, z, x, y, c):
        return ((z * 2 + x) * self.stride + self.rest, y * 2 + c)

    def shifted(self, j, second, first, other=False):
        if other:
            second, first = first, second
        across_x = self.c * second + (1 - self.c) * first
        across_y = self.c * first + (1 - self.c) * second
        return (self.z + j) % 4, (self.x + across_x) % 2, (self.y + across_y) % 2

    def first(self):
        return self.device(*self.shifted(0, 0, 1), self.c)

    def second(self):
        return self.device(*self.shifted(0, 1, 0), self.c)

    def partner(self):
        return self.device(self.z, self.x, self.y, 1 - self.c)

    def along(self, j):
        return self.device((self.z + j) % 4, self.x, self.y, self.c)

    def in_tensor(self, r):
        return self.device(self.z, self.x, (self.y + r // 2) % 2, (self.c + r % 2) % 2)

    def in_dp(self, j, i):
        return self.device((self.z + j) % 4, (self.x + i) % 2, self.y, self.c)


def remote(src, dst, send, recv, device):
    return pltpu.make_async_remote_copy(
        src_ref=src, dst_ref=dst, send_sem=send, recv_sem=recv, device_id=device,
        device_id_type=pl.DeviceIdType.MESH,
    )


def barrier(place):
    sem = pltpu.get_barrier_semaphore()
    peers = [place.in_dp(j, i) for j in range(4) for i in range(2) if j or i]
    peers += [place.in_tensor(r) for r in range(1, 4)]
    for peer in peers:
        pl.semaphore_signal(sem, inc=1, device_id=peer, device_id_type=pl.DeviceIdType.MESH)
    pl.semaphore_wait(sem, len(peers))


class Gather:
    def __init__(self, place, own, w, send, recv):
        self.place, self.own, self.w, self.send, self.recv = place, own, w, send, recv
        self.sent = []

    def piece(self, k, s, f, j):
        z, x, y = self.place.shifted(j, s, f)
        return self.w.at[k, y * 2 + self.place.c, pl.ds(pl.multiple_of((z * 2 + x) * 96, 96), 96), :]

    def push(self, k, src, dst, send, recv, device):
        copy = remote(src, dst, self.send.at[k, send], self.recv.at[k, recv], device)
        copy.start()
        self.sent.append(copy)

    def forward(self, k, s, f, j, to):
        here = self.piece(k, s, f, j)
        src = self.own.at[k] if (s, f, j) == (0, 0, 0) else here
        if "f" in to:
            self.push(k, src, here, 3 + j, 4 + j, self.place.first())
        if "s" in to:
            self.push(k, src, here, 7 + 4 * f + j, 8 + 4 * f + j, self.place.second())
        if "p" in to:
            self.push(k, src, here, 15 + 8 * s + 4 * f + j, 16 + 8 * s + 4 * f + j, self.place.partner())

    def along(self, k):
        for j in (1, 3, 2):
            self.push(k, self.own.at[k], self.piece(k, 0, 0, 0), j - 1, 4 - j, self.place.along(j))

    def wait(self, k, slot):
        here = self.own.at[k]
        remote(here, here, self.send.at[k, 0], self.recv.at[k, slot], self.place.partner()).wait_recv()

    def relay(self, k, s, f, j):
        self.wait(k, 8 * s + 4 * f + j)
        self.forward(k, s, f, j, "p" if s else "sp" if f else "fsp")

    def finish(self):
        for copy in self.sent:
            copy.wait_send()


def gather_kernel(
    dp_count, x_in, go_in, own, small_in,
    w, x_out, go_out, small_out,
    send, recv, local, tok_send, tok_recv, small_send, small_recv,
):
    place = Place(dp_count)
    tensor_rank = lax.axis_index("tensor")
    rows = pl.ds(pl.multiple_of(tensor_rank * 128, 128), 128)
    barrier(place)
    gather = Gather(place, own, w, send, recv)
    copies = []
    for i, (src, dst) in enumerate(((x_in, x_out), (go_in, go_out))):
        here = pltpu.make_async_copy(src.at[tensor_rank], dst.at[rows, :], local.at[i])
        here.start()
        copies.append(here)
    for k in range(3):
        here = pltpu.make_async_copy(own.at[k], gather.piece(k, 0, 0, 0), local.at[2 + k])
        here.start()
        copies.append(here)
    tokens = []
    def send_tokens(i, src, dst):
        for r in (2, 3, 1):
            other = ((place.y + r // 2) % 2) * 2 + (place.c + r % 2) % 2
            copy = remote(src.at[other], dst.at[rows, :], tok_send.at[i, r], tok_recv.at[i, r], place.in_tensor(r))
            copy.start()
            tokens.append(copy)
    send_tokens(0, x_in, x_out)
    here = pltpu.make_async_copy(small_in, small_out.at[0], local.at[5])
    here.start()
    copies.append(here)
    for j in range(4):
        for i in range(2):
            if j or i:
                slot = ((4 - j) % 4) * 2 + i
                copy = remote(small_in, small_out.at[slot], small_send.at[slot], small_recv.at[slot], place.in_dp(j, i))
                copy.start()
                tokens.append(copy)
    for k in range(3):
        gather.along(k)
        gather.forward(k, 0, 0, 0, "fsp")
        if k == 1:
            send_tokens(1, go_in, go_out)
    for k in range(3):
        for j in (1, 3, 2):
            gather.relay(k, 0, 0, j)
        for j in (0, 1, 3, 2):
            gather.relay(k, 0, 1, j)
        for f in range(2):
            for j in (0, 1, 3, 2):
                gather.relay(k, 1, f, j)
    for k in range(3):
        for slot in range(16, 32):
            gather.wait(k, slot)
    for copy in tokens:
        copy.wait()
    for copy in copies:
        copy.wait()
    gather.finish()


def gather_call(dp_count, tokens, grad_out, own, small):
    seq, width = tokens.shape[0] * tokens.shape[1], tokens.shape[2]
    shapes = (((3, 4, width, 768), BF16), ((seq, width), BF16), ((seq, width), BF16), ((8, 16, width), BF16))
    vmem = pl.BlockSpec(memory_space=pltpu.VMEM)
    dma = pltpu.SemaphoreType.DMA
    return pl.pallas_call(
        functools.partial(gather_kernel, dp_count),
        out_shape=[jax.ShapeDtypeStruct(s, d) for s, d in shapes],
        in_specs=[vmem] * 4,
        out_specs=[vmem] * 4,
        scratch_shapes=[dma((3, 31)), dma((3, 32)), dma((6,)), dma((2, 4)), dma((2, 4)), dma((8,)), dma((8,))],
        compiler_params=pltpu.CompilerParams(
            vmem_limit_bytes=VMEM_LIMIT, collective_id=0, has_side_effects=True
        ),
        name="gather",
    )(tokens, grad_out, own, small)


class Scatter:
    def __init__(self, place, g, inbox, out, send, recv):
        self.place, self.g, self.inbox, self.out, self.send, self.recv = place, g, inbox, out, send, recv
        self.sent = []

    def piece(self, k, s, f, j, other=False):
        z, x, y = self.place.shifted(j, s, f, other)
        core = 1 - self.place.c if other else self.place.c
        return (k, y * 2 + core, pl.multiple_of((z * 2 + x) * 96, 96))

    def push(self, k, where, slot, device):
        kind, t, row = where
        copy = remote(
            self.g.at[kind, t, pl.ds(row, 96), :], self.inbox.at[k, slot - 1],
            self.send.at[k, slot - 1], self.recv.at[k, slot - 1], device,
        )
        copy.start()
        self.sent.append(copy)

    def to_partner(self, k, s, f):
        for j in range(4):
            self.push(k, self.piece(k, s, f, j, True), 16 + 8 * s + 4 * f + j, self.place.partner())

    def wait(self, k, slot):
        here = self.inbox.at[k, slot - 1]
        remote(here, here, self.send.at[k, slot - 1], self.recv.at[k, slot - 1], self.place.partner()).wait_recv()

    def add(self, k, s, f, j):
        slots = [16 + 8 * s + 4 * f + j]
        if not s:
            slots.append(8 + 4 * f + j)
        if not s and not f:
            slots.append(4 + j)
        last = (s, f, j) == (0, 0, 0)
        if last:
            slots += [1, 2, 3]
        for slot in slots:
            self.wait(k, slot)
        kind, t, row = self.piece(k, s, f, j)

        @pl.loop(0, 3)
        def _(r):
            lines = pl.ds(pl.multiple_of(row + r * 32, 32), 32)
            total = self.g[kind, t, lines, :].astype(F32)
            for slot in slots:
                total += self.inbox[k, slot - 1, pl.ds(pl.multiple_of(r * 32, 32), 32), :].astype(F32)
            if last:
                self.out[k, pl.ds(pl.multiple_of(r * 32, 32), 32), :] = total
            else:
                self.g[kind, t, lines, :] = total.astype(BF16)

        if last:
            return
        if s:
            self.push(k, (kind, t, row), 8 + 4 * f + j, self.place.second())
        elif f:
            self.push(k, (kind, t, row), 4 + j, self.place.first())
        else:
            self.push(k, (kind, t, row), 4 - j, self.place.along(j))

    def finish(self):
        for copy in self.sent:
            copy.wait_send()


def sum_small(place, stages, inbox, out, send, recv):
    hops = [(0, place.partner()), (1, place.second()), (2, place.first())]
    sent = []
    for i, peer in hops:
        copy = remote(stages.at[i], inbox.at[i], send.at[i], recv.at[i], peer)
        copy.start()
        copy.wait_recv()
        sent.append(copy)
        stages[i + 1] = stages[i] + inbox[i]
    for j in range(1, 4):
        copy = remote(stages.at[3], inbox.at[6 - j], send.at[6 - j], recv.at[6 - j], place.along(j))
        copy.start()
        sent.append(copy)
    for copy in sent[3:]:
        copy.wait_recv()
    out[...] = (stages[3] + inbox[3]) + (inbox[4] + inbox[5])
    for copy in sent:
        copy.wait_send()


def scatter_kernel(
    dp_count, out_in, gtok_in, grads, small_in,
    output, gtok, shard, small,
    g, inbox, stages, small_inbox, send, recv, local, tok_send, tok_recv, small_send, small_recv,
):
    place = Place(dp_count)
    tensor_rank = lax.axis_index("tensor")
    load = pltpu.make_async_copy(grads, g, local.at[2])
    load.start()
    barrier(place)
    tokens = []
    for i, (src, dst) in enumerate(((out_in, output), (gtok_in, gtok))):
        for r in (2, 3, 1):
            other = ((place.y + r // 2) % 2) * 2 + (place.c + r % 2) % 2
            rows = pl.ds(pl.multiple_of(other * 128, 128), 128)
            copy = remote(src.at[rows, :], dst.at[tensor_rank], tok_send.at[i, r], tok_recv.at[i, r], place.in_tensor(r))
            copy.start()
            tokens.append(copy)
        rows = pl.ds(pl.multiple_of(tensor_rank * 128, 128), 128)
        here = pltpu.make_async_copy(src.at[rows, :], dst.at[tensor_rank], local.at[i])
        here.start()
        tokens.append(here)
    load.wait()
    scatter = Scatter(place, g, inbox, shard, send, recv)
    for k in (2, 1, 0):
        for s in (1, 0):
            for f in (1, 0):
                scatter.to_partner(k, s, f)
    stages[0] = small_in[...]
    sum_small(place, stages, small_inbox, small, small_send, small_recv)
    order = (2, 1, 0)
    for k in order:
        for f in (1, 0):
            for j in (2, 1, 3, 0):
                scatter.add(k, 1, f, j)
    for k in order:
        for j in (2, 1, 3, 0):
            scatter.add(k, 0, 1, j)
    for k in order:
        for j in (2, 1, 3):
            scatter.add(k, 0, 0, j)
    for k in order:
        scatter.add(k, 0, 0, 0)
    for copy in tokens:
        copy.wait()
    scatter.finish()


def scatter_call(dp_count, out, gtok, grads, small):
    seq, width = out.shape
    shapes = (((4, seq // 4, width), BF16), ((4, seq // 4, width), BF16), ((3, 96, width), F32), ((16, width), F32))
    vmem = pl.BlockSpec(memory_space=pltpu.VMEM)
    dma = pltpu.SemaphoreType.DMA
    return pl.pallas_call(
        functools.partial(scatter_kernel, dp_count),
        out_shape=[jax.ShapeDtypeStruct(s, d) for s, d in shapes],
        in_specs=[vmem, vmem, pl.BlockSpec(memory_space=pl.ANY), vmem],
        out_specs=[vmem] * 4,
        scratch_shapes=[
            pltpu.VMEM(grads.shape, BF16), pltpu.VMEM((3, 31, 96, width), BF16),
            pltpu.VMEM((4, 16, width), F32), pltpu.VMEM((6, 16, width), F32),
            dma((3, 31)), dma((3, 31)), dma((3,)), dma((2, 4)), dma((2, 4)), dma((6,)), dma((6,)),
        ],
        compiler_params=pltpu.CompilerParams(
            vmem_limit_bytes=VMEM_LIMIT, collective_id=1, has_side_effects=True
        ),
        name="scatter",
    )(out, gtok, grads, small)


def gather_groups(shard, dp_count, axis):
    stride = dp_count // 8
    if stride == 1:
        return shard
    groups = [[g * stride + i for i in range(stride)] for g in range(8)]
    return lax.all_gather(shard, "dp", axis=axis, tiled=True, axis_index_groups=groups)


def scatter_groups(shard, small, dp_count):
    stride = dp_count // 8
    if stride == 1:
        return shard, small
    groups = [[g * stride + i for i in range(stride)] for g in range(8)]
    shard = lax.psum_scatter(shard, "dp", scatter_dimension=1, tiled=True, axis_index_groups=groups)
    return shard, lax.psum(small, "dp", axis_index_groups=groups)


def pack_small(vectors, bias, dp_count, width):
    group = lax.axis_index("dp") // (dp_count // 8)
    part = vectors.shape[1]
    rows = lax.dynamic_update_slice(jnp.zeros((8, width), BF16), vectors, (0, group * part))
    units = lax.dynamic_update_slice(jnp.zeros((4 * width,), BF16), bias, (group * (4 * part),))
    qb = rows[0].reshape(4, 192)
    vb = rows[1].reshape(4, 192)
    none = jnp.zeros((4, 128), BF16)
    packed = jnp.concatenate([qb[:, :128], none, vb[:, :128], qb[:, 128:], none, vb[:, 128:], none], axis=1)
    return jnp.concatenate([rows, units.reshape(4, width), packed], axis=0)


def pack_attention(q, k, v, o):
    return jnp.concatenate(
        [q[:, :128], k[:, :128], v[:, :128], q[:, 128:], k[:, 128:], o[:, 128:], v[:, 128:], o[:, :128]], axis=1
    )


def shards(tokens, lengths, grad_out, qkv_weight, out_weight, up_weight, down_weight, vectors, hidden_bias):
    dp_count = lax.axis_size("dp")
    tensor_count = lax.axis_size("tensor")
    dp_rank = lax.axis_index("dp")
    tensor_rank = lax.axis_index("tensor")
    width = tokens.shape[2]
    seq = tokens.shape[1] * tensor_count
    part = width // dp_count

    own = jnp.stack([
        pack_attention(qkv_weight[0], qkv_weight[1], qkv_weight[2], out_weight.T), up_weight, down_weight.T
    ])
    own = gather_groups(own, dp_count, 1)
    small = pack_small(gather_groups(vectors, dp_count, 1), gather_groups(hidden_bias, dp_count, 0), dp_count, width)
    w, x, go, smalls = gather_call(dp_count, tokens, grad_out, own, small)
    sm = jnp.sum(smalls.astype(F32), axis=0)
    length = lax.dynamic_slice_in_dim(lengths, tensor_rank, 1).reshape(1, 1)

    out, *saved, gsm = forward_call(x, go, length, w, sm)
    gtok, grads, gsm = backward_call(x, length, w, sm, saved, gsm)

    output, gtok, g, gsm = scatter_call(dp_count, out, gtok, grads, gsm)
    grad_tokens = gtok.astype(F32)
    g, gsm = scatter_groups(g, gsm, dp_count)
    a = g[0]
    gq = jnp.concatenate([a[:, 0:128], a[:, 384:448]], axis=1)
    gk = jnp.concatenate([a[:, 128:256], a[:, 448:512]], axis=1)
    gv = jnp.concatenate([a[:, 256:384], a[:, 576:640]], axis=1)
    gout = jnp.concatenate([a[:, 640:768], a[:, 512:576]], axis=1).T
    packed = gsm[12:16]
    row_q = jnp.concatenate([packed[:, 0:128], packed[:, 384:448]], axis=1).reshape(1, width)
    row_v = jnp.concatenate([packed[:, 256:384], packed[:, 576:640]], axis=1).reshape(1, width)
    rows = jnp.concatenate([row_q, row_v, gsm[2:8]], axis=0)
    grad_vectors = lax.dynamic_slice_in_dim(rows, dp_rank * part, part, 1)
    units = gsm[8:12].reshape(-1)
    grad_bias = lax.dynamic_slice_in_dim(units, dp_rank * (part * 4), part * 4)
    return output, grad_tokens, jnp.stack([gq, gk, gv]), gout, g[1], g[2].T, grad_vectors, grad_bias


def solution(mesh):
    in_specs = (
        P("dp", "tensor", None), P("dp"), P("dp", "tensor", None), P(None, "dp", "tensor"), P("tensor", "dp"),
        P("dp", "tensor"), P("tensor", "dp"), P(None, "dp"), P("dp"),
    )
    out_specs = (
        P("dp", "tensor", None), P("dp", "tensor", None), P(None, "dp", "tensor"), P("tensor", "dp"),
        P("dp", "tensor"), P("tensor", "dp"), P(None, "dp"), P("dp"),
    )
    return jax.shard_map(shards, mesh=mesh, in_specs=in_specs, out_specs=out_specs, check_vma=False)
```

```python
import functools

import jax
import jax.numpy as jnp
import numpy as np
from jax import lax
from jax.experimental import pallas as pl
from jax.experimental.pallas import tpu as pltpu
from jax.sharding import PartitionSpec as P

HD = 64
EPS = 1e-12
NEG = -1e30
F32 = jnp.float32
BF16 = jnp.bfloat16
VMEM_LIMIT = 67043328
ROWS = 128


def dot(left, right):
    return lax.dot_general(left, right, (((1,), (0,)), ((), ())), preferred_element_type=F32)


def dot_nt(left, right):
    return lax.dot_general(left, right, (((1,), (1,)), ((), ())), preferred_element_type=F32)


def lane_masks(scale):
    lane = lax.broadcasted_iota(jnp.int32, (1, 128), 1)
    low = jnp.where(lane < HD, F32(scale), F32(0)).astype(BF16)
    high = jnp.where(lane < HD, F32(0), F32(scale)).astype(BF16)
    return low, high


def is_low(shape):
    return lax.broadcasted_iota(jnp.int32, shape, 1) < HD


def put_row(ref, row, span, value):
    old = ref[8:16, span]
    here = lax.broadcasted_iota(jnp.int32, old.shape, 0) == row
    ref[8:16, span] = jnp.where(here, value, old)


class Place:
    def __init__(self, dp_count):
        self.stride = dp_count // 8
        dp_rank = lax.axis_index("dp")
        tensor_rank = lax.axis_index("tensor")
        group = dp_rank // self.stride
        self.rest = dp_rank % self.stride
        self.z, self.x = group // 2, group % 2
        self.y, self.c = tensor_rank // 2, tensor_rank % 2

    def device(self, z, x, y, c):
        return ((z * 2 + x) * self.stride + self.rest, y * 2 + c)

    def shifted(self, j, second, first, other=False):
        if other:
            second, first = first, second
        across_x = self.c * second + (1 - self.c) * first
        across_y = self.c * first + (1 - self.c) * second
        return (self.z + j) % 4, (self.x + across_x) % 2, (self.y + across_y) % 2

    def first(self):
        return self.device(*self.shifted(0, 0, 1), self.c)

    def second(self):
        return self.device(*self.shifted(0, 1, 0), self.c)

    def partner(self):
        return self.device(self.z, self.x, self.y, 1 - self.c)

    def along(self, j):
        return self.device((self.z + j) % 4, self.x, self.y, self.c)

    def in_tensor(self, r):
        return self.device(self.z, self.x, (self.y + r // 2) % 2, (self.c + r % 2) % 2)

    def in_dp(self, j, i):
        return self.device((self.z + j) % 4, (self.x + i) % 2, self.y, self.c)


def remote(src, dst, send, recv, device):
    return pltpu.make_async_remote_copy(
        src_ref=src, dst_ref=dst, send_sem=send, recv_sem=recv, device_id=device,
        device_id_type=pl.DeviceIdType.MESH,
    )


def barrier(place):
    sem = pltpu.get_barrier_semaphore()
    peers = [place.in_dp(j, i) for j in range(4) for i in range(2) if j or i]
    peers += [place.in_tensor(r) for r in range(1, 4)]
    for peer in peers:
        pl.semaphore_signal(sem, inc=1, device_id=peer, device_id_type=pl.DeviceIdType.MESH)
    pl.semaphore_wait(sem, len(peers))


class Gather:
    def __init__(self, place, own, w, send, recv):
        self.place, self.own, self.w, self.send, self.recv = place, own, w, send, recv

    def piece(self, k, s, f, j):
        z, x, y = self.place.shifted(j, s, f)
        return self.w.at[k, y * 2 + self.place.c, pl.ds(pl.multiple_of((z * 2 + x) * 96, 96), 96), :]

    def push(self, k, src, dst, send, recv, device):
        remote(src, dst, self.send.at[k, send], self.recv.at[k, recv], device).start()

    def forward(self, k, s, f, j, to):
        here = self.piece(k, s, f, j)
        src = self.own.at[k] if (s, f, j) == (0, 0, 0) else here
        if "f" in to:
            self.push(k, src, here, 3 + j, 4 + j, self.place.first())
        if "s" in to:
            self.push(k, src, here, 7 + 4 * f + j, 8 + 4 * f + j, self.place.second())
        if "p" in to:
            self.push(k, src, here, 15 + 8 * s + 4 * f + j, 16 + 8 * s + 4 * f + j, self.place.partner())

    def along(self, k):
        for j in (1, 3, 2):
            self.push(k, self.own.at[k], self.piece(k, 0, 0, 0), j - 1, 4 - j, self.place.along(j))

    def start(self, k):
        self.forward(k, 0, 0, 0, "fsp")

    def wait(self, k, slot):
        here = self.own.at[k]
        remote(here, here, self.send.at[k, 0], self.recv.at[k, slot], self.place.partner()).wait_recv()

    def relay(self, k, s, f, order):
        for j in order:
            self.wait(k, 8 * s + 4 * f + j)
            self.forward(k, s, f, j, "p" if s else "sp" if f else "fsp")

    def others(self, k):
        @pl.loop(16, 32)
        def _(slot):
            self.wait(k, slot)

    def finish(self):
        for k in range(3):
            here = self.own.at[k]

            @pl.loop(0, 31)
            def _(slot):
                remote(here, here, self.send.at[k, slot], self.recv.at[k, 1], self.place.partner()).wait_send()


class Scatter:
    def __init__(self, place, g, boxes, sends, recvs, out):
        self.place, self.g, self.boxes, self.sends, self.recvs, self.out = place, g, boxes, sends, recvs, out

    def push(self, stage, src, index, sem, device):
        remote(
            src, self.boxes[stage].at[index], self.sends[stage].at[sem], self.recvs[stage].at[sem], device
        ).start()

    def piece(self, k, s, f, j):
        z, x, y = self.place.shifted(j, s, f)
        return k, y * 2 + self.place.c, pl.multiple_of((z * 2 + x) * 96, 96)

    def view(self, k, s, f, j):
        kind, t, row = self.piece(k, s, f, j)
        return self.g.at[kind, t, pl.ds(row, 96), :]

    def wait(self, stage, index, sem):
        here = self.boxes[stage].at[index]
        remote(here, here, self.sends[stage].at[sem], self.recvs[stage].at[sem], self.place.partner()).wait_recv()

    def to_partner(self, k, t, i):
        self.push(0, self.g.at[k, t], (k, i), (k, i), self.place.partner())

    def from_partner(self, k, i):
        self.wait(0, (k, i), (k, i))

    def across(self, k, f):
        for j in (2, 1, 3, 0):
            self.push(1, self.view(k, 1, f, j), (k, f, j), (k, 4 * f + j), self.place.second())

    def ready(self, k, i):
        if i == 0:
            self.across(k, 1)

            @pl.when(self.place.c == 0)
            def _():
                self.across(k, 0)
        else:
            @pl.when(self.place.c == 1)
            def _():
                self.across(k, 0)

    def total(self, k, f, j, parts, last=False):
        kind, t, row = self.piece(k, 0, f, j)

        @pl.loop(0, 3)
        def _(r):
            lines = pl.ds(pl.multiple_of(row + r * 32, 32), 32)
            local = pl.ds(pl.multiple_of(r * 32, 32), 32)
            value = self.g[kind, t, lines, :].astype(F32)
            for stage, index in parts:
                value += self.boxes[stage][(*index, local, slice(None))].astype(F32)
            if last:
                self.out[k, local, :] = value
            else:
                self.g[kind, t, lines, :] = value.astype(BF16)

    def add_far(self, k):
        for j in (2, 1, 3, 0):
            self.wait(1, (k, 1, j), (k, 4 + j))
            self.total(k, 1, j, [(1, (k, 1, j))])
            self.push(2, self.view(k, 0, 1, j), (k, j), (k, j), self.place.first())

    def add_near(self, k):
        for j in (2, 1, 3):
            self.wait(1, (k, 0, j), (k, j))
            self.wait(2, (k, j), (k, j))
            self.total(k, 0, j, [(1, (k, 0, j)), (2, (k, j))])
            self.push(3, self.view(k, 0, 0, j), (k, 3 - j), (k, 3 - j), self.place.along(j))

    def add_last(self, k):
        self.wait(1, (k, 0, 0), (k, 0))
        self.wait(2, (k, 0), (k, 0))
        for i in range(3):
            self.wait(3, (k, i), (k, i))
        self.total(k, 0, 0, [(1, (k, 0, 0)), (2, (k, 0)), (3, (k, 0)), (3, (k, 1)), (3, (k, 2))], True)

    def finish(self):
        counts = ((0, 2), (1, 8), (2, 4), (3, 3))
        for k in range(3):
            for stage, count in counts:
                here = self.g.at[0, 0] if stage == 0 else self.boxes[2].at[0, 0]

                @pl.loop(0, count)
                def _(i):
                    remote(
                        here, here, self.sends[stage].at[k, i], self.recvs[stage].at[k, i], self.place.partner()
                    ).wait_send()


class SmallSum:
    def __init__(self, place, stages, inbox, send, recv):
        self.place, self.stages, self.inbox, self.send, self.recv = place, stages, inbox, send, recv
        self.sent = []

    def push(self, stage, slot, peer):
        copy = remote(self.stages.at[stage], self.inbox.at[slot], self.send.at[slot], self.recv.at[slot], peer)
        copy.start()
        self.sent.append(copy)

    def start(self, i):
        if i < 3:
            self.push(i, i, (self.place.partner, self.place.second, self.place.first)[i]())
        else:
            for j in range(1, 4):
                self.push(3, 6 - j, self.place.along(j))

    def step(self, i):
        self.sent[i].wait_recv()
        self.stages[i + 1] = self.stages[i] + self.inbox[i]
        self.start(i + 1)

    def finish(self, out):
        for copy in self.sent[3:]:
            copy.wait_recv()
        out[...] = (self.stages[3] + self.inbox[3]) + (self.inbox[4] + self.inbox[5])
        for copy in self.sent:
            copy.wait_send()


class Tokens:
    def __init__(self, place, send, recv, local):
        self.place, self.send, self.recv, self.local = place, send, recv, local
        self.rank = place.y * 2 + place.c

    def other(self, r):
        return ((self.place.y + r // 2) % 2) * 2 + (self.place.c + r % 2) % 2

    def rows(self, rank):
        return pl.ds(pl.multiple_of(rank * 128, 128), 128)

    def gather(self, i, src, dst):
        here = dst.at[self.rows(self.rank), :]
        pltpu.make_async_copy(src.at[self.rank], here, self.local.at[i]).start()
        for r in (2, 3, 1):
            remote(
                src.at[self.other(r)], here, self.send.at[i, r], self.recv.at[i, r], self.place.in_tensor(r)
            ).start()

    def spread(self, i, src, dst):
        here = dst.at[self.rank]
        pltpu.make_async_copy(src.at[self.rows(self.rank), :], here, self.local.at[i]).start()
        for r in (2, 3, 1):
            remote(
                src.at[self.rows(self.other(r)), :], here, self.send.at[i, r], self.recv.at[i, r],
                self.place.in_tensor(r),
            ).start()

    def wait(self, i, block, arrive=True, leave=True):
        for r in (1, 2, 3):
            copy = remote(block, block, self.send.at[i, r], self.recv.at[i, r], self.place.in_tensor(r))
            if arrive:
                copy.wait_recv()
            if leave:
                copy.wait_send()
        if arrive:
            pltpu.make_async_copy(block, block, self.local.at[i]).wait()


def layer_kernel(
    dp_count, x_in, go_in, own, small_in, len_ref,
    output, gtok, shard, small,
    w, x, go, smalls, sm, qkv, ctx, act, gp, hb, n1, s1, g2, stat, gsm,
    acc, pre, low_grad, tall, gpre, gctx, gpacked,
    box_p, box_s, box_f, box_z, stages, small_box,
    send, recv, tok_send, tok_recv, tok_local, own_local, bias_send, bias_recv,
    send_p, recv_p, send_s, recv_s, send_f, recv_f, send_z, recv_z, small_send, small_recv,
):
    seq, width = x.shape
    blocks = seq // ROWS
    place = Place(dp_count)
    gather = Gather(place, own, w, send, recv)
    tokens = Tokens(place, tok_send, tok_recv, tok_local)
    near = (0, 1, 3, 2)
    line = (1, 3, 2)

    barrier(place)
    gather.along(0)
    gather.start(0)
    tokens.gather(0, x_in, x)
    for k in range(3):
        pltpu.make_async_copy(own.at[k], gather.piece(k, 0, 0, 0), own_local.at[k]).start()
    pltpu.make_async_copy(small_in, smalls.at[0], own_local.at[3]).start()
    for j in range(4):
        for i in range(2):
            if j or i:
                slot = ((4 - j) % 4) * 2 + i
                remote(
                    small_in, smalls.at[slot], bias_send.at[slot], bias_recv.at[slot], place.in_dp(j, i)
                ).start()
    gather.along(1)
    gather.start(1)
    gather.along(2)
    gather.relay(0, 0, 0, line)
    gather.relay(0, 0, 1, near)
    gather.relay(0, 1, 0, near)
    gather.relay(1, 0, 0, line)
    gather.relay(0, 1, 1, near)
    gather.start(2)
    for k in range(3):
        pltpu.make_async_copy(own.at[k], own.at[k], own_local.at[k]).wait()
    pltpu.make_async_copy(small_in, small_in, own_local.at[3]).wait()

    @pl.loop(1, 8)
    def _(slot):
        remote(small_in, small_in, bias_send.at[slot], bias_recv.at[slot], place.partner()).wait()

    total = smalls[0].astype(F32)
    for i in range(1, 8):
        total += smalls[i].astype(F32)
    sm[...] = total
    tokens.wait(0, x_in.at[0])
    gather.others(0)

    low, high = lane_masks(0.125)
    length = len_ref[0, 0]
    key_bias = jnp.where(lax.broadcasted_iota(jnp.int32, (1, seq), 1) < length, F32(0), F32(NEG))
    acc[...] = jnp.zeros_like(acc)

    attention_events = {
        0: lambda: gather.relay(1, 0, 1, (0, 1)),
        1: lambda: gather.relay(1, 0, 1, (3, 2)),
        2: lambda: gather.relay(2, 0, 0, line),
        3: lambda: gather.relay(1, 1, 0, near),
        4: lambda: tokens.gather(1, go_in, go),
        5: lambda: gather.relay(1, 1, 1, near),
        6: lambda: gather.relay(2, 0, 1, (0, 1)),
        7: lambda: gather.relay(2, 0, 1, (3, 2)),
    }

    @pl.loop(0, 4)
    def _(t):
        proj = dot(x[...], w[0, t, :, 0:640]) + sm[pl.ds(12 + t, 1), 0:640]
        qkv[t, :, 0:640] = proj.astype(BF16)
        q_two = pltpu.roll(jnp.where(is_low((seq, 128)), proj[:, 384:512] * 0.125, 0.0), 64, 1)
        qkv[t, :, 640:768] = q_two.astype(BF16)

        @pl.loop(0, seq // 256)
        def _(r):
            for slot, event in attention_events.items():
                pl.when(t * 2 + r == slot)(event)
            rows = pl.ds(pl.multiple_of(r * 256, 256), 256)
            q_pair = qkv[t, rows, 0:128]
            outs = []
            stats = []
            for h in range(3):
                if h < 2:
                    queries = q_pair * (low, high)[h]
                    keys = qkv[t, :, 128:256]
                    values = qkv[t, :, 256:384]
                else:
                    queries = qkv[t, rows, 640:768]
                    keys = qkv[t, :, 384:512]
                    values = qkv[t, :, 512:640]
                scores = dot_nt(queries, keys) + key_bias
                highest = jnp.max(scores, axis=1, keepdims=True)
                grown = jnp.exp(scores - highest)
                total = jnp.sum(grown, axis=1, keepdims=True)
                probs = (grown * (1.0 / total)).astype(BF16)
                outs.append(dot(probs, values))
                stats.append(highest + jnp.log(total))
            lowest = is_low((256, 128))
            ctx[t, rows, 0:128] = jnp.where(lowest, pltpu.roll(outs[2], 64, 1), 0.0).astype(BF16)
            ctx[t, rows, 128:256] = jnp.where(lowest, outs[0], outs[1]).astype(BF16)
            lane = lax.broadcasted_iota(jnp.int32, (256, 128), 1)
            stat[t, rows, :] = jnp.where(lane == 0, stats[0], jnp.where(lane == 1, stats[1], stats[2]))

        acc[...] += dot_nt(ctx[t], w[0, t, :, 512:768])

    @pl.loop(0, blocks)
    def _(r):
        rows = pl.ds(pl.multiple_of(r * ROWS, ROWS), ROWS)
        resid = x[rows, :].astype(F32) + acc[rows, :] + sm[2:3, :]
        centred = resid - jnp.mean(resid, axis=1, keepdims=True)
        scale = lax.rsqrt(jnp.mean(centred * centred, axis=1, keepdims=True) + EPS)
        normed = centred * scale
        hidden = normed * sm[3:4, :] + sm[4:5, :]
        n1[rows, :] = normed
        s1[rows, :] = jnp.broadcast_to(scale, (ROWS, 128))
        hb[rows, :] = hidden.astype(BF16)
        acc[rows, :] = hidden + sm[5:6, :]

    gather.relay(2, 1, 0, (0, 1))
    gather.others(1)
    up_events = {
        1: lambda: gather.relay(2, 1, 0, (3, 2)),
        2: lambda: gather.relay(2, 1, 1, (0, 1)),
        3: lambda: gather.relay(2, 1, 1, (3, 2)),
    }

    @pl.loop(0, 4)
    def _(t):
        for slot, event in up_events.items():
            pl.when(t == slot)(event)
        pre[...] = dot(hb[...], w[1, t])

        @pl.loop(0, blocks)
        def _(r):
            rows = pl.ds(pl.multiple_of(r * ROWS, ROWS), ROWS)
            u = pre[rows, :] + sm[pl.ds(8 + t, 1), :]
            cdf = 0.5 + 0.5 * lax.erf(u * F32(np.sqrt(0.5)))
            density = jnp.exp(u * u * -0.5) * F32(1.0 / np.sqrt(2.0 * np.pi))
            act[t, rows, :] = (u * cdf).astype(BF16)
            gp[t, rows, :] = (cdf + u * density).astype(BF16)

    gather.others(2)

    @pl.loop(0, 4)
    def _(t):
        acc[...] += dot_nt(act[t], w[2, t])

    tokens.wait(1, x_in.at[0])
    gsm[...] = jnp.zeros_like(gsm)

    @pl.loop(0, blocks)
    def _(r):
        rows = pl.ds(pl.multiple_of(r * ROWS, ROWS), ROWS)
        resid = acc[rows, :]
        centred = resid - jnp.mean(resid, axis=1, keepdims=True)
        scale = lax.rsqrt(jnp.mean(centred * centred, axis=1, keepdims=True) + EPS)
        normed = centred * scale
        gain = sm[6:7, :]
        cot = go[rows, :].astype(F32)
        go[rows, :] = (normed * gain + sm[7:8, :]).astype(BF16)
        e = cot * gain
        en = jnp.mean(e * normed, axis=1, keepdims=True)
        grad = scale * (e - jnp.mean(e, axis=1, keepdims=True) - normed * en)
        g2[rows, :] = grad
        gsm[5:6, :] += jnp.sum(grad, axis=0, keepdims=True)
        gsm[6:7, :] += jnp.sum(cot * normed, axis=0, keepdims=True)
        gsm[7:8, :] += jnp.sum(cot, axis=0, keepdims=True)

    tokens.spread(2, go, output)
    gather.finish()
    scatter = Scatter(
        place, w, (box_p, box_s, box_f, box_z), (send_p, send_s, send_f, send_z), (recv_p, recv_s, recv_f, recv_z),
        shard,
    )
    low_grad[...] = g2[...].astype(BF16)
    tall[0] = jnp.transpose(g2[...]).astype(BF16)
    tall[1] = jnp.transpose(hb[...].astype(F32)).astype(BF16)
    acc[...] = g2[...]

    def chunk(i, core):
        return ((place.y + 1 - i) % 2) * 2 + core

    def feed_back(t, store):
        grad_pre = dot(low_grad[...], w[2, t]) * gp[t].astype(F32)
        put_row(gsm, t, slice(0, 768), jnp.sum(grad_pre, axis=0, keepdims=True))
        gpre[...] = grad_pre.astype(BF16)
        store(2, dot(tall[0], act[t]))
        acc[...] += dot_nt(gpre[...], w[1, t])
        store(1, dot(tall[1], gpre[...]))

    @pl.loop(0, 2)
    def _(i):
        t = chunk(i, 1 - place.c)

        def store(k, value):
            w[k, t] = value.astype(BF16)
            scatter.to_partner(k, t, i)

        feed_back(t, store)

    @pl.loop(0, 2)
    def _(i):
        t = chunk(i, place.c)

        def store(k, value):
            scatter.from_partner(k, i)
            w[k, t] = (value + box_p[k, i].astype(F32)).astype(BF16)
            pl.when(i == 0)(lambda: scatter.ready(k, 0))
            pl.when(i == 1)(lambda: scatter.ready(k, 1))

        feed_back(t, store)

    @pl.loop(0, blocks)
    def _(r):
        rows = pl.ds(pl.multiple_of(r * ROWS, ROWS), ROWS)
        cot = acc[rows, :]
        normed = n1[rows, :]
        e = cot * sm[3:4, :]
        en = jnp.mean(e * normed, axis=1, keepdims=True)
        grad = s1[rows, 0:1] * (e - jnp.mean(e, axis=1, keepdims=True) - normed * en)
        acc[rows, :] = grad
        low_grad[rows, :] = grad.astype(BF16)
        gsm[2:3, :] += jnp.sum(grad, axis=0, keepdims=True)
        gsm[3:4, :] += jnp.sum(cot * normed, axis=0, keepdims=True)
        gsm[4:5, :] += jnp.sum(cot, axis=0, keepdims=True)

    tall[0] = jnp.transpose(acc[...]).astype(BF16)
    tall[1] = jnp.transpose(x[...].astype(F32)).astype(BF16)

    one_low, one_high = lane_masks(1.0)
    tall_bias = jnp.where(lax.broadcasted_iota(jnp.int32, (seq, 1), 0) < length, F32(0), F32(NEG))

    def attention_back(t, event, store):
        back = dot(low_grad[...], w[0, t, :, 512:768])
        gctx[:, 0:128] = pltpu.roll(jnp.where(is_low((seq, 128)), back[:, 0:128], 0.0), 64, 1).astype(BF16)
        gctx[:, 128:256] = back[:, 128:256].astype(BF16)
        log_rows = jnp.transpose(stat[t])
        grads_q = []
        grads_k = []
        grads_v = []
        for h in range(3):
            if h < 2:
                queries = qkv[t, :, 0:128] * (low, high)[h]
                keys = qkv[t, :, 128:256]
                values = qkv[t, :, 256:384]
                cots = gctx[:, 128:256] * (one_low, one_high)[h]
            else:
                queries = qkv[t, :, 640:768]
                keys = qkv[t, :, 384:512]
                values = qkv[t, :, 512:640]
                cots = gctx[:, 0:128]
            scores = dot_nt(keys, queries) + tall_bias
            probs = jnp.exp(scores - log_rows[h : h + 1, :])
            grad_probs = dot_nt(values, cots)
            row_dots = jnp.sum(grad_probs * probs, axis=0, keepdims=True)
            grad_scores = (probs * (grad_probs - row_dots)).astype(BF16)
            grads_v.append(dot(probs.astype(BF16), cots))
            grads_k.append(dot(grad_scores, queries))
            part = (0, HD, HD)[h]
            keys_tall = jnp.transpose(keys.astype(F32))[part : part + HD, :].astype(BF16)
            grads_q.append(dot(keys_tall, grad_scores) * 0.125)
        pair = jnp.transpose(jnp.concatenate([grads_q[0], grads_q[1]], axis=0))
        single = jnp.transpose(jnp.concatenate([grads_q[2], jnp.zeros_like(grads_q[2])], axis=0))
        tiles = [pair, grads_k[0] + grads_k[1], grads_v[0] + grads_v[1], single + grads_k[2], grads_v[2]]
        for i, tile in enumerate(tiles):
            span = slice(128 * i, 128 * i + 128)
            put_row(gsm, 4 + t, span, jnp.sum(tile, axis=0, keepdims=True))
            gpacked[:, span] = tile.astype(BF16)
        event()
        acc[...] += dot_nt(gpacked[...], w[0, t, :, 0:640])
        store(slice(0, 512), dot(tall[1], gpacked[:, 0:512]))
        store(slice(512, 640), dot(tall[1], gpacked[:, 512:640]) + dot(tall[0], ctx[t, :, 0:128]))
        store(slice(640, 768), dot(tall[0], ctx[t, :, 128:256]))

    @pl.loop(0, 2)
    def _(i):
        t = chunk(i, 1 - place.c)

        def store(span, value):
            w[0, t, :, span] = value.astype(BF16)

        def event():
            pl.when(i == 0)(lambda: scatter.add_far(2))
            pl.when(i == 1)(lambda: scatter.add_far(1))

        attention_back(t, event, store)
        scatter.to_partner(0, t, i)

    @pl.loop(0, 2)
    def _(i):
        t = chunk(i, place.c)

        def store(span, value):
            w[0, t, :, span] = (value + box_p[0, i, :, span].astype(F32)).astype(BF16)

        def event():
            pl.when(i == 0)(lambda: scatter.add_near(2))
            scatter.from_partner(0, i)

        attention_back(t, event, store)
        pl.when(i == 0)(lambda: scatter.ready(0, 0))
        pl.when(i == 1)(lambda: scatter.ready(0, 1))

    x[...] = acc[...].astype(BF16)
    stages[0] = gsm[...]
    sums = SmallSum(place, stages, small_box, small_send, small_recv)
    sums.start(0)
    scatter.add_near(1)
    scatter.add_far(0)
    tokens.spread(3, x, gtok)
    sums.step(0)
    scatter.add_last(2)
    sums.step(1)
    scatter.add_near(0)
    sums.step(2)
    scatter.add_last(1)
    sums.finish(small)
    scatter.add_last(0)
    for i in (2, 3):
        tokens.wait(i, x_in.at[0])
    scatter.finish()


def layer_call(dp_count, tokens, grad_out, own, small, length):
    part, width = tokens.shape[1], tokens.shape[2]
    seq = tokens.shape[0] * part
    shapes = (((4, part, width), BF16), ((4, part, width), BF16), ((3, 96, width), F32), ((16, width), F32))
    vmem = pl.BlockSpec(memory_space=pltpu.VMEM)
    smem = pl.BlockSpec(memory_space=pltpu.SMEM)
    dma = pltpu.SemaphoreType.DMA
    low_rows = pltpu.VMEM((seq, width), BF16)
    wide_rows = pltpu.VMEM((seq, width), F32)
    return pl.pallas_call(
        functools.partial(layer_kernel, dp_count),
        out_shape=[jax.ShapeDtypeStruct(s, d) for s, d in shapes],
        in_specs=[vmem] * 4 + [smem],
        out_specs=[vmem] * 4,
        scratch_shapes=[
            pltpu.VMEM((3, 4, width, 768), BF16), low_rows, low_rows, pltpu.VMEM((8, 16, width), BF16),
            pltpu.VMEM((16, width), F32), pltpu.VMEM((4, seq, 768), BF16), pltpu.VMEM((4, seq, 256), BF16),
            pltpu.VMEM((4, seq, 768), BF16), pltpu.VMEM((4, seq, 768), BF16), low_rows, wide_rows,
            pltpu.VMEM((seq, 128), F32), wide_rows, pltpu.VMEM((4, seq, 128), F32), pltpu.VMEM((16, width), F32),
            wide_rows, wide_rows, low_rows, pltpu.VMEM((2, width, seq), BF16), pltpu.VMEM((seq, 768), BF16),
            pltpu.VMEM((seq, 256), BF16), pltpu.VMEM((seq, 640), BF16),
            pltpu.VMEM((3, 2, width, 768), BF16), pltpu.VMEM((3, 2, 4, 96, width), BF16),
            pltpu.VMEM((3, 4, 96, width), BF16), pltpu.VMEM((3, 3, 96, width), BF16),
            pltpu.VMEM((4, 16, width), F32), pltpu.VMEM((6, 16, width), F32),
            dma((3, 31)), dma((3, 32)), dma((4, 4)), dma((4, 4)), dma((4,)), dma((4,)), dma((8,)), dma((8,)),
            dma((3, 2)), dma((3, 2)), dma((3, 8)), dma((3, 8)), dma((3, 4)), dma((3, 4)), dma((3, 3)), dma((3, 3)),
            dma((6,)), dma((6,)),
        ],
        compiler_params=pltpu.CompilerParams(
            vmem_limit_bytes=VMEM_LIMIT, collective_id=0, has_side_effects=True
        ),
        name="layer",
    )(tokens, grad_out, own, small, length)


def gather_groups(shard, dp_count, axis):
    stride = dp_count // 8
    if stride == 1:
        return shard
    groups = [[g * stride + i for i in range(stride)] for g in range(8)]
    return lax.all_gather(shard, "dp", axis=axis, tiled=True, axis_index_groups=groups)


def scatter_groups(shard, small, dp_count):
    stride = dp_count // 8
    if stride == 1:
        return shard, small
    groups = [[g * stride + i for i in range(stride)] for g in range(8)]
    shard = lax.psum_scatter(shard, "dp", scatter_dimension=1, tiled=True, axis_index_groups=groups)
    return shard, lax.psum(small, "dp", axis_index_groups=groups)


def pack_small(vectors, bias, dp_count, width):
    group = lax.axis_index("dp") // (dp_count // 8)
    part = vectors.shape[1]
    rows = lax.dynamic_update_slice(jnp.zeros((8, width), BF16), vectors, (0, group * part))
    units = lax.dynamic_update_slice(jnp.zeros((4 * width,), BF16), bias, (group * (4 * part),))
    qb = rows[0].reshape(4, 192)
    vb = rows[1].reshape(4, 192)
    none = jnp.zeros((4, 128), BF16)
    packed = jnp.concatenate([qb[:, :128], none, vb[:, :128], qb[:, 128:], none, vb[:, 128:], none], axis=1)
    return jnp.concatenate([rows, units.reshape(4, width), packed], axis=0)


def pack_attention(q, k, v, o):
    return jnp.concatenate(
        [q[:, :128], k[:, :128], v[:, :128], q[:, 128:], k[:, 128:], o[:, 128:], v[:, 128:], o[:, :128]], axis=1
    )


def shards(tokens, lengths, grad_out, qkv_weight, out_weight, up_weight, down_weight, vectors, hidden_bias):
    dp_count = lax.axis_size("dp")
    dp_rank = lax.axis_index("dp")
    tensor_rank = lax.axis_index("tensor")
    width = tokens.shape[2]
    part = width // dp_count

    own = jnp.stack([
        pack_attention(qkv_weight[0], qkv_weight[1], qkv_weight[2], out_weight.T), up_weight, down_weight.T
    ])
    own = gather_groups(own, dp_count, 1)
    small = pack_small(gather_groups(vectors, dp_count, 1), gather_groups(hidden_bias, dp_count, 0), dp_count, width)
    length = lax.dynamic_slice_in_dim(lengths, tensor_rank, 1).reshape(1, 1)
    output, gtok, g, gsm = layer_call(dp_count, tokens, grad_out, own, small, length)
    grad_tokens = gtok.astype(F32)
    g, gsm = scatter_groups(g, gsm, dp_count)
    a = g[0]
    gq = jnp.concatenate([a[:, 0:128], a[:, 384:448]], axis=1)
    gk = jnp.concatenate([a[:, 128:256], a[:, 448:512]], axis=1)
    gv = jnp.concatenate([a[:, 256:384], a[:, 576:640]], axis=1)
    gout = jnp.concatenate([a[:, 640:768], a[:, 512:576]], axis=1).T
    packed = gsm[12:16]
    row_q = jnp.concatenate([packed[:, 0:128], packed[:, 384:448]], axis=1).reshape(1, width)
    row_v = jnp.concatenate([packed[:, 256:384], packed[:, 576:640]], axis=1).reshape(1, width)
    rows = jnp.concatenate([row_q, row_v, gsm[2:8]], axis=0)
    grad_vectors = lax.dynamic_slice_in_dim(rows, dp_rank * part, part, 1)
    units = gsm[8:12].reshape(-1)
    grad_bias = lax.dynamic_slice_in_dim(units, dp_rank * (part * 4), part * 4)
    return output, grad_tokens, jnp.stack([gq, gk, gv]), gout, g[1], g[2].T, grad_vectors, grad_bias


def solution(mesh):
    in_specs = (
        P("dp", "tensor", None), P("dp"), P("dp", "tensor", None), P(None, "dp", "tensor"), P("tensor", "dp"),
        P("dp", "tensor"), P("tensor", "dp"), P(None, "dp"), P("dp"),
    )
    out_specs = (
        P("dp", "tensor", None), P("dp", "tensor", None), P(None, "dp", "tensor"), P("tensor", "dp"),
        P("dp", "tensor"), P("tensor", "dp"), P(None, "dp"), P("dp"),
    )
    return jax.shard_map(shards, mesh=mesh, in_specs=in_specs, out_specs=out_specs, check_vma=False)
```

```python
import functools

import jax
import jax.numpy as jnp
import numpy as np
from jax import lax
from jax.experimental import pallas as pl
from jax.experimental.pallas import tpu as pltpu
from jax.sharding import PartitionSpec as P

HD = 64
EPS = 1e-12
NEG = -1e30
F32 = jnp.float32
BF16 = jnp.bfloat16
VMEM_LIMIT = 67043328
ROWS = 128


def dot(left, right):
    return lax.dot_general(left, right, (((1,), (0,)), ((), ())), preferred_element_type=F32)


def dot_nt(left, right):
    return lax.dot_general(left, right, (((1,), (1,)), ((), ())), preferred_element_type=F32)


def lane_masks(scale):
    lane = lax.broadcasted_iota(jnp.int32, (1, 128), 1)
    low = jnp.where(lane < HD, F32(scale), F32(0)).astype(BF16)
    high = jnp.where(lane < HD, F32(0), F32(scale)).astype(BF16)
    return low, high


def is_low(shape):
    return lax.broadcasted_iota(jnp.int32, shape, 1) < HD


def put_row(ref, row, span, value):
    old = ref[8:16, span]
    here = lax.broadcasted_iota(jnp.int32, old.shape, 0) == row
    ref[8:16, span] = jnp.where(here, value, old)


class Place:
    def __init__(self, dp_count):
        self.stride = dp_count // 8
        dp_rank = lax.axis_index("dp")
        tensor_rank = lax.axis_index("tensor")
        group = dp_rank // self.stride
        self.rest = dp_rank % self.stride
        self.z, self.x = group // 2, group % 2
        self.y, self.c = tensor_rank // 2, tensor_rank % 2

    def device(self, z, x, y, c):
        return ((z * 2 + x) * self.stride + self.rest, y * 2 + c)

    def shifted(self, j, second, first, swapped):
        across_x = swapped * second + (1 - swapped) * first
        across_y = swapped * first + (1 - swapped) * second
        return (self.z + j) % 4, (self.x + across_x) % 2, (self.y + across_y) % 2

    def first(self, swapped):
        return self.device(*self.shifted(0, 0, 1, swapped), self.c)

    def second(self, swapped):
        return self.device(*self.shifted(0, 1, 0, swapped), self.c)

    def partner(self):
        return self.device(self.z, self.x, self.y, 1 - self.c)

    def along(self, j):
        return self.device((self.z + j) % 4, self.x, self.y, self.c)

    def in_tensor(self, r):
        return self.device(self.z, self.x, (self.y + r // 2) % 2, (self.c + r % 2) % 2)

    def in_dp(self, j, i):
        return self.device((self.z + j) % 4, (self.x + i) % 2, self.y, self.c)


def remote(src, dst, send, recv, device):
    return pltpu.make_async_remote_copy(
        src_ref=src, dst_ref=dst, send_sem=send, recv_sem=recv, device_id=device,
        device_id_type=pl.DeviceIdType.MESH,
    )


def barrier(place):
    sem = pltpu.get_barrier_semaphore()
    peers = [place.in_dp(j, i) for j in range(4) for i in range(2) if j or i]
    peers += [place.in_tensor(r) for r in range(1, 4)]
    for peer in peers:
        pl.semaphore_signal(sem, inc=1, device_id=peer, device_id_type=pl.DeviceIdType.MESH)
    pl.semaphore_wait(sem, len(peers))


class Gather:
    def __init__(self, place, own, w, send, recv):
        self.place, self.own, self.w, self.send, self.recv = place, own, w, send, recv

    def piece(self, k, s, f, j):
        z, x, y = self.place.shifted(j, s, f, self.swapped(k))
        return self.w.at[k, y * 2 + self.place.c, pl.ds(pl.multiple_of((z * 2 + x) * 96, 96), 96), :]

    def swapped(self, k):
        return 1 if k == 1 else self.place.c

    def push(self, k, src, dst, send, recv, device):
        remote(src, dst, self.send.at[k, send], self.recv.at[k, recv], device).start()

    def forward(self, k, s, f, j, to):
        here = self.piece(k, s, f, j)
        src = self.own[k] if (s, f, j) == (0, 0, 0) else here
        if "f" in to:
            self.push(k, src, here, 3 + j, 4 + j, self.place.first(self.swapped(k)))
        if "s" in to:
            self.push(k, src, here, 7 + 4 * f + j, 8 + 4 * f + j, self.place.second(self.swapped(k)))
        if "p" in to:
            self.push(k, src, here, 15 + 8 * s + 4 * f + j, 16 + 8 * s + 4 * f + j, self.place.partner())

    def along(self, k, f=0):
        here = self.piece(k, 0, f, 0)
        for j in (1, 3, 2):
            self.push(k, here if f else self.own[k], here, 4 * f + j - 1, 4 * f + 4 - j, self.place.along(j))

    def start(self, k):
        self.forward(k, 0, 0, 0, "fsp")

    def wait(self, k, slot):
        here = self.own[k]
        remote(here, here, self.send.at[k, 0], self.recv.at[k, slot], self.place.partner()).wait_recv()

    def relay(self, k, s, f, order):
        for j in order:
            self.wait(k, 8 * s + 4 * f + j)
            if k == 2 and (s, f, j) == (0, 1, 0):
                self.along(k, 1)
            self.forward(k, s, f, j, "p" if s else "sp" if f or k == 2 else "fsp")

    def others(self, k):
        @pl.loop(16, 32)
        def _(slot):
            self.wait(k, slot)

    def finish(self):
        for k in range(3):
            here = self.own[k]

            @pl.loop(0, 31)
            def _(slot):
                remote(here, here, self.send.at[k, slot], self.recv.at[k, 1], self.place.partner()).wait_send()


class Scatter:
    def __init__(self, place, g, boxes, sends, recvs, out):
        self.place, self.g, self.boxes, self.sends, self.recvs, self.out = place, g, boxes, sends, recvs, out

    def box(self, stage, part, *index):
        return self.boxes[stage].at[(part[1], *index, slice(None), pl.ds(*part[2]))]

    def push(self, stage, part, f_from, s_from, j, index, sem, device):
        k, t, row = self.piece(part, s_from, f_from, j)
        src = self.g.at[k, t, pl.ds(row, 96), pl.ds(*part[2])]
        remote(
            src, self.box(stage, part, *index), self.sends[stage].at[part[0], sem],
            self.recvs[stage].at[part[0], sem], device,
        ).start()

    def piece(self, part, s, f, j):
        z, x, y = self.place.shifted(j, s, f, self.place.c)
        return part[1], y * 2 + self.place.c, pl.multiple_of((z * 2 + x) * 96, 96)

    def wait(self, stage, part, index, sem):
        here = self.box(stage, part, *index)
        remote(
            here, here, self.sends[stage].at[part[0], sem], self.recvs[stage].at[part[0], sem], self.place.partner()
        ).wait_recv()

    def chunk_copy(self, k, t, i):
        return remote(
            self.g.at[k, t], self.boxes[0].at[k, i], self.sends[0].at[k, i], self.recvs[0].at[k, i],
            self.place.partner(),
        )

    def to_partner(self, k, t, i):
        self.chunk_copy(k, t, i).start()

    def from_partner(self, k, i):
        self.chunk_copy(k, 0, i).wait_recv()

    def across(self, part, f):
        for j in (2, 1, 3, 0):
            self.push(1, part, f, 1, j, (f, j), 4 * f + j, self.place.second(self.place.c))

    def ready(self, parts, i):
        if i == 0:
            for part in parts:
                self.across(part, 1)

        @pl.when(self.place.c == i)
        def _():
            for part in parts:
                self.across(part, 0)

    def total(self, part, f, j, views, last=False):
        k, t, row = self.piece(part, 0, f, j)
        columns = pl.ds(*part[2])

        @pl.loop(0, 3)
        def _(r):
            lines = pl.ds(pl.multiple_of(row + r * 32, 32), 32)
            local = pl.ds(pl.multiple_of(r * 32, 32), 32)
            value = self.g[k, t, lines, columns].astype(F32)
            for stage, index in views:
                value += self.boxes[stage][(k, *index, local, columns)].astype(F32)
            if last:
                self.out[k, local, columns] = value
            else:
                self.g[k, t, lines, columns] = value.astype(BF16)

    def add(self, part, f, j, arrived, last=False):
        for stage, index, sem in arrived:
            self.wait(stage, part, index, sem)
        self.total(part, f, j, [(stage, index) for stage, index, _ in arrived], last)

    def add_far(self, part):
        for j in (2, 1, 3, 0):
            self.add(part, 1, j, [(1, (1, j), 4 + j)])
            self.push(2, part, 1, 0, j, (j,), j, self.place.first(self.place.c))

    def add_near(self, part):
        for j in (2, 1, 3):
            self.add(part, 0, j, [(1, (0, j), j), (2, (j,), j)])
            self.push(3, part, 0, 0, j, (3 - j,), 3 - j, self.place.along(j))

    def add_last(self, part):
        arrived = [(1, (0, 0), 0), (2, (0,), 0), (3, (0,), 0), (3, (1,), 1), (3, (2,), 2)]
        self.add(part, 0, 0, arrived, True)

    def line_far(self, part):
        for j in (2, 1, 3):
            self.add(part, 1, j, [(1, (1, j), 4 + j)])
            self.push(2, part, 1, 0, j, (3 - j,), 3 - j, self.place.along(j))

    def line_near(self, part):
        for j in (2, 1, 3):
            self.add(part, 0, j, [(1, (0, j), j)])
            self.push(3, part, 0, 0, j, (3 - j,), 3 - j, self.place.along(j))

    def line_turn(self, part):
        self.add(part, 1, 0, [(1, (1, 0), 4), (2, (0,), 0), (2, (1,), 1), (2, (2,), 2)])
        self.push(2, part, 1, 0, 0, (3,), 3, self.place.first(self.place.c))

    def line_last(self, part):
        arrived = [(1, (0, 0), 0), (3, (0,), 0), (3, (1,), 1), (3, (2,), 2), (2, (3,), 3)]
        self.add(part, 0, 0, arrived, True)

    def finish(self, parts):
        for k in range(3):
            for i in range(2):
                self.chunk_copy(k, 0, i).wait_send()
        for part in parts:
            for stage, count in ((1, 8), (2, 4), (3, 3)):
                here = self.box(2, part, 0)

                @pl.loop(0, count)
                def _(i):
                    remote(
                        here, here, self.sends[stage].at[part[0], i], self.recvs[stage].at[part[0], i],
                        self.place.partner(),
                    ).wait_send()


class SmallSum:
    def __init__(self, place, stages, inbox, send, recv):
        self.place, self.stages, self.inbox, self.send, self.recv = place, stages, inbox, send, recv
        self.sent = []

    def push(self, stage, slot, peer):
        copy = remote(self.stages.at[stage], self.inbox.at[slot], self.send.at[slot], self.recv.at[slot], peer)
        copy.start()
        self.sent.append(copy)

    def start(self, i):
        peers = (self.place.partner(), self.place.second(self.place.c), self.place.first(self.place.c))
        if i < 3:
            self.push(i, i, peers[i])
        else:
            for j in range(1, 4):
                self.push(3, 6 - j, self.place.along(j))

    def step(self, i):
        self.sent[i].wait_recv()
        self.stages[i + 1] = self.stages[i] + self.inbox[i]
        self.start(i + 1)

    def finish(self, out):
        for copy in self.sent[3:]:
            copy.wait_recv()
        out[...] = (self.stages[3] + self.inbox[3]) + (self.inbox[4] + self.inbox[5])
        for copy in self.sent:
            copy.wait_send()


class Tokens:
    def __init__(self, place, send, recv, local):
        self.place, self.send, self.recv, self.local = place, send, recv, local
        self.rank = place.y * 2 + place.c

    def other(self, r):
        return ((self.place.y + r // 2) % 2) * 2 + (self.place.c + r % 2) % 2

    def rows(self, rank):
        return pl.ds(pl.multiple_of(rank * 128, 128), 128)

    def gather(self, i, src, dst):
        here = dst.at[self.rows(self.rank), :]
        pltpu.make_async_copy(src.at[self.rank], here, self.local.at[i]).start()
        for r in (2, 3, 1):
            remote(
                src.at[self.other(r)], here, self.send.at[i, r], self.recv.at[i, r], self.place.in_tensor(r)
            ).start()

    def spread(self, i, src, dst):
        here = dst.at[self.rank]
        pltpu.make_async_copy(src.at[self.rows(self.rank), :], here, self.local.at[i]).start()
        for r in (2, 3, 1):
            remote(
                src.at[self.rows(self.other(r)), :], here, self.send.at[i, r], self.recv.at[i, r],
                self.place.in_tensor(r),
            ).start()

    def wait(self, i, block, arrive=True, leave=True):
        for r in (1, 2, 3):
            copy = remote(block, block, self.send.at[i, r], self.recv.at[i, r], self.place.in_tensor(r))
            if arrive:
                copy.wait_recv()
            if leave:
                copy.wait_send()
        if arrive:
            pltpu.make_async_copy(block, block, self.local.at[i]).wait()


def steps(k, s, f, *order):
    return k, s, f, order


EARLY = (
    steps(0, 0, 1, 0), steps(0, 0, 0, 1, 3), steps(1, 0, 1, 0), steps(2, 0, 1, 0), steps(0, 0, 0, 2),
    steps(0, 0, 1, 1, 3), steps(0, 1, 0, 0), steps(0, 1, 1, 0), steps(0, 0, 1, 2), steps(1, 0, 0, 1),
    steps(0, 1, 0, 1, 3), steps(0, 1, 1, 1, 3), steps(1, 0, 0, 3), steps(0, 1, 0, 2), steps(0, 1, 1, 2),
)
X_AFTER = 6
IN_ATTENTION = (
    (steps(1, 0, 0, 2),), (steps(1, 0, 1, 1, 3),), (steps(1, 1, 0, 0),), (steps(1, 1, 1, 0), steps(2, 1, 0, 0)),
    (steps(2, 0, 0, 1),), (steps(1, 0, 1, 2),), (steps(1, 1, 0, 1, 3), steps(2, 1, 1, 0)), (steps(1, 1, 1, 1),),
    (steps(1, 1, 1, 3), steps(2, 0, 0, 3)), (steps(1, 1, 0, 2),), (steps(2, 0, 0, 2),), (steps(1, 1, 1, 2),),
)
IN_UP = (
    (steps(2, 0, 1, 1),), (steps(2, 1, 0, 1),), (steps(2, 1, 0, 3),), (steps(2, 0, 1, 3),), (steps(2, 1, 0, 2),),
    (steps(2, 1, 1, 1),), (steps(2, 0, 1, 2),), (steps(2, 1, 1, 3),),
)
LATE = (steps(2, 1, 1, 2),)
DOWN, UP, FRONT, BACK = (2, 2, (0, 768)), (1, 1, (0, 768)), (0, 0, (0, 512)), (3, 0, (512, 256))


def spots(rows, offset, gap=0):
    source = lax.broadcasted_iota(jnp.int32, (96, 768), 0) + rows
    target = lax.broadcasted_iota(jnp.int32, (96, 768), 1)
    moved = source + offset + jnp.where(source < 128, 0, gap)
    return jnp.where(target == moved, F32(1), F32(0)).astype(BF16)


def pack_small(place, vec_in, bias_in):
    group = place.z * 2 + place.x
    rows = vec_in[...]
    top = dot(rows, spots(96 * group, 0, 0))
    start = 96 * (group % 2)
    queries = dot(rows, spots(start, 0, 256))[0:1]
    values = dot(rows, spots(start, 256, 192))[1:2]
    units = bias_in[...].astype(F32)
    lane = lax.broadcasted_iota(jnp.int32, (1, 768), 1)
    units = jnp.where(lane // 384 == group % 2, jnp.concatenate([units, units], axis=1), 0.0)
    line = lax.broadcasted_iota(jnp.int32, (8, 768), 0)
    low = jnp.where(line == group // 2, units, 0.0) + jnp.where(line == 4 + group // 2, queries + values, 0.0)
    return jnp.concatenate([top, low], axis=0).astype(BF16)


def pack_attention(qkv_in, out_in):
    q, k, v = (qkv_in[i].astype(F32) for i in range(3))
    o = jnp.transpose(out_in[...].astype(F32))
    return jnp.concatenate([
        q[:, :128], k[:, :128], v[:, :128], jnp.concatenate([q[:, 128:], k[:, 128:]], axis=1),
        jnp.concatenate([o[:, 128:], v[:, 128:]], axis=1), o[:, :128],
    ], axis=1).astype(BF16)


def finish_kernel(
    dp_count, out_in, gtok_in, shard, small,
    output, gtok, qkv, out, up, down, vec, units,
):
    stride = dp_count // 8
    rank = lax.axis_index("dp")
    group, part = rank // stride, vec.shape[1]
    output[...] = out_in[...]
    gtok[...] = gtok_in[...].astype(F32)
    a = shard[0]
    qkv[0, :, 0:128] = a[:, 0:128]
    qkv[1, :, 0:128] = a[:, 128:256]
    qkv[2, :, 0:128] = a[:, 256:384]
    qkv[0, :, 128:192] = a[:, 384:448]
    qkv[1, :, 128:192] = pltpu.roll(a[:, 384:512], 64, 1)[:, 0:64]
    qkv[2, :, 128:192] = pltpu.roll(a[:, 512:640], 64, 1)[:, 0:64]
    out[0:128, :] = jnp.transpose(a[:, 640:768])
    out[128:192, :] = jnp.transpose(a[:, 512:640])[0:64]
    up[...] = shard[1]
    down[...] = shard[2]

    rest = rank % stride
    even = group % 2 == 0
    lane = lax.broadcasted_iota(jnp.int32, (1, 768), 1)

    def own_lines(row, first, second):
        near = pltpu.roll(row, jnp.where(even, (768 - first) % 768, 768 - first - 96), 1)
        far = pltpu.roll(row, 768 - second + 32, 1)
        return jnp.where(even | (lane < 32), near, far)

    line = lax.broadcasted_iota(jnp.int32, (8, 768), 0)
    packed = small[8:16, :]
    row = jnp.sum(jnp.where(line == 4 + group // 2, packed, 0.0), axis=0, keepdims=True)
    queries = own_lines(row, 0, 384)
    values = own_lines(row, 256, 576)
    lines = pltpu.roll(small[0:8, :], (768 - 96 * group) % 768, 1)
    lines = jnp.where(line == 0, queries, jnp.where(line == 1, values, lines))
    lines = pltpu.roll(lines, (768 - rest * part) % 768, 1)
    vec[...] = lines[:, 0:part]
    row = jnp.sum(jnp.where(line == group // 2, packed, 0.0), axis=0, keepdims=True)
    shift = 384 * (group % 2) + rest * 4 * part
    units[...] = pltpu.roll(row, (768 - shift) % 768, 1)[:, 0 : 4 * part]


def finish_call(dp_count, out, gtok, shard, small):
    rows, width = shard.shape[1], shard.shape[2]
    shapes = (
        (out.shape, BF16), (gtok.shape, F32), ((3, rows, width // 4), F32), ((width // 4, rows), F32),
        ((rows, width), F32), ((rows, width), F32), ((8, rows), F32), ((1, 4 * rows), F32),
    )
    vmem = pl.BlockSpec(memory_space=pltpu.VMEM)
    return pl.pallas_call(
        functools.partial(finish_kernel, dp_count),
        out_shape=[jax.ShapeDtypeStruct(s, d) for s, d in shapes],
        in_specs=[vmem] * 4,
        out_specs=[vmem] * 8,
        compiler_params=pltpu.CompilerParams(vmem_limit_bytes=32 * 1024 * 1024),
        name="finish",
    )(out, gtok, shard, small)


def layer_kernel(
    dp_count, x_in, go_in, qkv_in, out_in, up_in, down_in, vec_in, bias_in, len_ref,
    output, gtok, shard, small,
    own_first, small_in, w, x, go, smalls, sm, qkv, ctx, act, gp, hb, n1, s1, stat, gsm,
    acc, pre, low_grad, tall, gctx, gpacked,
    box_p, box_s, box_f, box_z, stages, small_box,
    send, recv, tok_send, tok_recv, tok_local, own_local, bias_send, bias_recv,
    send_p, recv_p, send_s, recv_s, send_f, recv_f, send_z, recv_z, small_send, small_recv,
):
    seq, width = x.shape
    blocks = seq // ROWS
    place = Place(dp_count)
    own = (own_first, up_in, down_in)
    gather = Gather(place, own, w, send, recv)
    own_first[...] = pack_attention(qkv_in, out_in)
    small_in[...] = pack_small(place, vec_in, bias_in)
    tokens = Tokens(place, tok_send, tok_recv, tok_local)

    barrier(place)
    gather.along(0)
    gather.start(0)
    for k in range(3):
        pltpu.make_async_copy(own[k], gather.piece(k, 0, 0, 0), own_local.at[k]).start()
    pltpu.make_async_copy(small_in, smalls.at[0], own_local.at[3]).start()
    for j in range(4):
        for i in range(2):
            if j or i:
                slot = ((4 - j) % 4) * 2 + i
                remote(
                    small_in, smalls.at[slot], bias_send.at[slot], bias_recv.at[slot], place.in_dp(j, i)
                ).start()
    for k in (1, 2):
        gather.along(k)
        gather.start(k)
    for event in EARLY[:X_AFTER]:
        gather.relay(*event)
    tokens.gather(0, x_in, x)
    for event in EARLY[X_AFTER:]:
        gather.relay(*event)
    for k in range(3):
        pltpu.make_async_copy(own[k], own[k], own_local.at[k]).wait()
    pltpu.make_async_copy(small_in, small_in, own_local.at[3]).wait()

    @pl.loop(1, 8)
    def _(slot):
        remote(small_in, small_in, bias_send.at[slot], bias_recv.at[slot], place.partner()).wait()

    total = smalls[0].astype(F32)
    for i in range(1, 8):
        total += smalls[i].astype(F32)
    sm[...] = total
    tokens.wait(0, x_in.at[0])
    gather.others(0)

    low, high = lane_masks(0.125)
    length = len_ref[place.y * 2 + place.c]
    key_bias = jnp.where(lax.broadcasted_iota(jnp.int32, (1, seq), 1) < length, F32(0), F32(NEG))
    acc[...] = jnp.zeros_like(acc)

    def relays(step, table):
        for n, events in enumerate(table):
            if events:
                @pl.when(step == n)
                def _():
                    for event in events:
                        gather.relay(*event)

    @pl.loop(0, 4)
    def _(t):
        relays(3 * t, IN_ATTENTION)
        proj = dot(x[...], w[0, t, :, 0:640]) + sm[pl.ds(12 + t, 1), 0:640]
        qkv[t, :, 0:640] = proj.astype(BF16)
        q_two = pltpu.roll(jnp.where(is_low((seq, 128)), proj[:, 384:512] * 0.125, 0.0), 64, 1)
        qkv[t, :, 640:768] = q_two.astype(BF16)

        @pl.loop(0, seq // 256)
        def _(r):
            relays(3 * t + r + 1, IN_ATTENTION)
            rows = pl.ds(pl.multiple_of(r * 256, 256), 256)
            q_pair = qkv[t, rows, 0:128]
            outs = []
            stats = []
            for h in range(3):
                if h < 2:
                    queries = q_pair * (low, high)[h]
                    keys = qkv[t, :, 128:256]
                    values = qkv[t, :, 256:384]
                else:
                    queries = qkv[t, rows, 640:768]
                    keys = qkv[t, :, 384:512]
                    values = qkv[t, :, 512:640]
                scores = dot_nt(queries, keys) + key_bias
                highest = jnp.max(scores, axis=1, keepdims=True)
                grown = jnp.exp(scores - highest)
                total = jnp.sum(grown, axis=1, keepdims=True)
                probs = (grown * (1.0 / total)).astype(BF16)
                outs.append(dot(probs, values))
                stats.append(highest + jnp.log(total))
            lowest = is_low((256, 128))
            ctx[t, rows, 0:128] = jnp.where(lowest, pltpu.roll(outs[2], 64, 1), 0.0).astype(BF16)
            ctx[t, rows, 128:256] = jnp.where(lowest, outs[0], outs[1]).astype(BF16)
            lane = lax.broadcasted_iota(jnp.int32, (256, 128), 1)
            stat[t, rows, :] = jnp.where(lane == 0, stats[0], jnp.where(lane == 1, stats[1], stats[2]))

        acc[...] += dot_nt(ctx[t], w[0, t, :, 512:768])

    @pl.loop(0, blocks)
    def _(r):
        rows = pl.ds(pl.multiple_of(r * ROWS, ROWS), ROWS)
        resid = x[rows, :].astype(F32) + acc[rows, :] + sm[2:3, :]
        centred = resid - jnp.mean(resid, axis=1, keepdims=True)
        scale = lax.rsqrt(jnp.mean(centred * centred, axis=1, keepdims=True) + EPS)
        normed = centred * scale
        hidden = normed * sm[3:4, :] + sm[4:5, :]
        n1[rows, :] = normed
        s1[rows, :] = jnp.broadcast_to(scale, (ROWS, 128))
        hb[rows, :] = hidden.astype(BF16)
        acc[rows, :] = hidden + sm[5:6, :]

    gather.others(1)

    @pl.loop(0, 4)
    def _(t):
        relays(2 * t, IN_UP)
        pre[...] = dot(hb[...], w[1, t])

        relays(2 * t + 1, IN_UP)

        @pl.loop(0, blocks)
        def _(r):
            rows = pl.ds(pl.multiple_of(r * ROWS, ROWS), ROWS)
            u = pre[rows, :] + sm[pl.ds(8 + t, 1), :]
            cdf = 0.5 + 0.5 * lax.erf(u * F32(np.sqrt(0.5)))
            density = jnp.exp(u * u * -0.5) * F32(1.0 / np.sqrt(2.0 * np.pi))
            act[t, rows, :] = (u * cdf).astype(BF16)
            gp[t, rows, :] = (cdf + u * density).astype(BF16)

    for event in LATE:
        gather.relay(*event)
    tokens.gather(1, go_in, go)
    gather.others(2)

    @pl.loop(0, 4)
    def _(t):
        acc[...] += dot_nt(act[t], w[2, t])

    gsm[...] = jnp.zeros_like(gsm)

    @pl.loop(0, blocks)
    def _(r):
        rows = pl.ds(pl.multiple_of(r * ROWS, ROWS), ROWS)
        resid = acc[rows, :]
        centred = resid - jnp.mean(resid, axis=1, keepdims=True)
        scale = lax.rsqrt(jnp.mean(centred * centred, axis=1, keepdims=True) + EPS)
        acc[rows, :] = centred * scale
        pre[rows, 0:128] = jnp.broadcast_to(scale, (ROWS, 128))

    tall[1] = jnp.transpose(hb[...].astype(F32)).astype(BF16)
    tokens.wait(1, x_in.at[0])

    @pl.loop(0, blocks)
    def _(r):
        rows = pl.ds(pl.multiple_of(r * ROWS, ROWS), ROWS)
        normed = acc[rows, :]
        gain = sm[6:7, :]
        cot = go[rows, :].astype(F32)
        go[rows, :] = (normed * gain + sm[7:8, :]).astype(BF16)
        e = cot * gain
        en = jnp.mean(e * normed, axis=1, keepdims=True)
        grad = pre[rows, 0:1] * (e - jnp.mean(e, axis=1, keepdims=True) - normed * en)
        acc[rows, :] = grad
        low_grad[rows, :] = grad.astype(BF16)
        gsm[5:6, :] += jnp.sum(grad, axis=0, keepdims=True)
        gsm[6:7, :] += jnp.sum(cot * normed, axis=0, keepdims=True)
        gsm[7:8, :] += jnp.sum(cot, axis=0, keepdims=True)

    tokens.spread(2, go, output)
    gather.finish()
    scatter = Scatter(
        place, w, (box_p, box_s, box_f, box_z), (send_p, send_s, send_f, send_z), (recv_p, recv_s, recv_f, recv_z),
        shard,
    )
    tall[0] = jnp.transpose(acc[...]).astype(BF16)

    def chunk(i, core):
        return ((place.y + 1 - i) % 2) * 2 + core

    def own_chunk(k, i, t, value):
        scatter.from_partner(k, i)
        w[k, t] = (value + box_p[k, i].astype(F32)).astype(BF16)
        parts = (DOWN,) if k == 2 else (UP,)
        pl.when(i == 0)(lambda: scatter.ready(parts, 0))
        pl.when(i == 1)(lambda: scatter.ready(parts, 1))

    def down_back(t):
        grad_pre = dot(low_grad[...], w[2, t]) * gp[t].astype(F32)
        put_row(gsm, t, slice(0, 768), jnp.sum(grad_pre, axis=0, keepdims=True))
        gp[t] = grad_pre.astype(BF16)
        return dot(tall[0], act[t])

    def up_back(t):
        acc[...] += dot_nt(gp[t], w[1, t])
        return dot(tall[1], gp[t])

    for k, back in ((2, down_back), (1, up_back)):
        @pl.loop(0, 2)
        def _(i):
            t = chunk(i, 1 - place.c)
            w[k, t] = back(t).astype(BF16)
            scatter.to_partner(k, t, i)

        @pl.loop(0, 2)
        def _(i):
            t = chunk(i, place.c)
            own_chunk(k, i, t, back(t))

    @pl.loop(0, blocks)
    def _(r):
        rows = pl.ds(pl.multiple_of(r * ROWS, ROWS), ROWS)
        cot = acc[rows, :]
        normed = n1[rows, :]
        e = cot * sm[3:4, :]
        en = jnp.mean(e * normed, axis=1, keepdims=True)
        grad = s1[rows, 0:1] * (e - jnp.mean(e, axis=1, keepdims=True) - normed * en)
        acc[rows, :] = grad
        low_grad[rows, :] = grad.astype(BF16)
        gsm[2:3, :] += jnp.sum(grad, axis=0, keepdims=True)
        gsm[3:4, :] += jnp.sum(cot * normed, axis=0, keepdims=True)
        gsm[4:5, :] += jnp.sum(cot, axis=0, keepdims=True)

    tall[0] = jnp.transpose(acc[...]).astype(BF16)
    tall[1] = jnp.transpose(x[...].astype(F32)).astype(BF16)

    one_low, one_high = lane_masks(1.0)
    tall_bias = jnp.where(lax.broadcasted_iota(jnp.int32, (seq, 1), 0) < length, F32(0), F32(NEG))

    def attention_back(t, event, store):
        back = dot(low_grad[...], w[0, t, :, 512:768])
        gctx[:, 0:128] = pltpu.roll(jnp.where(is_low((seq, 128)), back[:, 0:128], 0.0), 64, 1).astype(BF16)
        gctx[:, 128:256] = back[:, 128:256].astype(BF16)
        log_rows = jnp.transpose(stat[t])
        grads_q = []
        grads_k = []
        grads_v = []
        for h in range(3):
            if h < 2:
                queries = qkv[t, :, 0:128] * (low, high)[h]
                keys = qkv[t, :, 128:256]
                values = qkv[t, :, 256:384]
                cots = gctx[:, 128:256] * (one_low, one_high)[h]
            else:
                queries = qkv[t, :, 640:768]
                keys = qkv[t, :, 384:512]
                values = qkv[t, :, 512:640]
                cots = gctx[:, 0:128]
            scores = dot_nt(keys, queries) + tall_bias
            probs = jnp.exp(scores - log_rows[h : h + 1, :])
            grad_probs = dot_nt(values, cots)
            row_dots = jnp.sum(grad_probs * probs, axis=0, keepdims=True)
            grad_scores = (probs * (grad_probs - row_dots)).astype(BF16)
            grads_v.append(dot(probs.astype(BF16), cots))
            grads_k.append(dot(grad_scores, queries))
            part = (0, HD, HD)[h]
            keys_tall = jnp.transpose(keys.astype(F32))[part : part + HD, :].astype(BF16)
            grads_q.append(dot(keys_tall, grad_scores) * 0.125)
        pair = jnp.transpose(jnp.concatenate([grads_q[0], grads_q[1]], axis=0))
        single = jnp.transpose(jnp.concatenate([grads_q[2], jnp.zeros_like(grads_q[2])], axis=0))
        tiles = [pair, grads_k[0] + grads_k[1], grads_v[0] + grads_v[1], single + grads_k[2], grads_v[2]]
        for i, tile in enumerate(tiles):
            span = slice(128 * i, 128 * i + 128)
            put_row(gsm, 4 + t, span, jnp.sum(tile, axis=0, keepdims=True))
            gpacked[:, span] = tile.astype(BF16)
        event()
        acc[...] += dot_nt(gpacked[...], w[0, t, :, 0:640])
        store(slice(0, 512), dot(tall[1], gpacked[:, 0:512]))
        store(slice(512, 640), dot(tall[1], gpacked[:, 512:640]) + dot(tall[0], ctx[t, :, 0:128]))
        store(slice(640, 768), dot(tall[0], ctx[t, :, 128:256]))

    @pl.loop(0, 2)
    def _(i):
        t = chunk(i, 1 - place.c)

        def store(span, value):
            w[0, t, :, span] = value.astype(BF16)

        def event():
            pl.when(i == 0)(lambda: scatter.line_far(DOWN))
            pl.when(i == 1)(lambda: scatter.line_near(DOWN))

        attention_back(t, event, store)
        scatter.to_partner(0, t, i)

    @pl.loop(0, 2)
    def _(i):
        t = chunk(i, place.c)

        def store(span, value):
            w[0, t, :, span] = (value + box_p[0, i, :, span].astype(F32)).astype(BF16)

        def event():
            pl.when(i == 0)(lambda: scatter.add_far(UP))
            pl.when(i == 1)(lambda: scatter.line_turn(DOWN))
            scatter.from_partner(0, i)

        attention_back(t, event, store)
        pl.when(i == 0)(lambda: scatter.ready((FRONT, BACK), 0))
        pl.when(i == 1)(lambda: scatter.ready((FRONT, BACK), 1))

    x[...] = acc[...].astype(BF16)
    stages[0] = gsm[...]
    sums = SmallSum(place, stages, small_box, small_send, small_recv)
    sums.start(0)
    scatter.add_near(UP)
    scatter.add_far(FRONT)
    scatter.add_far(BACK)
    tokens.spread(3, x, gtok)
    sums.step(0)
    scatter.line_last(DOWN)
    sums.step(1)
    scatter.add_near(FRONT)
    sums.step(2)
    scatter.add_near(BACK)
    scatter.add_last(UP)
    sums.finish(small)
    scatter.add_last(FRONT)
    scatter.add_last(BACK)
    for i in (2, 3):
        tokens.wait(i, x_in.at[0])
    scatter.finish((DOWN, UP, FRONT, BACK))


def layer_call(dp_count, tokens, grad_out, weights, vectors, bias, lengths):
    part, width = tokens.shape[1], tokens.shape[2]
    seq = tokens.shape[0] * part
    shapes = (((4, part, width), BF16), ((4, part, width), BF16), ((3, 96, width), F32), ((16, width), F32))
    vmem = pl.BlockSpec(memory_space=pltpu.VMEM)
    smem = pl.BlockSpec(memory_space=pltpu.SMEM)
    dma = pltpu.SemaphoreType.DMA
    low_rows = pltpu.VMEM((seq, width), BF16)
    wide_rows = pltpu.VMEM((seq, width), F32)
    return pl.pallas_call(
        functools.partial(layer_kernel, dp_count),
        out_shape=[jax.ShapeDtypeStruct(s, d) for s, d in shapes],
        in_specs=[vmem] * 8 + [smem],
        out_specs=[vmem] * 4,
        scratch_shapes=[
            pltpu.VMEM((96, width), BF16), pltpu.VMEM((16, width), BF16),
            pltpu.VMEM((3, 4, width, 768), BF16), low_rows, low_rows, pltpu.VMEM((8, 16, width), BF16),
            pltpu.VMEM((16, width), F32), pltpu.VMEM((4, seq, 768), BF16), pltpu.VMEM((4, seq, 256), BF16),
            pltpu.VMEM((4, seq, 768), BF16), pltpu.VMEM((4, seq, 768), BF16), low_rows, wide_rows,
            pltpu.VMEM((seq, 128), F32), pltpu.VMEM((4, seq, 128), F32), pltpu.VMEM((16, width), F32),
            wide_rows, wide_rows, low_rows, pltpu.VMEM((2, width, seq), BF16),
            pltpu.VMEM((seq, 256), BF16), pltpu.VMEM((seq, 640), BF16),
            pltpu.VMEM((3, 2, width, 768), BF16), pltpu.VMEM((3, 2, 4, 96, width), BF16),
            pltpu.VMEM((3, 4, 96, width), BF16), pltpu.VMEM((3, 3, 96, width), BF16),
            pltpu.VMEM((4, 16, width), F32), pltpu.VMEM((6, 16, width), F32),
            dma((3, 31)), dma((3, 32)), dma((4, 4)), dma((4, 4)), dma((4,)), dma((4,)), dma((8,)), dma((8,)),
            dma((3, 2)), dma((3, 2)), dma((4, 8)), dma((4, 8)), dma((4, 4)), dma((4, 4)), dma((4, 3)), dma((4, 3)),
            dma((6,)), dma((6,)),
        ],
        compiler_params=pltpu.CompilerParams(
            vmem_limit_bytes=VMEM_LIMIT, collective_id=0, has_side_effects=True
        ),
        name="layer",
    )(tokens, grad_out, *weights, vectors, bias, lengths)


def gather_groups(shard, dp_count, axis):
    stride = dp_count // 8
    if stride == 1:
        return shard
    groups = [[g * stride + i for i in range(stride)] for g in range(8)]
    return lax.all_gather(shard, "dp", axis=axis, tiled=True, axis_index_groups=groups)


def scatter_groups(shard, small, dp_count):
    stride = dp_count // 8
    if stride == 1:
        return shard, small
    groups = [[g * stride + i for i in range(stride)] for g in range(8)]
    shard = lax.psum_scatter(shard, "dp", scatter_dimension=1, tiled=True, axis_index_groups=groups)
    return shard, lax.psum(small, "dp", axis_index_groups=groups)


def shards(tokens, lengths, grad_out, qkv_weight, out_weight, up_weight, down_weight, vectors, hidden_bias):
    dp_count = lax.axis_size("dp")
    weights = [
        gather_groups(weight, dp_count, axis)
        for weight, axis in ((qkv_weight, 1), (out_weight, 1), (up_weight, 0), (down_weight, 1))
    ]
    weights[3] = weights[3].T
    vectors = gather_groups(vectors, dp_count, 1)
    bias = gather_groups(hidden_bias, dp_count, 0).reshape(1, -1)
    output, gtok, g, gsm = layer_call(dp_count, tokens, grad_out, weights, vectors, bias, lengths)
    g, gsm = scatter_groups(g, gsm, dp_count)
    *results, down, vec, units = finish_call(dp_count, output, gtok, g, gsm)
    return *results, down.T, vec, units.reshape(-1)


def solution(mesh):
    in_specs = (
        P("dp", "tensor", None), P("dp"), P("dp", "tensor", None), P(None, "dp", "tensor"), P("tensor", "dp"),
        P("dp", "tensor"), P("tensor", "dp"), P(None, "dp"), P("dp"),
    )
    out_specs = (
        P("dp", "tensor", None), P("dp", "tensor", None), P(None, "dp", "tensor"), P("tensor", "dp"),
        P("dp", "tensor"), P("tensor", "dp"), P(None, "dp"), P("dp"),
    )
    return jax.shard_map(shards, mesh=mesh, in_specs=in_specs, out_specs=out_specs, check_vma=False)
```

```python
import functools

import jax
import jax.numpy as jnp
import numpy as np
from jax import lax
from jax.experimental import pallas as pl
from jax.experimental.pallas import tpu as pltpu
from jax.sharding import PartitionSpec as P

HD = 64
EPS = 1e-12
NEG = -1e30
F32 = jnp.float32
BF16 = jnp.bfloat16
VMEM_LIMIT = 67043328
ROWS = 128


def dot(left, right):
    return lax.dot_general(left, right, (((1,), (0,)), ((), ())), preferred_element_type=F32)


def dot_nt(left, right):
    return lax.dot_general(left, right, (((1,), (1,)), ((), ())), preferred_element_type=F32)


def lane_masks(scale):
    lane = lax.broadcasted_iota(jnp.int32, (1, 128), 1)
    low = jnp.where(lane < HD, F32(scale), F32(0)).astype(BF16)
    high = jnp.where(lane < HD, F32(0), F32(scale)).astype(BF16)
    return low, high


def is_low(shape):
    return lax.broadcasted_iota(jnp.int32, shape, 1) < HD


def put_row(ref, row, span, value):
    old = ref[8:16, span]
    here = lax.broadcasted_iota(jnp.int32, old.shape, 0) == row
    ref[8:16, span] = jnp.where(here, value, old)


class Place:
    def __init__(self, dp_count):
        self.stride = dp_count // 8
        dp_rank = lax.axis_index("dp")
        tensor_rank = lax.axis_index("tensor")
        group = dp_rank // self.stride
        self.rest = dp_rank % self.stride
        self.z, self.x = group // 2, group % 2
        self.y, self.c = tensor_rank // 2, tensor_rank % 2

    def device(self, z, x, y, c):
        return ((z * 2 + x) * self.stride + self.rest, y * 2 + c)

    def shifted(self, j, second, first, swapped):
        across_x = swapped * second + (1 - swapped) * first
        across_y = swapped * first + (1 - swapped) * second
        return (self.z + j) % 4, (self.x + across_x) % 2, (self.y + across_y) % 2

    def first(self, swapped):
        return self.device(*self.shifted(0, 0, 1, swapped), self.c)

    def second(self, swapped):
        return self.device(*self.shifted(0, 1, 0, swapped), self.c)

    def partner(self):
        return self.device(self.z, self.x, self.y, 1 - self.c)

    def along(self, j):
        return self.device((self.z + j) % 4, self.x, self.y, self.c)

    def in_tensor(self, r):
        return self.device(self.z, self.x, (self.y + r // 2) % 2, (self.c + r % 2) % 2)

    def in_dp(self, j, i):
        return self.device((self.z + j) % 4, (self.x + i) % 2, self.y, self.c)


def remote(src, dst, send, recv, device):
    return pltpu.make_async_remote_copy(
        src_ref=src, dst_ref=dst, send_sem=send, recv_sem=recv, device_id=device,
        device_id_type=pl.DeviceIdType.MESH,
    )


def barrier(place):
    sem = pltpu.get_barrier_semaphore()
    peers = [place.in_dp(j, i) for j in range(4) for i in range(2) if j or i]
    peers += [place.in_tensor(r) for r in range(1, 4)]
    for peer in peers:
        pl.semaphore_signal(sem, inc=1, device_id=peer, device_id_type=pl.DeviceIdType.MESH)
    pl.semaphore_wait(sem, len(peers))


class Gather:
    def __init__(self, place, own, w, send, recv):
        self.place, self.own, self.w, self.send, self.recv = place, own, w, send, recv

    def piece(self, k, s, f, j):
        z, x, y = self.place.shifted(j, s, f, self.swapped(k))
        return self.w.at[k, y * 2 + self.place.c, pl.ds(pl.multiple_of((z * 2 + x) * 96, 96), 96), :]

    def swapped(self, k):
        return 1 if k == 1 else self.place.c

    def push(self, k, src, dst, send, recv, device):
        remote(src, dst, self.send.at[k, send], self.recv.at[k, recv], device).start()

    def forward(self, k, s, f, j, to):
        here = self.piece(k, s, f, j)
        src = self.own[k] if (s, f, j) == (0, 0, 0) else here
        if "f" in to:
            self.push(k, src, here, 3 + j, 4 + j, self.place.first(self.swapped(k)))
        if "s" in to:
            self.push(k, src, here, 7 + 4 * f + j, 8 + 4 * f + j, self.place.second(self.swapped(k)))
        if "p" in to:
            self.push(k, src, here, 15 + 8 * s + 4 * f + j, 16 + 8 * s + 4 * f + j, self.place.partner())

    def along(self, k, f=0):
        here = self.piece(k, 0, f, 0)
        for j in (1, 3, 2):
            self.push(k, here if f else self.own[k], here, 4 * f + j - 1, 4 * f + 4 - j, self.place.along(j))

    def start(self, k):
        self.forward(k, 0, 0, 0, "fsp")

    def wait(self, k, slot):
        here = self.own[k]
        remote(here, here, self.send.at[k, 0], self.recv.at[k, slot], self.place.partner()).wait_recv()

    def relay(self, k, s, f, order):
        for j in order:
            self.wait(k, 8 * s + 4 * f + j)
            if k == 2 and (s, f, j) == (0, 1, 0):
                self.along(k, 1)
            self.forward(k, s, f, j, "p" if s else "sp" if f or k == 2 else "fsp")

    def others(self, k):
        @pl.loop(16, 32)
        def _(slot):
            self.wait(k, slot)

    def finish(self):
        for k in range(3):
            here = self.own[k]

            @pl.loop(0, 31)
            def _(slot):
                remote(here, here, self.send.at[k, slot], self.recv.at[k, 1], self.place.partner()).wait_send()


class Scatter:
    def __init__(self, place, g, boxes, sends, recvs, out):
        self.place, self.g, self.boxes, self.sends, self.recvs, self.out = place, g, boxes, sends, recvs, out

    def swapped(self, part):
        return self.place.c

    def box(self, stage, part, *index):
        return self.boxes[stage].at[(part[1], *index, slice(None), pl.ds(*part[2]))]

    def push(self, stage, part, f_from, s_from, j, index, sem, device):
        k, t, row = self.piece(part, s_from, f_from, j)
        src = self.g.at[k, t, pl.ds(row, 96), pl.ds(*part[2])]
        remote(
            src, self.box(stage, part, *index), self.sends[stage].at[part[0], sem],
            self.recvs[stage].at[part[0], sem], device,
        ).start()

    def piece(self, part, s, f, j):
        z, x, y = self.place.shifted(j, s, f, self.swapped(part))
        return part[1], y * 2 + self.place.c, pl.multiple_of((z * 2 + x) * 96, 96)

    def wait(self, stage, part, index, sem):
        here = self.box(stage, part, *index)
        remote(
            here, here, self.sends[stage].at[part[0], sem], self.recvs[stage].at[part[0], sem], self.place.partner()
        ).wait_recv()

    def chunk_copy(self, k, t, i):
        return remote(
            self.g.at[k, t], self.boxes[0].at[k, i], self.sends[0].at[k, i], self.recvs[0].at[k, i],
            self.place.partner(),
        )

    def to_partner(self, k, t, i):
        self.chunk_copy(k, t, i).start()

    def from_partner(self, k, i):
        self.chunk_copy(k, 0, i).wait_recv()

    def across(self, part, f):
        for j in (2, 1, 3, 0):
            self.push(1, part, f, 1, j, (f, j), 4 * f + j, self.place.second(self.swapped(part)))

    def ready(self, parts, i):
        if i == 0:
            for part in parts:
                self.across(part, 1)

        for part in parts:
            pl.when(self.swapped(part) == i)(lambda: self.across(part, 0))

    def total(self, part, f, j, views, last=False):
        k, t, row = self.piece(part, 0, f, j)
        columns = pl.ds(*part[2])

        @pl.loop(0, 3)
        def _(r):
            lines = pl.ds(pl.multiple_of(row + r * 32, 32), 32)
            local = pl.ds(pl.multiple_of(r * 32, 32), 32)
            value = self.g[k, t, lines, columns].astype(F32)
            for stage, index in views:
                value += self.boxes[stage][(k, *index, local, columns)].astype(F32)
            if last:
                self.out[k, local, columns] = value
            else:
                self.g[k, t, lines, columns] = value.astype(BF16)

    def add(self, part, f, j, arrived, last=False):
        for stage, index, sem in arrived:
            self.wait(stage, part, index, sem)
        self.total(part, f, j, [(stage, index) for stage, index, _ in arrived], last)

    def add_far(self, part, line=(2, 1, 3, 0)):
        for j in line:
            self.add(part, 1, j, [(1, (1, j), 4 + j)])
            self.push(2, part, 1, 0, j, (j,), j, self.place.first(self.swapped(part)))

    def add_near(self, part, line=(2, 1, 3)):
        for j in line:
            self.add(part, 0, j, [(1, (0, j), j), (2, (j,), j)])
            self.push(3, part, 0, 0, j, (3 - j,), 3 - j, self.place.along(j))

    def add_last(self, part):
        arrived = [(1, (0, 0), 0), (2, (0,), 0), (3, (0,), 0), (3, (1,), 1), (3, (2,), 2)]
        self.add(part, 0, 0, arrived, True)

    def line_far(self, part, line=(2, 1, 3)):
        for j in line:
            self.add(part, 1, j, [(1, (1, j), 4 + j)])
            self.push(2, part, 1, 0, j, (3 - j,), 3 - j, self.place.along(j))

    def line_near(self, part, line=(2, 1, 3)):
        for j in line:
            self.add(part, 0, j, [(1, (0, j), j)])
            self.push(3, part, 0, 0, j, (3 - j,), 3 - j, self.place.along(j))

    def line_turn(self, part):
        self.add(part, 1, 0, [(1, (1, 0), 4), (2, (0,), 0), (2, (1,), 1), (2, (2,), 2)])
        self.push(2, part, 1, 0, 0, (3,), 3, self.place.first(self.swapped(part)))

    def line_last(self, part):
        arrived = [(1, (0, 0), 0), (3, (0,), 0), (3, (1,), 1), (3, (2,), 2), (2, (3,), 3)]
        self.add(part, 0, 0, arrived, True)

    def finish(self, parts):
        for k in range(3):
            for i in range(2):
                self.chunk_copy(k, 0, i).wait_send()
        for part in parts:
            for stage, count in ((1, 8), (2, 4), (3, 3)):
                here = self.box(2, part, 0)

                @pl.loop(0, count)
                def _(i):
                    remote(
                        here, here, self.sends[stage].at[part[0], i], self.recvs[stage].at[part[0], i],
                        self.place.partner(),
                    ).wait_send()


class SmallSum:
    def __init__(self, place, stages, inbox, send, recv):
        self.place, self.stages, self.inbox, self.send, self.recv = place, stages, inbox, send, recv
        self.sent = []

    def push(self, stage, slot, peer):
        copy = remote(self.stages.at[stage], self.inbox.at[slot], self.send.at[slot], self.recv.at[slot], peer)
        copy.start()
        self.sent.append(copy)

    def start(self, i):
        peers = (self.place.partner(), self.place.second(self.place.c), self.place.first(self.place.c))
        if i < 3:
            self.push(i, i, peers[i])
        else:
            for j in range(1, 4):
                self.push(3, 6 - j, self.place.along(j))

    def step(self, i):
        self.sent[i].wait_recv()
        self.stages[i + 1] = self.stages[i] + self.inbox[i]
        self.start(i + 1)

    def finish(self, out):
        for copy in self.sent[3:]:
            copy.wait_recv()
        out[...] = (self.stages[3] + self.inbox[3]) + (self.inbox[4] + self.inbox[5])
        for copy in self.sent:
            copy.wait_send()


class Tokens:
    def __init__(self, place, send, recv, local):
        self.place, self.send, self.recv, self.local = place, send, recv, local
        self.rank = place.y * 2 + place.c

    def other(self, r):
        return ((self.place.y + r // 2) % 2) * 2 + (self.place.c + r % 2) % 2

    def rows(self, rank):
        return pl.ds(pl.multiple_of(rank * 128, 128), 128)

    def gather(self, i, src, dst):
        here = dst.at[self.rows(self.rank), :]
        pltpu.make_async_copy(src.at[self.rank], here, self.local.at[i]).start()
        for r in (2, 3, 1):
            remote(
                src.at[self.other(r)], here, self.send.at[i, r], self.recv.at[i, r], self.place.in_tensor(r)
            ).start()

    def spread(self, i, src, dst):
        here = dst.at[self.rank]
        pltpu.make_async_copy(src.at[self.rows(self.rank), :], here, self.local.at[i]).start()
        for r in (2, 3, 1):
            remote(
                src.at[self.rows(self.other(r)), :], here, self.send.at[i, r], self.recv.at[i, r],
                self.place.in_tensor(r),
            ).start()

    def wait(self, i, block, arrive=True, leave=True):
        for r in (1, 2, 3):
            copy = remote(block, block, self.send.at[i, r], self.recv.at[i, r], self.place.in_tensor(r))
            if arrive:
                copy.wait_recv()
            if leave:
                copy.wait_send()
        if arrive:
            pltpu.make_async_copy(block, block, self.local.at[i]).wait()


def steps(k, s, f, *order):
    return k, s, f, order


EARLY = (
    steps(0, 0, 1, 0), steps(0, 0, 0, 1, 3), steps(1, 0, 1, 0), steps(2, 0, 1, 0), steps(0, 0, 0, 2),
    steps(0, 0, 1, 1, 3), steps(0, 1, 0, 0), steps(0, 1, 1, 0), steps(0, 0, 1, 2), steps(1, 0, 0, 1),
    steps(0, 1, 0, 1, 3), steps(0, 1, 1, 1, 3), steps(1, 0, 0, 3), steps(0, 1, 0, 2), steps(0, 1, 1, 2),
)
X_AFTER = 6
IN_ATTENTION = (
    (steps(1, 0, 0, 2),), (steps(1, 0, 1, 1, 3),), (steps(1, 1, 0, 0),), (steps(1, 1, 1, 0), steps(2, 1, 0, 0)),
    (steps(2, 0, 0, 1),), (steps(1, 0, 1, 2),), (steps(1, 1, 0, 1, 3), steps(2, 1, 1, 0)), (steps(1, 1, 1, 1),),
    (steps(1, 1, 1, 3), steps(2, 0, 0, 3)), (steps(1, 1, 0, 2),), (steps(2, 0, 0, 2),), (steps(1, 1, 1, 2),),
)
IN_UP = (
    (steps(2, 0, 1, 1),), (steps(2, 1, 0, 1),), (steps(2, 1, 0, 3),), (steps(2, 0, 1, 3),), (steps(2, 1, 0, 2),),
    (steps(2, 1, 1, 1),), (steps(2, 0, 1, 2),), (steps(2, 1, 1, 3),),
)
LATE = (steps(2, 1, 1, 2),)
DOWN, UP, FRONT, BACK = (2, 2, (0, 768)), (1, 1, (0, 768)), (0, 0, (0, 512)), (3, 0, (512, 256))


def sums_in_up(scatter):
    return (
        ((1, scatter.line_far, DOWN),),
        ((1, scatter.line_near, DOWN, (2, 1)),),
    )


def sums_in_attention(scatter):
    return (
        ((0, scatter.line_near, DOWN, (3,)), (0, scatter.add_far, UP, (2,)), (1, scatter.add_near, UP, (2,))),
        ((0, scatter.add_far, UP, (1,)), (1, scatter.add_near, UP, (1,))),
        ((0, scatter.add_far, UP, (3,)), (1, scatter.add_near, UP, (3,))),
        ((0, scatter.add_far, UP, (0,)),),
        (),
        ((0, scatter.line_turn, DOWN),),
        (),
        (),
    )


def spots(rows, offset, gap=0):
    source = lax.broadcasted_iota(jnp.int32, (96, 768), 0) + rows
    target = lax.broadcasted_iota(jnp.int32, (96, 768), 1)
    moved = source + offset + jnp.where(source < 128, 0, gap)
    return jnp.where(target == moved, F32(1), F32(0)).astype(BF16)


def pack_small(place, vec_in, bias_in):
    group = place.z * 2 + place.x
    rows = vec_in[...]
    top = dot(rows, spots(96 * group, 0, 0))
    start = 96 * (group % 2)
    queries = dot(rows, spots(start, 0, 256))[0:1]
    values = dot(rows, spots(start, 256, 192))[1:2]
    units = bias_in[...].astype(F32).reshape(1, bias_in.shape[0])
    lane = lax.broadcasted_iota(jnp.int32, (1, 768), 1)
    units = jnp.where(lane // 384 == group % 2, jnp.concatenate([units, units], axis=1), 0.0)
    line = lax.broadcasted_iota(jnp.int32, (8, 768), 0)
    low = jnp.where(line == group // 2, units, 0.0) + jnp.where(line == 4 + group // 2, queries + values, 0.0)
    return jnp.concatenate([top, low], axis=0).astype(BF16)


def pack_attention(qkv_in, out_in):
    q, k, v = (qkv_in[i].astype(F32) for i in range(3))
    o = jnp.transpose(out_in[...].astype(F32))
    return jnp.concatenate([
        q[:, :128], k[:, :128], v[:, :128], jnp.concatenate([q[:, 128:], k[:, 128:]], axis=1),
        jnp.concatenate([o[:, 128:], v[:, 128:]], axis=1), o[:, :128],
    ], axis=1).astype(BF16)


def finish_kernel(
    dp_count, out_in, gtok_in, shard, small,
    output, gtok, qkv, out, up, down, vec, units,
):
    stride = dp_count // 8
    rank = lax.axis_index("dp")
    group, part = rank // stride, vec.shape[1]
    output[...] = out_in[...]
    gtok[...] = gtok_in[...].astype(F32)
    a = shard[0]
    qkv[0, :, 0:128] = a[:, 0:128]
    qkv[1, :, 0:128] = a[:, 128:256]
    qkv[2, :, 0:128] = a[:, 256:384]
    qkv[0, :, 128:192] = a[:, 384:448]
    qkv[1, :, 128:192] = pltpu.roll(a[:, 384:512], 64, 1)[:, 0:64]
    qkv[2, :, 128:192] = pltpu.roll(a[:, 512:640], 64, 1)[:, 0:64]
    out[0:128, :] = jnp.transpose(a[:, 640:768])
    out[128:192, :] = jnp.transpose(a[:, 512:640])[0:64]
    up[...] = shard[1]
    down[...] = shard[2]

    rest = rank % stride
    even = group % 2 == 0
    lane = lax.broadcasted_iota(jnp.int32, (1, 768), 1)

    def own_lines(row, first, second):
        near = pltpu.roll(row, jnp.where(even, (768 - first) % 768, 768 - first - 96), 1)
        far = pltpu.roll(row, 768 - second + 32, 1)
        return jnp.where(even | (lane < 32), near, far)

    line = lax.broadcasted_iota(jnp.int32, (8, 768), 0)
    packed = small[8:16, :]
    row = jnp.sum(jnp.where(line == 4 + group // 2, packed, 0.0), axis=0, keepdims=True)
    queries = own_lines(row, 0, 384)
    values = own_lines(row, 256, 576)
    lines = pltpu.roll(small[0:8, :], (768 - 96 * group) % 768, 1)
    lines = jnp.where(line == 0, queries, jnp.where(line == 1, values, lines))
    lines = pltpu.roll(lines, (768 - rest * part) % 768, 1)
    vec[...] = lines[:, 0:part]
    row = jnp.sum(jnp.where(line == group // 2, packed, 0.0), axis=0, keepdims=True)
    shift = 384 * (group % 2) + rest * 4 * part
    units[...] = pltpu.roll(row, (768 - shift) % 768, 1)[:, 0 : 4 * part].reshape(4 * part)


def finish_call(dp_count, out, gtok, shard, small):
    rows, width = shard.shape[1], shard.shape[2]
    shapes = (
        (out.shape, BF16), (gtok.shape, F32), ((3, rows, width // 4), F32), ((width // 4, rows), F32),
        ((rows, width), F32), ((rows, width), F32), ((8, rows), F32), ((4 * rows,), F32),
    )
    vmem = pl.BlockSpec(memory_space=pltpu.VMEM)
    return pl.pallas_call(
        functools.partial(finish_kernel, dp_count),
        out_shape=[jax.ShapeDtypeStruct(s, d) for s, d in shapes],
        in_specs=[vmem] * 4,
        out_specs=[vmem] * 8,
        compiler_params=pltpu.CompilerParams(vmem_limit_bytes=VMEM_LIMIT),
        name="finish",
    )(out, gtok, shard, small)


def layer_kernel(
    dp_count, x_in, go_in, qkv_in, out_in, up_in, down_in, vec_in, bias_in, len_ref,
    output, gtok, shard, small,
    own_first, small_in, w, x, go, smalls, sm, qkv, ctx, act, gp, hb, n1, s1, stat, gsm,
    acc, pre, low_grad, tall, gctx, gpacked,
    box_p, box_s, box_f, box_z, stages, small_box,
    send, recv, tok_send, tok_recv, tok_local, own_local, bias_send, bias_recv,
    send_p, recv_p, send_s, recv_s, send_f, recv_f, send_z, recv_z, small_send, small_recv,
):
    seq, width = x.shape
    blocks = seq // ROWS
    place = Place(dp_count)
    own = (own_first, up_in, down_in)
    gather = Gather(place, own, w, send, recv)
    own_first[...] = pack_attention(qkv_in, out_in)
    small_in[...] = pack_small(place, vec_in, bias_in)
    tokens = Tokens(place, tok_send, tok_recv, tok_local)

    barrier(place)
    gather.along(0)
    gather.start(0)
    for k in range(3):
        pltpu.make_async_copy(own[k], gather.piece(k, 0, 0, 0), own_local.at[k]).start()
    pltpu.make_async_copy(small_in, smalls.at[0], own_local.at[3]).start()
    for j in range(4):
        for i in range(2):
            if j or i:
                slot = ((4 - j) % 4) * 2 + i
                remote(
                    small_in, smalls.at[slot], bias_send.at[slot], bias_recv.at[slot], place.in_dp(j, i)
                ).start()
    for k in (1, 2):
        gather.along(k)
        gather.start(k)
    for event in EARLY[:X_AFTER]:
        gather.relay(*event)
    tokens.gather(0, x_in, x)
    for event in EARLY[X_AFTER:]:
        gather.relay(*event)
    for k in range(3):
        pltpu.make_async_copy(own[k], own[k], own_local.at[k]).wait()
    pltpu.make_async_copy(small_in, small_in, own_local.at[3]).wait()

    @pl.loop(1, 8)
    def _(slot):
        remote(small_in, small_in, bias_send.at[slot], bias_recv.at[slot], place.partner()).wait()

    total = smalls[0].astype(F32)
    for i in range(1, 8):
        total += smalls[i].astype(F32)
    sm[...] = total
    tokens.wait(0, x_in.at[0])
    gather.others(0)

    low, high = lane_masks(0.125)
    length = len_ref[place.y * 2 + place.c]
    key_bias = jnp.where(lax.broadcasted_iota(jnp.int32, (1, seq), 1) < length, F32(0), F32(NEG))
    acc[...] = jnp.zeros_like(acc)

    def relays(step, table):
        for n, events in enumerate(table):
            if events:
                @pl.when(step == n)
                def _():
                    for event in events:
                        gather.relay(*event)

    @pl.loop(0, 4)
    def _(t):
        relays(3 * t, IN_ATTENTION)
        proj = dot(x[...], w[0, t, :, 0:640]) + sm[pl.ds(12 + t, 1), 0:640]
        qkv[t, :, 0:640] = proj.astype(BF16)
        q_two = pltpu.roll(jnp.where(is_low((seq, 128)), proj[:, 384:512] * 0.125, 0.0), 64, 1)
        qkv[t, :, 640:768] = q_two.astype(BF16)

        @pl.loop(0, seq // 256)
        def _(r):
            relays(3 * t + r + 1, IN_ATTENTION)
            rows = pl.ds(pl.multiple_of(r * 256, 256), 256)
            q_pair = qkv[t, rows, 0:128]
            outs = []
            stats = []
            for h in range(3):
                if h < 2:
                    queries = q_pair * (low, high)[h]
                    keys = qkv[t, :, 128:256]
                    values = qkv[t, :, 256:384]
                else:
                    queries = qkv[t, rows, 640:768]
                    keys = qkv[t, :, 384:512]
                    values = qkv[t, :, 512:640]
                scores = dot_nt(queries, keys) + key_bias
                highest = jnp.max(scores, axis=1, keepdims=True)
                grown = jnp.exp(scores - highest)
                total = jnp.sum(grown, axis=1, keepdims=True)
                probs = (grown * (1.0 / total)).astype(BF16)
                outs.append(dot(probs, values))
                stats.append(highest + jnp.log(total))
            lowest = is_low((256, 128))
            ctx[t, rows, 0:128] = jnp.where(lowest, pltpu.roll(outs[2], 64, 1), 0.0).astype(BF16)
            ctx[t, rows, 128:256] = jnp.where(lowest, outs[0], outs[1]).astype(BF16)
            lane = lax.broadcasted_iota(jnp.int32, (256, 128), 1)
            stat[t, rows, :] = jnp.where(lane == 0, stats[0], jnp.where(lane == 1, stats[1], stats[2]))

        acc[...] += dot_nt(ctx[t], w[0, t, :, 512:768])

    @pl.loop(0, blocks)
    def _(r):
        rows = pl.ds(pl.multiple_of(r * ROWS, ROWS), ROWS)
        resid = x[rows, :].astype(F32) + acc[rows, :] + sm[2:3, :]
        centred = resid - jnp.mean(resid, axis=1, keepdims=True)
        scale = lax.rsqrt(jnp.mean(centred * centred, axis=1, keepdims=True) + EPS)
        normed = centred * scale
        hidden = normed * sm[3:4, :] + sm[4:5, :]
        n1[rows, :] = normed
        s1[rows, :] = jnp.broadcast_to(scale, (ROWS, 128))
        hb[rows, :] = hidden.astype(BF16)
        acc[rows, :] = hidden + sm[5:6, :]

    gather.others(1)

    @pl.loop(0, 4)
    def _(t):
        relays(2 * t, IN_UP)
        pre[...] = dot(hb[...], w[1, t])

        relays(2 * t + 1, IN_UP)

        @pl.loop(0, blocks)
        def _(r):
            rows = pl.ds(pl.multiple_of(r * ROWS, ROWS), ROWS)
            u = pre[rows, :] + sm[pl.ds(8 + t, 1), :]
            cdf = 0.5 + 0.5 * lax.erf(u * F32(np.sqrt(0.5)))
            density = jnp.exp(u * u * -0.5) * F32(1.0 / np.sqrt(2.0 * np.pi))
            act[t, rows, :] = (u * cdf).astype(BF16)
            gp[t, rows, :] = (cdf + u * density).astype(BF16)

    for event in LATE:
        gather.relay(*event)
    tokens.gather(1, go_in, go)
    gather.others(2)

    @pl.loop(0, 4)
    def _(t):
        acc[...] += dot_nt(act[t], w[2, t])

    gsm[...] = jnp.zeros_like(gsm)

    @pl.loop(0, blocks)
    def _(r):
        rows = pl.ds(pl.multiple_of(r * ROWS, ROWS), ROWS)
        resid = acc[rows, :]
        centred = resid - jnp.mean(resid, axis=1, keepdims=True)
        scale = lax.rsqrt(jnp.mean(centred * centred, axis=1, keepdims=True) + EPS)
        acc[rows, :] = centred * scale
        pre[rows, 0:128] = jnp.broadcast_to(scale, (ROWS, 128))

    tall[1] = jnp.transpose(hb[...].astype(F32)).astype(BF16)
    tokens.wait(1, x_in.at[0])

    @pl.loop(0, blocks)
    def _(r):
        rows = pl.ds(pl.multiple_of(r * ROWS, ROWS), ROWS)
        normed = acc[rows, :]
        gain = sm[6:7, :]
        cot = go[rows, :].astype(F32)
        go[rows, :] = (normed * gain + sm[7:8, :]).astype(BF16)
        e = cot * gain
        en = jnp.mean(e * normed, axis=1, keepdims=True)
        grad = pre[rows, 0:1] * (e - jnp.mean(e, axis=1, keepdims=True) - normed * en)
        acc[rows, :] = grad
        low_grad[rows, :] = grad.astype(BF16)
        gsm[5:6, :] += jnp.sum(grad, axis=0, keepdims=True)
        gsm[6:7, :] += jnp.sum(cot * normed, axis=0, keepdims=True)
        gsm[7:8, :] += jnp.sum(cot, axis=0, keepdims=True)

    tokens.spread(2, go, output)
    gather.finish()
    scatter = Scatter(
        place, w, (box_p, box_s, box_f, box_z), (send_p, send_s, send_f, send_z), (recv_p, recv_s, recv_f, recv_z),
        shard,
    )
    tall[0] = jnp.transpose(acc[...]).astype(BF16)

    def chunk(i, core):
        return ((place.y + 1 - i) % 2) * 2 + core

    def own_chunk(k, i, t, value):
        scatter.from_partner(k, i)
        w[k, t] = (value + box_p[k, i].astype(F32)).astype(BF16)
        parts = (DOWN,) if k == 2 else (UP,)
        pl.when(i == 0)(lambda: scatter.ready(parts, 0))
        pl.when(i == 1)(lambda: scatter.ready(parts, 1))

    def down_back(t):
        grad_pre = dot(low_grad[...], w[2, t]) * gp[t].astype(F32)
        put_row(gsm, t, slice(0, 768), jnp.sum(grad_pre, axis=0, keepdims=True))
        gp[t] = grad_pre.astype(BF16)
        return dot(tall[0], act[t])

    def up_back(t):
        acc[...] += dot_nt(gp[t], w[1, t])
        return dot(tall[1], gp[t])

    def sums_at(i, events):
        for turn in (0, 1):
            now = [event for event in events if event[0] == turn]
            if now:
                @pl.when(i == turn)
                def _():
                    for _, function, *arguments in now:
                        function(*arguments)

    for k, back in ((2, down_back), (1, up_back)):
        events = ((), ()) if k == 2 else sums_in_up(scatter)

        @pl.loop(0, 2)
        def _(i):
            t = chunk(i, 1 - place.c)
            w[k, t] = back(t).astype(BF16)
            scatter.to_partner(k, t, i)
            sums_at(i, events[0])
            t = chunk(i, place.c)
            own_chunk(k, i, t, back(t))
            sums_at(i, events[1])

    @pl.loop(0, blocks)
    def _(r):
        rows = pl.ds(pl.multiple_of(r * ROWS, ROWS), ROWS)
        cot = acc[rows, :]
        normed = n1[rows, :]
        e = cot * sm[3:4, :]
        en = jnp.mean(e * normed, axis=1, keepdims=True)
        grad = s1[rows, 0:1] * (e - jnp.mean(e, axis=1, keepdims=True) - normed * en)
        acc[rows, :] = grad
        low_grad[rows, :] = grad.astype(BF16)
        gsm[2:3, :] += jnp.sum(grad, axis=0, keepdims=True)
        gsm[3:4, :] += jnp.sum(cot * normed, axis=0, keepdims=True)
        gsm[4:5, :] += jnp.sum(cot, axis=0, keepdims=True)

    tall[0] = jnp.transpose(acc[...]).astype(BF16)
    tall[1] = jnp.transpose(x[...].astype(F32)).astype(BF16)

    one_low, one_high = lane_masks(1.0)
    tall_bias = jnp.where(lax.broadcasted_iota(jnp.int32, (seq, 1), 0) < length, F32(0), F32(NEG))

    def attention_back(t, event, store):
        back = dot(low_grad[...], w[0, t, :, 512:768])
        gctx[:, 0:128] = pltpu.roll(jnp.where(is_low((seq, 128)), back[:, 0:128], 0.0), 64, 1).astype(BF16)
        gctx[:, 128:256] = back[:, 128:256].astype(BF16)
        log_rows = jnp.transpose(stat[t])
        grads_q = []
        grads_k = []
        grads_v = []
        for h in range(3):
            if h < 2:
                queries = qkv[t, :, 0:128] * (low, high)[h]
                keys = qkv[t, :, 128:256]
                values = qkv[t, :, 256:384]
                cots = gctx[:, 128:256] * (one_low, one_high)[h]
            else:
                queries = qkv[t, :, 640:768]
                keys = qkv[t, :, 384:512]
                values = qkv[t, :, 512:640]
                cots = gctx[:, 0:128]
            scores = dot_nt(keys, queries) + tall_bias
            probs = jnp.exp(scores - log_rows[h : h + 1, :])
            grad_probs = dot_nt(values, cots)
            row_dots = jnp.sum(grad_probs * probs, axis=0, keepdims=True)
            grad_scores = (probs * (grad_probs - row_dots)).astype(BF16)
            grads_v.append(dot(probs.astype(BF16), cots))
            grads_k.append(dot(grad_scores, queries))
            part = (0, HD, HD)[h]
            keys_tall = jnp.transpose(keys.astype(F32))[part : part + HD, :].astype(BF16)
            grads_q.append(dot(keys_tall, grad_scores) * 0.125)
            event(h)
        pair = jnp.transpose(jnp.concatenate([grads_q[0], grads_q[1]], axis=0))
        single = jnp.transpose(jnp.concatenate([grads_q[2], jnp.zeros_like(grads_q[2])], axis=0))
        tiles = [pair, grads_k[0] + grads_k[1], grads_v[0] + grads_v[1], single + grads_k[2], grads_v[2]]
        for i, tile in enumerate(tiles):
            span = slice(128 * i, 128 * i + 128)
            put_row(gsm, 4 + t, span, jnp.sum(tile, axis=0, keepdims=True))
            gpacked[:, span] = tile.astype(BF16)
        event(3)
        acc[...] += dot_nt(gpacked[...], w[0, t, :, 0:640])
        store(slice(0, 512), dot(tall[1], gpacked[:, 0:512]))
        store(slice(512, 640), dot(tall[1], gpacked[:, 512:640]) + dot(tall[0], ctx[t, :, 0:128]))
        store(slice(640, 768), dot(tall[0], ctx[t, :, 128:256]))

    @pl.loop(0, 2)
    def _(i):
        other = chunk(i, 1 - place.c)
        mine = chunk(i, place.c)

        def store_other(span, value):
            w[0, other, :, span] = value.astype(BF16)

        def store_mine(span, value):
            w[0, mine, :, span] = (value + box_p[0, i, :, span].astype(F32)).astype(BF16)

        events = sums_in_attention(scatter)

        def event_other(h):
            sums_at(i, events[h])

        def event_mine(h):
            sums_at(i, events[4 + h])
            if h == 3:
                scatter.from_partner(0, i)

        attention_back(other, event_other, store_other)
        scatter.to_partner(0, other, i)
        attention_back(mine, event_mine, store_mine)
        pl.when(i == 0)(lambda: scatter.ready((FRONT, BACK), 0))
        pl.when(i == 1)(lambda: scatter.ready((FRONT, BACK), 1))

    x[...] = acc[...].astype(BF16)
    stages[0] = gsm[...]
    sums = SmallSum(place, stages, small_box, small_send, small_recv)
    sums.start(0)
    scatter.add_far(FRONT)
    scatter.add_far(BACK)
    tokens.spread(3, x, gtok)
    sums.step(0)
    scatter.add_near(FRONT)
    sums.step(1)
    scatter.add_near(BACK)
    sums.step(2)
    scatter.line_last(DOWN)
    scatter.add_last(UP)
    sums.finish(small)
    scatter.add_last(FRONT)
    scatter.add_last(BACK)
    for i in (2, 3):
        tokens.wait(i, x_in.at[0])
    scatter.finish((DOWN, UP, FRONT, BACK))


def layer_call(dp_count, tokens, grad_out, weights, vectors, bias, lengths):
    part, width = tokens.shape[1], tokens.shape[2]
    seq = tokens.shape[0] * part
    shapes = (((4, part, width), BF16), ((4, part, width), BF16), ((3, 96, width), F32), ((16, width), F32))
    vmem = pl.BlockSpec(memory_space=pltpu.VMEM)
    smem = pl.BlockSpec(memory_space=pltpu.SMEM)
    dma = pltpu.SemaphoreType.DMA
    low_rows = pltpu.VMEM((seq, width), BF16)
    wide_rows = pltpu.VMEM((seq, width), F32)
    return pl.pallas_call(
        functools.partial(layer_kernel, dp_count),
        out_shape=[jax.ShapeDtypeStruct(s, d) for s, d in shapes],
        in_specs=[vmem] * 8 + [smem],
        out_specs=[vmem] * 4,
        scratch_shapes=[
            pltpu.VMEM((96, width), BF16), pltpu.VMEM((16, width), BF16),
            pltpu.VMEM((3, 4, width, 768), BF16), low_rows, low_rows, pltpu.VMEM((8, 16, width), BF16),
            pltpu.VMEM((16, width), F32), pltpu.VMEM((4, seq, 768), BF16), pltpu.VMEM((4, seq, 256), BF16),
            pltpu.VMEM((4, seq, 768), BF16), pltpu.VMEM((4, seq, 768), BF16), low_rows, wide_rows,
            pltpu.VMEM((seq, 128), F32), pltpu.VMEM((4, seq, 128), F32), pltpu.VMEM((16, width), F32),
            wide_rows, wide_rows, low_rows, pltpu.VMEM((2, width, seq), BF16),
            pltpu.VMEM((seq, 256), BF16), pltpu.VMEM((seq, 640), BF16),
            pltpu.VMEM((3, 2, width, 768), BF16), pltpu.VMEM((3, 2, 4, 96, width), BF16),
            pltpu.VMEM((3, 4, 96, width), BF16), pltpu.VMEM((3, 3, 96, width), BF16),
            pltpu.VMEM((4, 16, width), F32), pltpu.VMEM((6, 16, width), F32),
            dma((3, 31)), dma((3, 32)), dma((4, 4)), dma((4, 4)), dma((4,)), dma((4,)), dma((8,)), dma((8,)),
            dma((3, 2)), dma((3, 2)), dma((4, 8)), dma((4, 8)), dma((4, 4)), dma((4, 4)), dma((4, 3)), dma((4, 3)),
            dma((6,)), dma((6,)),
        ],
        compiler_params=pltpu.CompilerParams(
            vmem_limit_bytes=VMEM_LIMIT, collective_id=0, has_side_effects=True
        ),
        name="layer",
    )(tokens, grad_out, *weights, vectors, bias, lengths)


def gather_groups(shard, dp_count, axis):
    stride = dp_count // 8
    if stride == 1:
        return shard
    groups = [[g * stride + i for i in range(stride)] for g in range(8)]
    return lax.all_gather(shard, "dp", axis=axis, tiled=True, axis_index_groups=groups)


def scatter_groups(shard, small, dp_count):
    stride = dp_count // 8
    if stride == 1:
        return shard, small
    groups = [[g * stride + i for i in range(stride)] for g in range(8)]
    shard = lax.psum_scatter(shard, "dp", scatter_dimension=1, tiled=True, axis_index_groups=groups)
    return shard, lax.psum(small, "dp", axis_index_groups=groups)


def shards(tokens, lengths, grad_out, qkv_weight, out_weight, up_weight, down_weight, vectors, hidden_bias):
    dp_count = lax.axis_size("dp")
    weights = [
        gather_groups(weight, dp_count, axis)
        for weight, axis in ((qkv_weight, 1), (out_weight, 1), (up_weight, 0), (down_weight, 1))
    ]
    weights[3] = weights[3].T
    vectors = gather_groups(vectors, dp_count, 1)
    bias = gather_groups(hidden_bias, dp_count, 0)
    output, gtok, g, gsm = layer_call(dp_count, tokens, grad_out, weights, vectors, bias, lengths)
    g, gsm = scatter_groups(g, gsm, dp_count)
    *results, down, vec, units = finish_call(dp_count, output, gtok, g, gsm)
    return *results, down.T, vec, units


def solution(mesh):
    in_specs = (
        P("dp", "tensor", None), P("dp"), P("dp", "tensor", None), P(None, "dp", "tensor"), P("tensor", "dp"),
        P("dp", "tensor"), P("tensor", "dp"), P(None, "dp"), P("dp"),
    )
    out_specs = (
        P("dp", "tensor", None), P("dp", "tensor", None), P(None, "dp", "tensor"), P("tensor", "dp"),
        P("dp", "tensor"), P("tensor", "dp"), P(None, "dp"), P("dp"),
    )
    return jax.shard_map(shards, mesh=mesh, in_specs=in_specs, out_specs=out_specs, check_vma=False)
```

```python
import functools

import jax
import jax.numpy as jnp
import numpy as np
from jax import lax
from jax.experimental import pallas as pl
from jax.experimental.pallas import tpu as pltpu
from jax.sharding import PartitionSpec as P

HD = 64
EPS = 1e-12
NEG = -1e30
F32 = jnp.float32
BF16 = jnp.bfloat16
VMEM_LIMIT = 67043328
ROWS = 128


def dot(left, right):
    return lax.dot_general(left, right, (((1,), (0,)), ((), ())), preferred_element_type=F32)


def dot_nt(left, right):
    return lax.dot_general(left, right, (((1,), (1,)), ((), ())), preferred_element_type=F32)


def lane_masks(scale):
    lane = lax.broadcasted_iota(jnp.int32, (1, 128), 1)
    low = jnp.where(lane < HD, F32(scale), F32(0)).astype(BF16)
    high = jnp.where(lane < HD, F32(0), F32(scale)).astype(BF16)
    return low, high


def is_low(shape):
    return lax.broadcasted_iota(jnp.int32, shape, 1) < HD


def put_row(ref, row, span, value):
    old = ref[8:16, span]
    here = lax.broadcasted_iota(jnp.int32, old.shape, 0) == row
    ref[8:16, span] = jnp.where(here, value, old)


class Place:
    def __init__(self, dp_count):
        self.stride = dp_count // 8
        dp_rank = lax.axis_index("dp")
        tensor_rank = lax.axis_index("tensor")
        group = dp_rank // self.stride
        self.rest = dp_rank % self.stride
        self.z, self.x = group // 2, group % 2
        self.y, self.c = tensor_rank // 2, tensor_rank % 2

    def device(self, z, x, y, c):
        return ((z * 2 + x) * self.stride + self.rest, y * 2 + c)

    def shifted(self, j, second, first, swapped):
        across_x = swapped * second + (1 - swapped) * first
        across_y = swapped * first + (1 - swapped) * second
        return (self.z + j) % 4, (self.x + across_x) % 2, (self.y + across_y) % 2

    def first(self, swapped):
        return self.device(*self.shifted(0, 0, 1, swapped), self.c)

    def second(self, swapped):
        return self.device(*self.shifted(0, 1, 0, swapped), self.c)

    def partner(self):
        return self.device(self.z, self.x, self.y, 1 - self.c)

    def along(self, j):
        return self.device((self.z + j) % 4, self.x, self.y, self.c)

    def in_tensor(self, r):
        return self.device(self.z, self.x, (self.y + r // 2) % 2, (self.c + r % 2) % 2)

    def in_dp(self, j, i):
        return self.device((self.z + j) % 4, (self.x + i) % 2, self.y, self.c)


def remote(src, dst, send, recv, device):
    return pltpu.make_async_remote_copy(
        src_ref=src, dst_ref=dst, send_sem=send, recv_sem=recv, device_id=device,
        device_id_type=pl.DeviceIdType.MESH,
    )


def barrier(place):
    sem = pltpu.get_barrier_semaphore()
    peers = [place.in_dp(j, i) for j in range(4) for i in range(2) if j or i]
    peers += [place.in_tensor(r) for r in range(1, 4)]
    for peer in peers:
        pl.semaphore_signal(sem, inc=1, device_id=peer, device_id_type=pl.DeviceIdType.MESH)
    pl.semaphore_wait(sem, len(peers))


class Gather:
    def __init__(self, place, own, w, send, recv):
        self.place, self.own, self.w, self.send, self.recv = place, own, w, send, recv

    def piece(self, k, s, f, j):
        z, x, y = self.place.shifted(j, s, f, self.swapped(k))
        return self.w.at[k, y * 2 + self.place.c, pl.ds(pl.multiple_of((z * 2 + x) * 96, 96), 96), :]

    def swapped(self, k):
        return 1 if k == 1 else self.place.c

    def push(self, k, src, dst, send, recv, device):
        remote(src, dst, self.send.at[k, send], self.recv.at[k, recv], device).start()

    def forward(self, k, s, f, j, to):
        here = self.piece(k, s, f, j)
        src = self.own[k] if (s, f, j) == (0, 0, 0) else here
        if "f" in to:
            self.push(k, src, here, 3 + j, 4 + j, self.place.first(self.swapped(k)))
        if "s" in to:
            self.push(k, src, here, 7 + 4 * f + j, 8 + 4 * f + j, self.place.second(self.swapped(k)))
        if "p" in to:
            self.push(k, src, here, 15 + 8 * s + 4 * f + j, 16 + 8 * s + 4 * f + j, self.place.partner())

    def along(self, k, f=0):
        here = self.piece(k, 0, f, 0)
        for j in (1, 3, 2):
            self.push(k, here if f else self.own[k], here, 4 * f + j - 1, 4 * f + 4 - j, self.place.along(j))

    def start(self, k):
        self.forward(k, 0, 0, 0, "fsp")

    def wait(self, k, slot):
        here = self.own[k]
        remote(here, here, self.send.at[k, 0], self.recv.at[k, slot], self.place.partner()).wait_recv()

    def relay(self, k, s, f, order):
        for j in order:
            self.wait(k, 8 * s + 4 * f + j)
            self.forward(k, s, f, j, "p" if s else "sp" if f else "fsp")

    def others(self, k):
        @pl.loop(16, 32)
        def _(slot):
            self.wait(k, slot)

    def finish(self):
        for k in range(3):
            here = self.own[k]

            @pl.loop(0, 31)
            def _(slot):
                remote(here, here, self.send.at[k, slot], self.recv.at[k, 1], self.place.partner()).wait_send()


class Scatter:
    def __init__(self, place, g, boxes, sends, recvs, out):
        self.place, self.g, self.boxes, self.sends, self.recvs, self.out = place, g, boxes, sends, recvs, out

    def swapped(self, part):
        return self.place.c

    def box(self, stage, part, *index):
        return self.boxes[stage].at[(part[1], *index, slice(None), pl.ds(*part[2]))]

    def push(self, stage, part, f_from, s_from, j, index, sem, device):
        k, t, row = self.piece(part, s_from, f_from, j)
        src = self.g.at[k, t, pl.ds(row, 96), pl.ds(*part[2])]
        remote(
            src, self.box(stage, part, *index), self.sends[stage].at[part[0], sem],
            self.recvs[stage].at[part[0], sem], device,
        ).start()

    def piece(self, part, s, f, j):
        z, x, y = self.place.shifted(j, s, f, self.swapped(part))
        return part[1], y * 2 + self.place.c, pl.multiple_of((z * 2 + x) * 96, 96)

    def wait(self, stage, part, index, sem):
        here = self.box(stage, part, *index)
        remote(
            here, here, self.sends[stage].at[part[0], sem], self.recvs[stage].at[part[0], sem], self.place.partner()
        ).wait_recv()

    def chunk_copy(self, k, t, i):
        return remote(
            self.g.at[k, t], self.boxes[0].at[k, i], self.sends[0].at[k, i], self.recvs[0].at[k, i],
            self.place.partner(),
        )

    def to_partner(self, k, t, i):
        self.chunk_copy(k, t, i).start()

    def from_partner(self, k, i):
        self.chunk_copy(k, 0, i).wait_recv()

    def across(self, part, f):
        for j in (2, 1, 3, 0):
            self.push(1, part, f, 1, j, (f, j), 4 * f + j, self.place.second(self.swapped(part)))

    def ready(self, parts, i):
        if i == 0:
            for part in parts:
                self.across(part, 1)

        for part in parts:
            pl.when(self.swapped(part) == i)(lambda: self.across(part, 0))

    def total(self, part, f, j, views, last=False):
        k, t, row = self.piece(part, 0, f, j)
        columns = pl.ds(*part[2])

        @pl.loop(0, 3)
        def _(r):
            lines = pl.ds(pl.multiple_of(row + r * 32, 32), 32)
            local = pl.ds(pl.multiple_of(r * 32, 32), 32)
            value = self.g[k, t, lines, columns].astype(F32)
            for stage, index in views:
                value += self.boxes[stage][(k, *index, local, columns)].astype(F32)
            if last:
                self.out[k, local, columns] = value
            else:
                self.g[k, t, lines, columns] = value.astype(BF16)

    def add(self, part, f, j, arrived, last=False):
        for stage, index, sem in arrived:
            self.wait(stage, part, index, sem)
        self.total(part, f, j, [(stage, index) for stage, index, _ in arrived], last)

    def add_far(self, part, line=(2, 1, 3, 0)):
        for j in line:
            self.add(part, 1, j, [(1, (1, j), 4 + j)])
            self.push(2, part, 1, 0, j, (j,), j, self.place.first(self.swapped(part)))

    def add_near(self, part, line=(2, 1, 3)):
        for j in line:
            self.add(part, 0, j, [(1, (0, j), j), (2, (j,), j)])
            self.push(3, part, 0, 0, j, (3 - j,), 3 - j, self.place.along(j))

    def add_last(self, part):
        arrived = [(1, (0, 0), 0), (2, (0,), 0), (3, (0,), 0), (3, (1,), 1), (3, (2,), 2)]
        self.add(part, 0, 0, arrived, True)

    def line_far(self, part, line=(2, 1, 3)):
        for j in line:
            self.add(part, 1, j, [(1, (1, j), 4 + j)])
            self.push(2, part, 1, 0, j, (3 - j,), 3 - j, self.place.along(j))

    def line_near(self, part, line=(2, 1, 3)):
        for j in line:
            self.add(part, 0, j, [(1, (0, j), j)])
            self.push(3, part, 0, 0, j, (3 - j,), 3 - j, self.place.along(j))

    def line_turn(self, part):
        self.add(part, 1, 0, [(1, (1, 0), 4), (2, (0,), 0), (2, (1,), 1), (2, (2,), 2)])
        self.push(2, part, 1, 0, 0, (3,), 3, self.place.first(self.swapped(part)))

    def line_last(self, part):
        arrived = [(1, (0, 0), 0), (3, (0,), 0), (3, (1,), 1), (3, (2,), 2), (2, (3,), 3)]
        self.add(part, 0, 0, arrived, True)

    def finish(self, parts):
        for k in range(3):
            for i in range(2):
                self.chunk_copy(k, 0, i).wait_send()
        for part in parts:
            for stage, count in ((1, 8), (2, 4), (3, 3)):
                here = self.box(2, part, 0)

                @pl.loop(0, count)
                def _(i):
                    remote(
                        here, here, self.sends[stage].at[part[0], i], self.recvs[stage].at[part[0], i],
                        self.place.partner(),
                    ).wait_send()


class SmallSum:
    def __init__(self, place, stages, inbox, send, recv):
        self.place, self.stages, self.inbox, self.send, self.recv = place, stages, inbox, send, recv
        self.sent = []

    def push(self, stage, slot, peer):
        copy = remote(self.stages.at[stage], self.inbox.at[slot], self.send.at[slot], self.recv.at[slot], peer)
        copy.start()
        self.sent.append(copy)

    def start(self, i):
        peers = (self.place.partner(), self.place.second(self.place.c), self.place.first(self.place.c))
        if i < 3:
            self.push(i, i, peers[i])
        else:
            for j in range(1, 4):
                self.push(3, 6 - j, self.place.along(j))

    def step(self, i):
        self.sent[i].wait_recv()
        self.stages[i + 1] = self.stages[i] + self.inbox[i]
        self.start(i + 1)

    def finish(self, out):
        for copy in self.sent[3:]:
            copy.wait_recv()
        out[...] = (self.stages[3] + self.inbox[3]) + (self.inbox[4] + self.inbox[5])
        for copy in self.sent:
            copy.wait_send()


class Tokens:
    def __init__(self, place, send, recv, local):
        self.place, self.send, self.recv, self.local = place, send, recv, local
        self.rank = place.y * 2 + place.c

    def other(self, r):
        return ((self.place.y + r // 2) % 2) * 2 + (self.place.c + r % 2) % 2

    def rows(self, rank):
        return pl.ds(pl.multiple_of(rank * 128, 128), 128)

    def gather(self, i, src, dst):
        here = dst.at[self.rows(self.rank), :]
        pltpu.make_async_copy(src.at[self.rank], here, self.local.at[i]).start()
        for r in (2, 3, 1):
            remote(
                src.at[self.other(r)], here, self.send.at[i, r], self.recv.at[i, r], self.place.in_tensor(r)
            ).start()

    def spread(self, i, src, dst):
        here = dst.at[self.rank]
        pltpu.make_async_copy(src.at[self.rows(self.rank), :], here, self.local.at[i]).start()
        for r in (2, 3, 1):
            remote(
                src.at[self.rows(self.other(r)), :], here, self.send.at[i, r], self.recv.at[i, r],
                self.place.in_tensor(r),
            ).start()

    def wait(self, i, block, arrive=True, leave=True):
        for r in (1, 2, 3):
            copy = remote(block, block, self.send.at[i, r], self.recv.at[i, r], self.place.in_tensor(r))
            if arrive:
                copy.wait_recv()
            if leave:
                copy.wait_send()
        if arrive:
            pltpu.make_async_copy(block, block, self.local.at[i]).wait()


def steps(k, s, f, *order):
    return k, s, f, order


EARLY = (
    steps(0, 0, 1, 0), steps(0, 0, 0, 1, 3), steps(1, 0, 1, 0), steps(2, 0, 1, 0), steps(0, 0, 0, 2),
    steps(0, 0, 1, 1, 3), steps(0, 1, 0, 0), steps(0, 1, 1, 0), steps(0, 0, 1, 2), steps(1, 0, 0, 1),
    steps(0, 1, 0, 1, 3), steps(0, 1, 1, 1, 3), steps(1, 0, 0, 3), steps(0, 1, 0, 2), steps(0, 1, 1, 2),
)
X_AFTER = 6
IN_ATTENTION = (
    (steps(1, 0, 0, 2),), (steps(1, 0, 1, 1, 3),), (steps(1, 1, 0, 0),), (steps(1, 1, 1, 0), steps(2, 1, 0, 0)),
    (steps(2, 0, 0, 1),), (steps(1, 0, 1, 2),), (steps(1, 1, 0, 1, 3), steps(2, 1, 1, 0)), (steps(1, 1, 1, 1),),
    (steps(1, 1, 1, 3), steps(2, 0, 0, 3)), (steps(1, 1, 0, 2),), (steps(2, 0, 0, 2),), (steps(1, 1, 1, 2),),
)
IN_UP = (
    (steps(2, 0, 1, 1),), (steps(2, 1, 0, 1),), (steps(2, 1, 0, 3),), (steps(2, 0, 1, 3),), (steps(2, 1, 0, 2),),
    (steps(2, 1, 1, 1),), (steps(2, 0, 1, 2),), (steps(2, 1, 1, 3),),
)
LATE = (steps(2, 1, 1, 2),)
DOWN, UP, FRONT, BACK = (2, 2, (0, 768)), (1, 1, (0, 768)), (0, 0, (0, 512)), (3, 0, (512, 256))


def sums_in_up(scatter):
    return (
        ((1, scatter.line_far, DOWN),),
        ((1, scatter.line_near, DOWN, (2, 1)),),
    )


def sums_in_attention(scatter):
    return (
        ((0, scatter.line_near, DOWN, (3,)), (0, scatter.add_far, UP, (2,)), (1, scatter.add_near, UP, (2,))),
        ((0, scatter.add_far, UP, (1,)), (1, scatter.add_near, UP, (1,))),
        ((0, scatter.add_far, UP, (3,)), (1, scatter.add_near, UP, (3,))),
        ((0, scatter.add_far, UP, (0,)),),
        (),
        ((0, scatter.line_turn, DOWN),),
        (),
        (),
    )


def spots(rows, offset, gap=0):
    source = lax.broadcasted_iota(jnp.int32, (96, 768), 0) + rows
    target = lax.broadcasted_iota(jnp.int32, (96, 768), 1)
    moved = source + offset + jnp.where(source < 128, 0, gap)
    return jnp.where(target == moved, F32(1), F32(0)).astype(BF16)


def pack_small(place, vec_in, bias_in):
    group = place.z * 2 + place.x
    rows = vec_in[...]
    top = dot(rows, spots(96 * group, 0, 0))
    start = 96 * (group % 2)
    queries = dot(rows, spots(start, 0, 256))[0:1]
    values = dot(rows, spots(start, 256, 192))[1:2]
    units = bias_in[...].astype(F32).reshape(1, bias_in.shape[0])
    lane = lax.broadcasted_iota(jnp.int32, (1, 768), 1)
    units = jnp.where(lane // 384 == group % 2, jnp.concatenate([units, units], axis=1), 0.0)
    line = lax.broadcasted_iota(jnp.int32, (8, 768), 0)
    low = jnp.where(line == group // 2, units, 0.0) + jnp.where(line == 4 + group // 2, queries + values, 0.0)
    return jnp.concatenate([top, low], axis=0).astype(BF16)


def pack_attention(qkv_in, out_in):
    q, k, v = (qkv_in[i].astype(F32) for i in range(3))
    o = jnp.transpose(out_in[...].astype(F32))
    return jnp.concatenate([
        q[:, :128], k[:, :128], v[:, :128], jnp.concatenate([q[:, 128:], k[:, 128:]], axis=1),
        jnp.concatenate([o[:, 128:], v[:, 128:]], axis=1), o[:, :128],
    ], axis=1).astype(BF16)


def finish_kernel(
    dp_count, out_in, gtok_in, shard, small,
    output, gtok, qkv, out, up, down, vec, units,
):
    stride = dp_count // 8
    rank = lax.axis_index("dp")
    group, part = rank // stride, vec.shape[1]
    output[...] = out_in[...]
    gtok[...] = gtok_in[...].astype(F32)
    a = shard[0]
    qkv[0, :, 0:128] = a[:, 0:128]
    qkv[1, :, 0:128] = a[:, 128:256]
    qkv[2, :, 0:128] = a[:, 256:384]
    qkv[0, :, 128:192] = a[:, 384:448]
    qkv[1, :, 128:192] = pltpu.roll(a[:, 384:512], 64, 1)[:, 0:64]
    qkv[2, :, 128:192] = pltpu.roll(a[:, 512:640], 64, 1)[:, 0:64]
    out[0:128, :] = jnp.transpose(a[:, 640:768])
    out[128:192, :] = jnp.transpose(a[:, 512:640])[0:64]
    up[...] = shard[1]
    down[...] = shard[2]

    rest = rank % stride
    even = group % 2 == 0
    lane = lax.broadcasted_iota(jnp.int32, (1, 768), 1)

    def own_lines(row, first, second):
        near = pltpu.roll(row, jnp.where(even, (768 - first) % 768, 768 - first - 96), 1)
        far = pltpu.roll(row, 768 - second + 32, 1)
        return jnp.where(even | (lane < 32), near, far)

    line = lax.broadcasted_iota(jnp.int32, (8, 768), 0)
    packed = small[8:16, :]
    row = jnp.sum(jnp.where(line == 4 + group // 2, packed, 0.0), axis=0, keepdims=True)
    queries = own_lines(row, 0, 384)
    values = own_lines(row, 256, 576)
    lines = pltpu.roll(small[0:8, :], (768 - 96 * group) % 768, 1)
    lines = jnp.where(line == 0, queries, jnp.where(line == 1, values, lines))
    lines = pltpu.roll(lines, (768 - rest * part) % 768, 1)
    vec[...] = lines[:, 0:part]
    row = jnp.sum(jnp.where(line == group // 2, packed, 0.0), axis=0, keepdims=True)
    shift = 384 * (group % 2) + rest * 4 * part
    units[...] = pltpu.roll(row, (768 - shift) % 768, 1)[:, 0 : 4 * part].reshape(4 * part)


def finish_call(dp_count, out, gtok, shard, small):
    rows, width = shard.shape[1], shard.shape[2]
    shapes = (
        (out.shape, BF16), (gtok.shape, F32), ((3, rows, width // 4), F32), ((width // 4, rows), F32),
        ((rows, width), F32), ((rows, width), F32), ((8, rows), F32), ((4 * rows,), F32),
    )
    vmem = pl.BlockSpec(memory_space=pltpu.VMEM)
    return pl.pallas_call(
        functools.partial(finish_kernel, dp_count),
        out_shape=[jax.ShapeDtypeStruct(s, d) for s, d in shapes],
        in_specs=[vmem] * 4,
        out_specs=[vmem] * 8,
        compiler_params=pltpu.CompilerParams(vmem_limit_bytes=VMEM_LIMIT),
        name="finish",
    )(out, gtok, shard, small)


def layer_kernel(
    dp_count, x_in, go_in, qkv_in, out_in, up_in, down_in, vec_in, bias_in, len_ref,
    output, gtok, shard, small,
    own_first, small_in, w, x, go, smalls, sm, qkv, ctx, act, gp, hb, n1, s1, stat, gsm,
    acc, pre, low_grad, tall, gctx, gpacked,
    box_p, box_s, box_f, box_z, stages, small_box,
    send, recv, tok_send, tok_recv, tok_local, own_local, bias_send, bias_recv,
    send_p, recv_p, send_s, recv_s, send_f, recv_f, send_z, recv_z, small_send, small_recv,
):
    seq, width = x.shape
    blocks = seq // ROWS
    place = Place(dp_count)
    own = (own_first, up_in, down_in)
    gather = Gather(place, own, w, send, recv)
    own_first[...] = pack_attention(qkv_in, out_in)
    small_in[...] = pack_small(place, vec_in, bias_in)
    tokens = Tokens(place, tok_send, tok_recv, tok_local)

    barrier(place)
    gather.along(0)
    gather.start(0)
    for k in range(3):
        pltpu.make_async_copy(own[k], gather.piece(k, 0, 0, 0), own_local.at[k]).start()
    pltpu.make_async_copy(small_in, smalls.at[0], own_local.at[3]).start()
    for j in range(4):
        for i in range(2):
            if j or i:
                slot = ((4 - j) % 4) * 2 + i
                remote(
                    small_in, smalls.at[slot], bias_send.at[slot], bias_recv.at[slot], place.in_dp(j, i)
                ).start()
    for k in (1, 2):
        gather.along(k)
        gather.start(k)
    for event in EARLY[:X_AFTER]:
        gather.relay(*event)
    tokens.gather(0, x_in, x)
    for event in EARLY[X_AFTER:]:
        gather.relay(*event)
    for k in range(3):
        pltpu.make_async_copy(own[k], own[k], own_local.at[k]).wait()
    pltpu.make_async_copy(small_in, small_in, own_local.at[3]).wait()

    @pl.loop(1, 8)
    def _(slot):
        remote(small_in, small_in, bias_send.at[slot], bias_recv.at[slot], place.partner()).wait()

    total = smalls[0].astype(F32)
    for i in range(1, 8):
        total += smalls[i].astype(F32)
    sm[...] = total
    tokens.wait(0, x_in.at[0])
    gather.others(0)

    low, high = lane_masks(0.125)
    length = len_ref[place.y * 2 + place.c]
    key_bias = jnp.where(lax.broadcasted_iota(jnp.int32, (1, seq), 1) < length, F32(0), F32(NEG))
    acc[...] = jnp.zeros_like(acc)

    def relays(step, table):
        for n, events in enumerate(table):
            if events:
                @pl.when(step == n)
                def _():
                    for event in events:
                        gather.relay(*event)

    @pl.loop(0, 4)
    def _(t):
        relays(3 * t, IN_ATTENTION)
        proj = dot(x[...], w[0, t, :, 0:640]) + sm[pl.ds(12 + t, 1), 0:640]
        qkv[t, :, 0:640] = proj.astype(BF16)
        q_two = pltpu.roll(jnp.where(is_low((seq, 128)), proj[:, 384:512] * 0.125, 0.0), 64, 1)
        qkv[t, :, 640:768] = q_two.astype(BF16)

        @pl.loop(0, seq // 256)
        def _(r):
            relays(3 * t + r + 1, IN_ATTENTION)
            rows = pl.ds(pl.multiple_of(r * 256, 256), 256)
            q_pair = qkv[t, rows, 0:128]
            outs = []
            stats = []
            for h in range(3):
                if h < 2:
                    queries = q_pair * (low, high)[h]
                    keys = qkv[t, :, 128:256]
                    values = qkv[t, :, 256:384]
                else:
                    queries = qkv[t, rows, 640:768]
                    keys = qkv[t, :, 384:512]
                    values = qkv[t, :, 512:640]
                scores = dot_nt(queries, keys) + key_bias
                highest = jnp.max(scores, axis=1, keepdims=True)
                grown = jnp.exp(scores - highest)
                total = jnp.sum(grown, axis=1, keepdims=True)
                probs = (grown * (1.0 / total)).astype(BF16)
                outs.append(dot(probs, values))
                stats.append(highest + jnp.log(total))
            lowest = is_low((256, 128))
            ctx[t, rows, 0:128] = jnp.where(lowest, pltpu.roll(outs[2], 64, 1), 0.0).astype(BF16)
            ctx[t, rows, 128:256] = jnp.where(lowest, outs[0], outs[1]).astype(BF16)
            lane = lax.broadcasted_iota(jnp.int32, (256, 128), 1)
            stat[t, rows, :] = jnp.where(lane == 0, stats[0], jnp.where(lane == 1, stats[1], stats[2]))

        acc[...] += dot_nt(ctx[t], w[0, t, :, 512:768])

    @pl.loop(0, blocks)
    def _(r):
        rows = pl.ds(pl.multiple_of(r * ROWS, ROWS), ROWS)
        resid = x[rows, :].astype(F32) + acc[rows, :] + sm[2:3, :]
        centred = resid - jnp.mean(resid, axis=1, keepdims=True)
        scale = lax.rsqrt(jnp.mean(centred * centred, axis=1, keepdims=True) + EPS)
        normed = centred * scale
        hidden = normed * sm[3:4, :] + sm[4:5, :]
        n1[rows, :] = normed
        s1[rows, :] = jnp.broadcast_to(scale, (ROWS, 128))
        hb[rows, :] = hidden.astype(BF16)
        acc[rows, :] = hidden + sm[5:6, :]

    gather.others(1)

    @pl.loop(0, 4)
    def _(t):
        relays(2 * t, IN_UP)
        pre[...] = dot(hb[...], w[1, t])

        relays(2 * t + 1, IN_UP)

        @pl.loop(0, blocks)
        def _(r):
            rows = pl.ds(pl.multiple_of(r * ROWS, ROWS), ROWS)
            u = pre[rows, :] + sm[pl.ds(8 + t, 1), :]
            cdf = 0.5 + 0.5 * lax.erf(u * F32(np.sqrt(0.5)))
            density = jnp.exp(u * u * -0.5) * F32(1.0 / np.sqrt(2.0 * np.pi))
            act[t, rows, :] = (u * cdf).astype(BF16)
            gp[t, rows, :] = (cdf + u * density).astype(BF16)

    tokens.gather(1, go_in, go)
    for event in LATE:
        gather.relay(*event)
    gather.others(2)

    @pl.loop(0, 4)
    def _(t):
        acc[...] += dot_nt(act[t], w[2, t])

    gsm[...] = jnp.zeros_like(gsm)

    @pl.loop(0, blocks)
    def _(r):
        rows = pl.ds(pl.multiple_of(r * ROWS, ROWS), ROWS)
        resid = acc[rows, :]
        centred = resid - jnp.mean(resid, axis=1, keepdims=True)
        scale = lax.rsqrt(jnp.mean(centred * centred, axis=1, keepdims=True) + EPS)
        acc[rows, :] = centred * scale
        pre[rows, 0:128] = jnp.broadcast_to(scale, (ROWS, 128))

    tall[1] = jnp.transpose(hb[...].astype(F32)).astype(BF16)
    tokens.wait(1, x_in.at[0])

    @pl.loop(0, blocks)
    def _(r):
        rows = pl.ds(pl.multiple_of(r * ROWS, ROWS), ROWS)
        normed = acc[rows, :]
        gain = sm[6:7, :]
        cot = go[rows, :].astype(F32)
        go[rows, :] = (normed * gain + sm[7:8, :]).astype(BF16)
        e = cot * gain
        en = jnp.mean(e * normed, axis=1, keepdims=True)
        grad = pre[rows, 0:1] * (e - jnp.mean(e, axis=1, keepdims=True) - normed * en)
        acc[rows, :] = grad
        low_grad[rows, :] = grad.astype(BF16)
        gsm[5:6, :] += jnp.sum(grad, axis=0, keepdims=True)
        gsm[6:7, :] += jnp.sum(cot * normed, axis=0, keepdims=True)
        gsm[7:8, :] += jnp.sum(cot, axis=0, keepdims=True)

    tokens.spread(2, go, output)
    gather.finish()
    scatter = Scatter(
        place, w, (box_p, box_s, box_f, box_z), (send_p, send_s, send_f, send_z), (recv_p, recv_s, recv_f, recv_z),
        shard,
    )
    tall[0] = jnp.transpose(acc[...]).astype(BF16)

    def chunk(i, core):
        return ((place.y + 1 - i) % 2) * 2 + core

    def own_chunk(k, i, t, value):
        scatter.from_partner(k, i)
        w[k, t] = (value + box_p[k, i].astype(F32)).astype(BF16)
        parts = (DOWN,) if k == 2 else (UP,)
        pl.when(i == 0)(lambda: scatter.ready(parts, 0))
        pl.when(i == 1)(lambda: scatter.ready(parts, 1))

    def down_back(t):
        grad_pre = dot(low_grad[...], w[2, t]) * gp[t].astype(F32)
        put_row(gsm, t, slice(0, 768), jnp.sum(grad_pre, axis=0, keepdims=True))
        gp[t] = grad_pre.astype(BF16)
        return dot(tall[0], act[t])

    def up_back(t):
        acc[...] += dot_nt(gp[t], w[1, t])
        return dot(tall[1], gp[t])

    def sums_at(i, events):
        for turn in (0, 1):
            now = [event for event in events if event[0] == turn]
            if now:
                @pl.when(i == turn)
                def _():
                    for _, function, *arguments in now:
                        function(*arguments)

    for k, back in ((2, down_back), (1, up_back)):
        events = ((), ()) if k == 2 else sums_in_up(scatter)

        @pl.loop(0, 2)
        def _(i):
            t = chunk(i, 1 - place.c)
            w[k, t] = back(t).astype(BF16)
            scatter.to_partner(k, t, i)
            sums_at(i, events[0])
            t = chunk(i, place.c)
            own_chunk(k, i, t, back(t))
            sums_at(i, events[1])

    @pl.loop(0, blocks)
    def _(r):
        rows = pl.ds(pl.multiple_of(r * ROWS, ROWS), ROWS)
        cot = acc[rows, :]
        normed = n1[rows, :]
        e = cot * sm[3:4, :]
        en = jnp.mean(e * normed, axis=1, keepdims=True)
        grad = s1[rows, 0:1] * (e - jnp.mean(e, axis=1, keepdims=True) - normed * en)
        acc[rows, :] = grad
        low_grad[rows, :] = grad.astype(BF16)
        gsm[2:3, :] += jnp.sum(grad, axis=0, keepdims=True)
        gsm[3:4, :] += jnp.sum(cot * normed, axis=0, keepdims=True)
        gsm[4:5, :] += jnp.sum(cot, axis=0, keepdims=True)

    tall[0] = jnp.transpose(acc[...]).astype(BF16)
    tall[1] = jnp.transpose(x[...].astype(F32)).astype(BF16)

    one_low, one_high = lane_masks(1.0)
    tall_bias = jnp.where(lax.broadcasted_iota(jnp.int32, (seq, 1), 0) < length, F32(0), F32(NEG))

    def attention_back(t, event, store):
        back = dot(low_grad[...], w[0, t, :, 512:768])
        gctx[:, 0:128] = pltpu.roll(jnp.where(is_low((seq, 128)), back[:, 0:128], 0.0), 64, 1).astype(BF16)
        gctx[:, 128:256] = back[:, 128:256].astype(BF16)
        log_rows = jnp.transpose(stat[t])
        grads_q = []
        grads_k = []
        grads_v = []
        for h in range(3):
            if h < 2:
                queries = qkv[t, :, 0:128] * (low, high)[h]
                keys = qkv[t, :, 128:256]
                values = qkv[t, :, 256:384]
                cots = gctx[:, 128:256] * (one_low, one_high)[h]
            else:
                queries = qkv[t, :, 640:768]
                keys = qkv[t, :, 384:512]
                values = qkv[t, :, 512:640]
                cots = gctx[:, 0:128]
            scores = dot_nt(keys, queries) + tall_bias
            probs = jnp.exp(scores - log_rows[h : h + 1, :])
            grad_probs = dot_nt(values, cots)
            row_dots = jnp.sum(grad_probs * probs, axis=0, keepdims=True)
            grad_scores = (probs * (grad_probs - row_dots)).astype(BF16)
            grads_v.append(dot(probs.astype(BF16), cots))
            grads_k.append(dot(grad_scores, queries))
            part = (0, HD, HD)[h]
            keys_tall = jnp.transpose(keys.astype(F32))[part : part + HD, :].astype(BF16)
            grads_q.append(dot(keys_tall, grad_scores) * 0.125)
            event(h)
        pair = jnp.transpose(jnp.concatenate([grads_q[0], grads_q[1]], axis=0))
        single = jnp.transpose(jnp.concatenate([grads_q[2], jnp.zeros_like(grads_q[2])], axis=0))
        tiles = [pair, grads_k[0] + grads_k[1], grads_v[0] + grads_v[1], single + grads_k[2], grads_v[2]]
        for i, tile in enumerate(tiles):
            span = slice(128 * i, 128 * i + 128)
            put_row(gsm, 4 + t, span, jnp.sum(tile, axis=0, keepdims=True))
            gpacked[:, span] = tile.astype(BF16)
        event(3)
        acc[...] += dot_nt(gpacked[...], w[0, t, :, 0:640])
        store(slice(0, 512), dot(tall[1], gpacked[:, 0:512]))
        store(slice(512, 640), dot(tall[1], gpacked[:, 512:640]) + dot(tall[0], ctx[t, :, 0:128]))
        store(slice(640, 768), dot(tall[0], ctx[t, :, 128:256]))

    @pl.loop(0, 2)
    def _(i):
        other = chunk(i, 1 - place.c)
        mine = chunk(i, place.c)

        def store_other(span, value):
            w[0, other, :, span] = value.astype(BF16)

        def store_mine(span, value):
            w[0, mine, :, span] = (value + box_p[0, i, :, span].astype(F32)).astype(BF16)

        events = sums_in_attention(scatter)

        def event_other(h):
            sums_at(i, events[h])

        def event_mine(h):
            sums_at(i, events[4 + h])
            if h == 3:
                scatter.from_partner(0, i)

        attention_back(other, event_other, store_other)
        scatter.to_partner(0, other, i)
        attention_back(mine, event_mine, store_mine)
        pl.when(i == 0)(lambda: scatter.ready((FRONT, BACK), 0))
        pl.when(i == 1)(lambda: scatter.ready((FRONT, BACK), 1))

    x[...] = acc[...].astype(BF16)
    stages[0] = gsm[...]
    sums = SmallSum(place, stages, small_box, small_send, small_recv)
    sums.start(0)
    scatter.add_far(FRONT)
    scatter.add_far(BACK)
    tokens.spread(3, x, gtok)
    sums.step(0)
    scatter.add_near(FRONT)
    sums.step(1)
    scatter.add_near(BACK)
    sums.step(2)
    scatter.line_last(DOWN)
    scatter.add_last(UP)
    sums.finish(small)
    scatter.add_last(FRONT)
    scatter.add_last(BACK)
    for i in (2, 3):
        tokens.wait(i, x_in.at[0])
    scatter.finish((DOWN, UP, FRONT, BACK))


def layer_call(dp_count, tokens, grad_out, weights, vectors, bias, lengths):
    part, width = tokens.shape[1], tokens.shape[2]
    seq = tokens.shape[0] * part
    shapes = (((4, part, width), BF16), ((4, part, width), BF16), ((3, 96, width), F32), ((16, width), F32))
    vmem = pl.BlockSpec(memory_space=pltpu.VMEM)
    smem = pl.BlockSpec(memory_space=pltpu.SMEM)
    dma = pltpu.SemaphoreType.DMA
    low_rows = pltpu.VMEM((seq, width), BF16)
    wide_rows = pltpu.VMEM((seq, width), F32)
    return pl.pallas_call(
        functools.partial(layer_kernel, dp_count),
        out_shape=[jax.ShapeDtypeStruct(s, d) for s, d in shapes],
        in_specs=[vmem] * 8 + [smem],
        out_specs=[vmem] * 4,
        scratch_shapes=[
            pltpu.VMEM((96, width), BF16), pltpu.VMEM((16, width), BF16),
            pltpu.VMEM((3, 4, width, 768), BF16), low_rows, low_rows, pltpu.VMEM((8, 16, width), BF16),
            pltpu.VMEM((16, width), F32), pltpu.VMEM((4, seq, 768), BF16), pltpu.VMEM((4, seq, 256), BF16),
            pltpu.VMEM((4, seq, 768), BF16), pltpu.VMEM((4, seq, 768), BF16), low_rows, wide_rows,
            pltpu.VMEM((seq, 128), F32), pltpu.VMEM((4, seq, 128), F32), pltpu.VMEM((16, width), F32),
            wide_rows, wide_rows, low_rows, pltpu.VMEM((2, width, seq), BF16),
            pltpu.VMEM((seq, 256), BF16), pltpu.VMEM((seq, 640), BF16),
            pltpu.VMEM((3, 2, width, 768), BF16), pltpu.VMEM((3, 2, 4, 96, width), BF16),
            pltpu.VMEM((3, 4, 96, width), BF16), pltpu.VMEM((3, 3, 96, width), BF16),
            pltpu.VMEM((4, 16, width), F32), pltpu.VMEM((6, 16, width), F32),
            dma((3, 31)), dma((3, 32)), dma((4, 4)), dma((4, 4)), dma((4,)), dma((4,)), dma((8,)), dma((8,)),
            dma((3, 2)), dma((3, 2)), dma((4, 8)), dma((4, 8)), dma((4, 4)), dma((4, 4)), dma((4, 3)), dma((4, 3)),
            dma((6,)), dma((6,)),
        ],
        compiler_params=pltpu.CompilerParams(
            vmem_limit_bytes=VMEM_LIMIT, collective_id=0, has_side_effects=True
        ),
        name="layer",
    )(tokens, grad_out, *weights, vectors, bias, lengths)


def gather_groups(shard, dp_count, axis):
    stride = dp_count // 8
    if stride == 1:
        return shard
    groups = [[g * stride + i for i in range(stride)] for g in range(8)]
    return lax.all_gather(shard, "dp", axis=axis, tiled=True, axis_index_groups=groups)


def scatter_groups(shard, small, dp_count):
    stride = dp_count // 8
    if stride == 1:
        return shard, small
    groups = [[g * stride + i for i in range(stride)] for g in range(8)]
    shard = lax.psum_scatter(shard, "dp", scatter_dimension=1, tiled=True, axis_index_groups=groups)
    return shard, lax.psum(small, "dp", axis_index_groups=groups)


def shards(tokens, lengths, grad_out, qkv_weight, out_weight, up_weight, down_weight, vectors, hidden_bias):
    dp_count = lax.axis_size("dp")
    weights = [
        gather_groups(weight, dp_count, axis)
        for weight, axis in ((qkv_weight, 1), (out_weight, 1), (up_weight, 0), (down_weight, 1))
    ]
    weights[3] = weights[3].T
    vectors = gather_groups(vectors, dp_count, 1)
    bias = gather_groups(hidden_bias, dp_count, 0)
    output, gtok, g, gsm = layer_call(dp_count, tokens, grad_out, weights, vectors, bias, lengths)
    g, gsm = scatter_groups(g, gsm, dp_count)
    *results, down, vec, units = finish_call(dp_count, output, gtok, g, gsm)
    return *results, down.T, vec, units


def solution(mesh):
    in_specs = (
        P("dp", "tensor", None), P("dp"), P("dp", "tensor", None), P(None, "dp", "tensor"), P("tensor", "dp"),
        P("dp", "tensor"), P("tensor", "dp"), P(None, "dp"), P("dp"),
    )
    out_specs = (
        P("dp", "tensor", None), P("dp", "tensor", None), P(None, "dp", "tensor"), P("tensor", "dp"),
        P("dp", "tensor"), P("tensor", "dp"), P(None, "dp"), P("dp"),
    )
    return jax.shard_map(shards, mesh=mesh, in_specs=in_specs, out_specs=out_specs, check_vma=False)
```
